32 devices in a mesh: macro: 16 (over z, x, core), vox: 2 (over y).
Axes of the slice: x: 2, y: 2, z: 4, core: 2. Of those that a mesh axis runs over, the one named last changes fastest.
Arguments:
- displacement: float32 [3, 1024], P(None, 'macro'), may hold values from -1.2 to 1.2
- load: float32 [3, 1024], P(None, 'macro'), may hold values from -6 to 6
- conn: int32 [8, 1024], P(None, 'macro'), may hold values from 0 to 79
- halo_list: int32 [256], P('macro'), may hold values from 0 to 63
- grad_ops: float32 [3, 8, 1024], P(None, None, 'macro'), may hold values from -3 to 3
- volume: float32 [1024], P('macro'), may hold values from 0.5 to 2
- elastic_moduli: float32 [2, 1024], P(None, 'macro'), may hold values from 1 to 4
- plastic_mask: int32 [1024], P('macro'), may hold values from 0 to 1, as said below
- new_owner: int32 [1024], P('macro'), may hold values from -1 to 15, as said below
- state: float32 [7, 1024, 16, 256], P(None, 'macro', 'vox'), may hold values from -0.6 to 1, as said below
- micro_moduli: float32 [4, 16, 256], P(None, 'vox'), may hold values from 0.5 to 6
Outputs:
- residual: float32 [3, 1024], P(None, 'macro')
- moved_state: float32 [7, 384, 16, 256], P(None, 'macro', 'vox')
The draws below stay inside these ranges and needn't reach their ends.
Inputs may be any that keep to these rules, and one draw needn't show every extreme that they name: `plastic_mask`: each group's 64 points hold at most 48 plastic ones, 384 in all. `new_owner`: -1 exactly at elastic points; every group becomes the owner of exactly 24 plastic points, at most 3 of them from any one group. `state`: component 6 is nonnegative.
All inputs are finite; a program needn't handle non-finite values.
Results may differ from the reference program's by a relative error of at most 0.0001.
Values sent between devices are 32-bit elements; how exact they have to be, the bound alone decides.
A program may use at most 64 MiB of HBM per device.

```python
import math
import jax
import jax.numpy as jnp
from jax import lax

GROUPS = 16
ELEM_DEV = 64
NODE_DEV = 64
HALO_NODES = 16
RECV_AGG = 24
VOX_SIDE = 16
VOX_PLANE = 256
SWEEPS = 4


def owner_plan(key):
    folded = jax.random.fold_in(key, 7)
    key_count, key_pick, key_dest = jax.random.split(folded, 3)
    middle = GROUPS // 2
    levels = jnp.arange(middle, dtype=jnp.int32)
    spread = RECV_AGG * levels // (middle - 1)
    counts = jnp.concatenate([RECV_AGG + spread, RECV_AGG - spread])
    counts = counts[jax.random.permutation(key_count, GROUPS)]
    orders = jax.vmap(lambda k: jax.random.permutation(k, ELEM_DEV))(jax.random.split(key_pick, GROUPS))
    ranking = jnp.argsort(orders, axis=1)
    plastic = (ranking < counts[:, None]).reshape(-1)
    running = jnp.cumsum(plastic.astype(jnp.int32)) - 1
    targets = jax.random.permutation(key_dest, GROUPS).astype(jnp.int32)
    owners = targets[running % GROUPS]
    return (plastic.astype(jnp.int32), jnp.where(plastic, owners, -1).astype(jnp.int32))


def draw_plastic_mask(key, part):
    return owner_plan(key)[0]


def draw_new_owner(key, part):
    return owner_plan(key)[1]


def draw_state(key, part):
    first, second = jax.random.split(jax.random.fold_in(key, 11))
    extent = (6, GROUPS * ELEM_DEV, VOX_SIDE, VOX_PLANE)
    single = (1, GROUPS * ELEM_DEV, VOX_SIDE, VOX_PLANE)
    plastic_part = jnp.clip(0.15 * jax.random.normal(first, extent, jnp.float32), -0.6, 0.6)
    hardening = jax.random.uniform(second, single, jnp.float32, 0.0, 0.5)
    return jnp.concatenate([plastic_part, hardening], axis=0)


def draw_micro_moduli(key, part):
    noise = jax.random.uniform(jax.random.fold_in(key, 13), (4, VOX_SIDE, VOX_PLANE), jnp.float32)
    basis = 0.5 * jnp.exp(noise * jnp.log(4.0))
    ramp = 1.0 + 2.0 * jnp.arange(VOX_SIDE, dtype=jnp.float32) / (VOX_SIDE - 1)
    return basis * ramp[None, :, None]


def with_ends(array, stream_key, least, high):
    shape = array.shape
    place = [jax.random.randint(jax.random.fold_in(stream_key, axis), (), 0, shape[axis]) for axis in range(len(shape))]
    array = array.at[tuple(place)].set(least)
    longest = shape.index(max(shape))
    place[longest] = (place[longest] + 1) % shape[longest]
    return array.at[tuple(place)].set(high)


def steps_of(stream_key, dims, cuts, low, high):
    def one(dim, shards_of):
        heights = jax.random.uniform(jax.random.fold_in(jax.random.fold_in(stream_key, 6), dim), (shards_of,), jnp.float32, low / len(cuts), high / len(cuts))
        return jnp.repeat(jnp.exp(heights), dims[dim] // shards_of).reshape((-1,) + (1,) * (len(dims) - dim - 1))

    factor_of = one(*cuts[0])
    for cut in cuts[1:]:
        factor_of = factor_of * one(*cut)
    return factor_of


def gaussian(own_key, dims, scale, most, cuts=(), kind=jnp.bfloat16):
    array = jax.random.normal(own_key, dims, jnp.float32) * scale
    if len(cuts) > 0:
        array = steps_of(own_key, dims, cuts, -0.22, 0.18) * array
    return jnp.clip(array, min=-most, max=most).astype(kind)


def setup_inputs(seed: int = 0) -> dict:
    key_list = jax.random.split(jax.random.key(seed), 12)
    return {
        "displacement": gaussian(key_list[0], (3, GROUPS * NODE_DEV), 0.2, 1.2, ((1, 16),), jnp.float32),
        "load": gaussian(key_list[1], (3, GROUPS * NODE_DEV), 1.0, 6.0, ((1, 16),), jnp.float32),
        "conn": with_ends(jax.random.randint(key_list[2], (8, GROUPS * ELEM_DEV), 0, NODE_DEV + HALO_NODES), jax.random.fold_in(key_list[2], 1), 0, (NODE_DEV + HALO_NODES) - 1).astype(jnp.int32),
        "halo_list": with_ends(jax.random.randint(key_list[3], (GROUPS * HALO_NODES,), 0, NODE_DEV), jax.random.fold_in(key_list[3], 1), 0, NODE_DEV - 1).astype(jnp.int32),
        "grad_ops": gaussian(key_list[4], (3, 8, GROUPS * ELEM_DEV), 0.5, 3.0, ((2, 16),), jnp.float32),
        "volume": jnp.clip(jnp.exp(math.log(2.0) - 1.3862944 * jax.random.uniform(key_list[5], (GROUPS * ELEM_DEV,), jnp.float32) ** steps_of(key_list[5], (GROUPS * ELEM_DEV,), ((0, 16),), -0.2, 0.2)), 0.5, 2.0),
        "elastic_moduli": jnp.clip(jnp.exp(math.log(4.0) - 1.3862944 * jax.random.uniform(key_list[6], (2, GROUPS * ELEM_DEV), jnp.float32) ** steps_of(key_list[6], (2, GROUPS * ELEM_DEV), ((1, 16),), -0.2, 0.2)), 1.0, 4.0),
        "plastic_mask": draw_plastic_mask(jax.random.fold_in(key_list[11], 71), 0),
        "new_owner": draw_new_owner(jax.random.fold_in(key_list[11], 71), 0),
        "state": draw_state(jax.random.fold_in(key_list[11], 71), 0),
        "micro_moduli": draw_micro_moduli(jax.random.fold_in(key_list[11], 71), 0),
    }


LAM_REF = 3.0
MU_REF = 3.0

def strain_tensor(disp_el, grad_el):
    products = [[lax.optimization_barrier(jnp.sum(disp_el[i] * grad_el[j], axis=0)) for j in range(3)] for i in range(3)]
    return jnp.stack([products[0][0], products[1][1], products[2][2], 0.5 * (products[1][2] + products[2][1]), 0.5 * (products[0][2] + products[2][0]), 0.5 * (products[0][1] + products[1][0])])

def full_tensor(voigt):
    return [[voigt[0], voigt[5], voigt[4]], [voigt[5], voigt[1], voigt[3]], [voigt[4], voigt[3], voigt[2]]]

def nodal_forces(stress, grad_el, volume):
    tensor = full_tensor(stress)
    return jnp.stack([volume * (tensor[i][0] * grad_el[0] + tensor[i][1] * grad_el[1] + tensor[i][2] * grad_el[2]) for i in range(3)])

def elastic_stress(strain, moduli):
    lame_first = moduli[0]
    shear_mod = moduli[1]
    trace = strain[0] + strain[1] + strain[2]
    return jnp.stack([lame_first * trace + 2.0 * shear_mod * strain[c] for c in range(3)] + [2.0 * shear_mod * strain[c] for c in range(3, 6)])

def return_map(strain, state, props):
    lame_first, shear_mod, yield_base, harden = (props[0], props[1], props[2], props[3])
    elastic = [strain[c] - state[c] for c in range(6)]
    trace = elastic[0] + elastic[1] + elastic[2]
    trial = [lame_first * trace + 2.0 * shear_mod * elastic[c] for c in range(3)] + [2.0 * shear_mod * elastic[c] for c in range(3, 6)]
    pressure = (trial[0] + trial[1] + trial[2]) / 3.0
    deviator = [trial[0] - pressure, trial[1] - pressure, trial[2] - pressure, trial[3], trial[4], trial[5]]
    squared = deviator[0] ** 2 + deviator[1] ** 2 + deviator[2] ** 2 + 2.0 * (deviator[3] ** 2 + deviator[4] ** 2 + deviator[5] ** 2)
    equivalent = jnp.sqrt(1.5 * squared)
    strength = yield_base + harden * state[6]
    excess = jnp.maximum(equivalent - strength, 0.0)
    stiffer = 3.0 * shear_mod + harden
    factor = excess / (stiffer * jnp.maximum(equivalent, strength))
    stress = jnp.stack([trial[c] - 3.0 * shear_mod * factor * deviator[c] for c in range(6)])
    new_state = jnp.stack([state[c] + 1.5 * factor * deviator[c] for c in range(6)] + [state[6] + excess / stiffer])
    return (stress, new_state)

def green_apply(tau, freq_x, freq_y, freq_z):
    trac_x = tau[0] * freq_x + tau[5] * freq_y + tau[4] * freq_z
    trac_y = tau[5] * freq_x + tau[1] * freq_y + tau[3] * freq_z
    trac_z = tau[4] * freq_x + tau[3] * freq_y + tau[2] * freq_z
    norm_sq = freq_x * freq_x + freq_y * freq_y + freq_z * freq_z
    inverse = jnp.where(norm_sq > 0, 1.0 / jnp.maximum(norm_sq, 1.0), 0.0)
    coupling = (LAM_REF + MU_REF) / (LAM_REF + 2.0 * MU_REF)
    along = (freq_x * trac_x + freq_y * trac_y + freq_z * trac_z) * inverse
    wave_x = (trac_x - coupling * along * freq_x) * inverse / MU_REF
    wave_y = (trac_y - coupling * along * freq_y) * inverse / MU_REF
    wave_z = (trac_z - coupling * along * freq_z) * inverse / MU_REF
    return [freq_x * wave_x, freq_y * wave_y, freq_z * wave_z, 0.5 * (freq_y * wave_z + freq_z * wave_y), 0.5 * (freq_x * wave_z + freq_z * wave_x), 0.5 * (freq_x * wave_y + freq_y * wave_x)]

def solve_block(states, strains, props):
    index = jnp.arange(VOX_SIDE, dtype=jnp.int32)
    signed = jnp.where(index < VOX_SIDE // 2, index, index - VOX_SIDE).astype(jnp.float32)
    freq_x = signed[:, None, None]
    freq_y = signed[None, :, None]
    freq_z = signed[None, None, :]
    field = jnp.broadcast_to(strains[:, :, None, None, None], (6,) + states.shape[1:])
    for iteration in range(SWEEPS):
        stress, _ = return_map(field, states, props)
        spectrum = jnp.fft.fftn(stress, axes=(2, 3, 4))
        update = jnp.stack(green_apply([spectrum[c] for c in range(6)], freq_x, freq_y, freq_z))
        field = field - jnp.real(jnp.fft.ifftn(update, axes=(2, 3, 4)))
    stress, new_state = return_map(field, states, props)
    return (new_state, lax.optimization_barrier(jnp.mean(stress, axis=(2, 3, 4))))

def reference(displacement, load, conn, halo_list, grad_ops, volume, elastic_moduli, plastic_mask, new_owner, state, micro_moduli):
    points = GROUPS * ELEM_DEV
    point_ids = jnp.arange(points, dtype=jnp.int32)
    group_of = point_ids // ELEM_DEV
    previous = (group_of - 1) % GROUPS
    halo_slot = jnp.clip(conn - NODE_DEV, 0, HALO_NODES - 1)
    halo_node = previous[None, :] * NODE_DEV + halo_list[previous[None, :] * HALO_NODES + halo_slot]
    global_node = jnp.where(conn < NODE_DEV, group_of[None, :] * NODE_DEV + conn, halo_node).astype(jnp.int32)
    disp_el = displacement[:, global_node]
    strain = strain_tensor(disp_el, grad_ops)
    plastic = plastic_mask == 1
    sort_key = jnp.where(plastic, new_owner * points + point_ids, GROUPS * points + point_ids)
    chosen = jnp.argsort(sort_key)[:GROUPS * RECV_AGG].astype(jnp.int32)
    blocks = chosen.reshape(-1, 8)
    cube_moduli = micro_moduli.reshape(4, VOX_SIDE, VOX_SIDE, VOX_SIDE)

    def solve_one(indices):
        states = state[:, indices].reshape(7, 8, VOX_SIDE, VOX_SIDE, VOX_SIDE)
        return solve_block(states, strain[:, indices], cube_moduli)
    new_states, averaged = lax.map(solve_one, blocks)
    moved_state = jnp.transpose(new_states, (1, 0, 2, 3, 4, 5)).reshape(7, GROUPS * RECV_AGG, VOX_SIDE, VOX_PLANE)
    averaged = jnp.transpose(averaged, (1, 0, 2)).reshape(6, GROUPS * RECV_AGG)
    stress = elastic_stress(strain, elastic_moduli).at[:, chosen].set(averaged)
    forces = nodal_forces(stress, grad_ops, volume)
    assembled = jnp.zeros((3, GROUPS * NODE_DEV), jnp.float32).at[:, global_node].add(forces)
    return (assembled - load, moved_state)
```

```python
import functools
import math

import jax
import jax.numpy as jnp
import numpy as np
from jax import lax
from jax.experimental import pallas as pl
from jax.experimental.pallas import tpu as pltpu
from jax.sharding import PartitionSpec as P

RECV_AGG = 24
PLASTIC_MAX = 48
VOX_SIDE = 16
VOX_PLANE = 256
SWEEPS = 4
HALF = VOX_SIDE // 2
LANES = 128

LAM_REF = 3.0
MU_REF = 3.0
FULL_PREC = lax.Precision.HIGHEST

ROOT = math.sqrt(0.5)
COS1 = math.cos(math.pi / 8)
COS3 = math.cos(3 * math.pi / 8)
PAIRS = [(i, j) for i in range(6) for j in range(i, 6)]


def shifted(block, axis, distance):
    devices = range(lax.axis_size(axis))
    route = [((i - distance) % len(devices), i) for i in devices]
    return lax.ppermute(block, axis, route)


def green_tables():
    line = np.arange(VOX_SIDE)
    signed = np.where(line < HALF, line, line - VOX_SIDE).astype(np.float64)
    freq = np.stack(np.meshgrid(signed, signed, signed, indexing="ij"))
    norm = np.sum(freq * freq, axis=0)
    inverse = np.where(norm > 0, 1.0 / np.maximum(norm, 1.0), 0.0)
    coupling = (LAM_REF + MU_REF) / (LAM_REF + 2.0 * MU_REF)
    spots = [(0, 0), (1, 1), (2, 2), (1, 2), (0, 2), (0, 1)]
    table = np.zeros((6, 6) + norm.shape)
    for j, (a, b) in enumerate(spots):
        tau = np.zeros((3, 3))
        tau[a, b] = tau[b, a] = 1.0
        trac = np.einsum("ij,jxyz->ixyz", tau, freq)
        along = np.sum(freq * trac, axis=0) * inverse
        wave = (trac - coupling * along * freq) * inverse / MU_REF
        for i, (c, d) in enumerate(spots):
            table[i, j] = 0.5 * (freq[c] * wave[d] + freq[d] * wave[c])
    back = -line % VOX_SIDE
    flipped = table[:, :, back][:, :, :, back][:, :, :, :, back]
    even = 0.5 * (table + flipped) / VOX_SIDE**3
    even[:, 3:] *= 0.5
    stacked = np.stack([even[i, j] for i, j in PAIRS])
    return stacked.reshape(len(PAIRS), VOX_SIDE, VOX_PLANE).astype(np.float32)


def plane_tables():
    plane = np.arange(VOX_PLANE)
    rows, cols = plane // VOX_SIDE, plane % VOX_SIDE
    phase = (rows[:, None] * rows[None, :] + cols[:, None] * cols[None, :]) % VOX_SIDE
    angle = phase * (2.0 * math.pi / VOX_SIDE)
    plus = jnp.asarray((np.cos(angle) + np.sin(angle)).astype(np.float32))
    minus = jnp.asarray((np.cos(angle) - np.sin(angle)).astype(np.float32))
    out = []
    for table in (plus, minus):
        high = table.astype(jnp.bfloat16)
        out += [high, (table - high.astype(jnp.float32)).astype(jnp.bfloat16)]
    return jnp.stack(out)


def cosine_line(a):
    sums = [None] + [a[x] + a[8 - x] for x in (1, 2, 3)]
    diffs = [None] + [a[x] - a[8 - x] for x in (1, 2, 3)]
    even0, odd0 = a[0] + a[8], a[0] - a[8]
    outer, inner = even0 + a[4], even0 - a[4]
    spread = sums[1] + sums[3]
    slant = ROOT * (sums[1] - sums[3])
    mid = ROOT * diffs[2]
    first = COS1 * diffs[1] + COS3 * diffs[3]
    second = COS3 * diffs[1] - COS1 * diffs[3]
    top, low = odd0 + mid, odd0 - mid
    core = outer + sums[2]
    return [
        core + spread,
        top + first,
        inner + slant,
        low + second,
        outer - sums[2],
        low - second,
        inner - slant,
        top - first,
        core - spread,
    ]


def sine_line(b):
    sums = [None] + [b[x] + b[8 - x] for x in (1, 2, 3)]
    diffs = [None] + [b[x] - b[8 - x] for x in (1, 2, 3)]
    slant = ROOT * (diffs[1] + diffs[3])
    mid = ROOT * sums[2]
    first = COS3 * sums[1] + COS1 * sums[3]
    second = COS1 * sums[1] - COS3 * sums[3]
    return [
        None,
        (first + mid) + b[4],
        slant + diffs[2],
        (second + mid) - b[4],
        diffs[1] - diffs[3],
        (second - mid) + b[4],
        slant - diffs[2],
        (first - mid) - b[4],
    ]


def split_dot(block, table_ref, first):
    high = block.astype(jnp.bfloat16)
    low = (block - high.astype(jnp.float32)).astype(jnp.bfloat16)
    dot = functools.partial(jnp.dot, preferred_element_type=jnp.float32)
    return dot(high, table_ref[first]) + (dot(high, table_ref[first + 1]) + dot(low, table_ref[first]))


def voxel_law(strain, state, props, row):
    lam, mu = props[0, row, :], props[1, row, :]
    yield_base, harden = props[2, row, :], props[3, row, :]
    two_mu, three_mu = 2.0 * mu, 3.0 * mu
    stiff_inv = 1.0 / (three_mu + harden)
    bulk = lam + two_mu * (1.0 / 3.0)
    elastic = [strain[c] - state[c] for c in range(6)]
    trace = elastic[0] + elastic[1] + elastic[2]
    third = trace * (1.0 / 3.0)
    shape = [elastic[c] - third for c in range(3)] + elastic[3:]
    normal = shape[0] * shape[0] + shape[1] * shape[1] + shape[2] * shape[2]
    shear = shape[3] * shape[3] + shape[4] * shape[4] + shape[5] * shape[5]
    equivalent = two_mu * jnp.sqrt(1.5 * (normal + 2.0 * shear))
    strength = yield_base + harden * state[6]
    gain = jnp.maximum(equivalent - strength, 0.0) * stiff_inv
    factor = gain / jnp.maximum(equivalent, strength)
    keep = two_mu * (1.0 - three_mu * factor)
    pressure = bulk * trace
    stress = [pressure + keep * shape[c] for c in range(3)] + [keep * shape[c] for c in range(3, 6)]
    return stress, shape, (1.5 * two_mu) * factor, gain


def solve_rows(pieces, strain, out, props, green, plane, buffers):
    stx, eps, work, cos_ref, sin_ref = buffers
    ranks, rows, _, thickness, _ = pieces.shape

    def bring(c, carry):
        for h in range(ranks):
            stx[c, h * thickness : (h + 1) * thickness] = jnp.swapaxes(pieces[h, :, c], 0, 1)
        return carry

    lax.fori_loop(0, 7, bring, 0)
    for c in range(6):
        eps[c] = jnp.broadcast_to(strain[:, c : c + 1][None], (VOX_SIDE, rows, VOX_PLANE))

    def sweep(step, carry):
        for h in range(ranks):

            def law(place, inner, h=h):
                x = h * thickness + place
                strain = [eps[c, x] for c in range(6)]
                state = [stx[c, x] for c in range(7)]
                stress = voxel_law(strain, state, props.at[h], pl.ds(place, 1))[0]
                for c in range(6):
                    work[c, x] = stress[c]
                return inner

            lax.fori_loop(0, thickness, law, 0)

        def forward(c, inner):
            field = [work[c, x] for x in range(VOX_SIDE)]
            sums = [field[0]] + [field[x] + field[VOX_SIDE - x] for x in range(1, HALF)] + [field[HALF]]
            diffs = [None] + [field[x] - field[VOX_SIDE - x] for x in range(1, HALF)]
            for k, value in enumerate(cosine_line(sums)):
                cos_ref[c, k] = value
            for k, value in enumerate(sine_line(diffs)):
                if k > 0:
                    sin_ref[c, k - 1] = value
            return inner

        lax.fori_loop(0, 6, forward, 0)

        def transform():
            for ref, first in ((cos_ref, 0), (sin_ref, 2)):
                flat = ref[...].reshape(6 * ref.shape[1] * rows, VOX_PLANE)
                ref[...] = split_dot(flat, plane, first).reshape(ref.shape)

        def apply(field, k):
            row = pl.ds(k, 1)
            field = field[:3] + [2.0 * field[c] for c in range(3, 6)]
            total = [None] * 6
            for n, (i, j) in enumerate(PAIRS):
                entry = green[n, row, :]
                for a, b in [(i, j), (j, i)][: 1 + (i != j)]:
                    term = entry * field[b]
                    total[a] = term if total[a] is None else total[a] + term
            return total

        transform()
        for k in (0, HALF):
            result = apply([cos_ref[c, k] for c in range(6)], k)
            for c in range(6):
                cos_ref[c, k] = result[c]

        def mix(k, inner):
            even = [cos_ref[c, k] for c in range(6)]
            odd = [sin_ref[c, k - 1] for c in range(6)]
            ahead = apply([even[c] + odd[c] for c in range(6)], k)
            behind = apply([even[c] - odd[c] for c in range(6)], VOX_SIDE - k)
            for c in range(6):
                cos_ref[c, k] = ahead[c] + behind[c]
                sin_ref[c, k - 1] = ahead[c] - behind[c]
            return inner

        lax.fori_loop(1, HALF, mix, 0)
        transform()

        def backward(c, inner):
            even = cosine_line([cos_ref[c, k] for k in range(HALF + 1)])
            odd = sine_line([None] + [sin_ref[c, k - 1] for k in range(1, HALF)])
            eps[c, 0] = eps[c, 0] - even[0]
            eps[c, HALF] = eps[c, HALF] - even[HALF]
            for x in range(1, HALF):
                eps[c, x] = eps[c, x] - (even[x] + odd[x])
                eps[c, VOX_SIDE - x] = eps[c, VOX_SIDE - x] - (even[x] - odd[x])
            return inner

        lax.fori_loop(0, 6, backward, 0)
        return carry

    lax.fori_loop(0, SWEEPS, sweep, 0)
    totals = (jnp.zeros((rows, VOX_PLANE), jnp.float32),) * 6
    for h in range(ranks):

        def finish(place, totals, h=h):
            x = h * thickness + place
            strain = [eps[c, x] for c in range(6)]
            state = [stx[c, x] for c in range(7)]
            stress, shape, scale, gain = voxel_law(strain, state, props.at[h], pl.ds(place, 1))
            for c in range(6):
                stx[c, x] = state[c] + scale * shape[c]
            stx[6, x] = state[6] + gain
            return tuple(totals[c] + stress[c] for c in range(6))

        totals = lax.fori_loop(0, thickness, finish, totals)

    def give(c, carry):
        for h in range(ranks):
            out[h, :, c] = jnp.swapaxes(stx[c, h * thickness : (h + 1) * thickness], 0, 1)
        return carry

    lax.fori_loop(0, 7, give, 0)
    lane = lax.broadcasted_iota(jnp.int32, (rows, LANES), 1)
    means = jnp.zeros((rows, LANES), jnp.float32)
    for c in range(6):
        total = jnp.sum(totals[c], axis=1, keepdims=True) / VOX_SIDE**3
        means = jnp.where(lane == c, total, means)
    return means


def drain(ref, sem):
    pltpu.make_async_copy(ref, ref, sem).wait()


def exchange_kernel(
    raws,
    source_ref,
    note_ref,
    strain_ref,
    state_hbm,
    props_hbm,
    green_hbm,
    plane_hbm,
    got,
    mean_src_out,
    mean_raw_out,
    note_out,
    *scratch,
):
    (st, raw_send, raw_recv, ex_send, ex_recv, new_src, new_raw, props, green, plane) = scratch[:10]
    buffers = scratch[10:15]
    (note_recv, mean_src, mean_raw, mean_stage, load_sem, recv, sent) = scratch[15:]
    levels, groups = got.shape[:2]
    ranks, rows = ex_recv.shape[1:3]
    sources = levels - raws
    me, mine = lax.axis_index("macro"), lax.axis_index("vox")
    my_row, my_side = me // ranks, me % ranks
    R_PROPS, R_NOTE, R_RAW, R_MRAW, R_EX = 0, 1, 2, 3, 4
    R_MEAN, R_GOT = R_EX + sources, R_EX + 2 * sources

    def push(src, dst, kind, group, rank):
        pltpu.make_async_remote_copy(
            src_ref=src,
            dst_ref=dst,
            send_sem=sent.at[kind],
            recv_sem=recv.at[kind],
            device_id={"macro": group, "vox": rank},
            device_id_type=pl.DeviceIdType.MESH,
        ).start()

    def deliver(src, dst, kind, group, rank):
        here = (group == me) & (rank == mine)

        @pl.when(here)
        def _():
            pltpu.make_async_copy(src, dst, recv.at[kind]).start()

        @pl.when(jnp.logical_not(here))
        def _():
            push(src, dst, kind, group, rank)

    def settle(first, one_less, kind, fewer):
        @pl.when(fewer)
        def _():
            drain(one_less, sent.at[kind])

        @pl.when(jnp.logical_not(fewer))
        def _():
            drain(first, sent.at[kind])

    def turn(step, count, block, spot):
        planes = count // block
        line, lane = spot // block, spot % block
        ring = step // block
        line = jnp.where(2 * line < planes, planes - 1 - ring, ring)
        return line * block + (lane + step) % block

    state_copy = pltpu.make_async_copy(state_hbm, st, load_sem.at[0])
    state_copy.start()
    green_copy = pltpu.make_async_copy(green_hbm, green, load_sem.at[1])
    plane_copy = pltpu.make_async_copy(plane_hbm, plane, load_sem.at[2])
    props_copy = pltpu.make_async_copy(props_hbm, props.at[mine], load_sem.at[3])
    green_copy.start()
    plane_copy.start()
    props_copy.start()

    barrier = pltpu.get_barrier_semaphore()
    total = groups * ranks
    flat = me * ranks + mine

    def greet(k, carry):
        other = (flat + k) % total
        pl.semaphore_signal(
            barrier,
            inc=1,
            device_id={"macro": other // ranks, "vox": other % ranks},
            device_id_type=pl.DeviceIdType.MESH,
        )
        return carry

    lax.fori_loop(1, total, greet, 0)
    state_copy.wait()
    for lv in range(sources):
        for o in range(ranks):

            def gather(i, carry, lv=lv, o=o):
                slab = st[:, source_ref[lv * groups + ranks * i + (mine + o) % ranks]]
                if o == 0:
                    ex_recv[lv, mine, i] = slab
                else:
                    ex_send[lv, o - 1, i] = slab
                return carry

            lax.fori_loop(0, rows, gather, 0)
    if raws:

        def gather_raw(d, carry):
            raw_send[d] = st[:, source_ref[sources * groups + d]]
            return carry

        lax.fori_loop(0, groups, gather_raw, 0)
    pl.semaphore_wait(barrier, total - 1)

    for o in range(1, ranks):
        push(props_hbm, props.at[mine], R_PROPS, me, (mine + o) % ranks)

    def trade(lv):
        for o in range(1, ranks):
            push(ex_send.at[lv, o - 1], ex_recv.at[lv, mine], R_EX + lv, me, (mine + o) % ranks)

    trade(0)
    block = math.gcd(groups, 4)

    def send_note(t, carry):
        d = turn(t, groups, block, me)
        deliver(note_ref.at[d], note_recv.at[my_side * rows + my_row], R_NOTE, d, mine)
        return carry

    lax.fori_loop(0, groups, send_note, 0)
    if raws:

        def send_raw(t, carry):
            d = turn(t, groups, block, me)
            deliver(raw_send.at[d], raw_recv.at[mine, my_row], R_RAW, d, my_side)
            return carry

        lax.fori_loop(0, groups, send_raw, 0)
    for lv in range(1, sources):
        trade(lv)
    green_copy.wait()
    plane_copy.wait()
    props_copy.wait()
    if ranks > 1:
        drain(props.at[pl.ds(0, ranks - 1)], recv.at[R_PROPS])
    row_block = math.gcd(rows, 2)
    for lv in range(sources):
        if ranks > 1:
            drain(ex_recv.at[lv, pl.ds(0, ranks - 1)], recv.at[R_EX + lv])
        means = solve_rows(ex_recv.at[lv], strain_ref[lv], new_src.at[lv], props, green, plane, buffers)
        mean_src[lv, mine] = means
        for o in range(1, ranks):
            push(mean_src.at[lv, mine], mean_src.at[lv, mine], R_MEAN + lv, me, (mine + o) % ranks)

        def send_new(t, carry, lv=lv):
            i = turn(t, rows, row_block, my_row)
            for o in range(ranks):
                h = (mine + o) % ranks
                deliver(new_src.at[lv, h, i], got.at[lv, me], R_GOT + lv, ranks * i + mine, h)
            return carry

        lax.fori_loop(0, rows, send_new, 0)
    drain(note_recv, recv.at[R_NOTE])
    if raws:
        drain(raw_recv, recv.at[R_RAW])
        strain = note_recv[pl.ds(mine * rows, rows), 0, :]
        means = solve_rows(raw_recv, strain, new_raw, props, green, plane, buffers)
        for i in range(rows):
            mean_stage[i] = jnp.broadcast_to(means[i : i + 1, :], (8, LANES))

        def send_back(t, carry):
            i = turn(t, rows, row_block, my_row)
            for h in range(ranks):
                deliver(mean_stage.at[i], mean_raw.at[me], R_MRAW, ranks * i + mine, h)
            return carry

        lax.fori_loop(0, rows, send_back, 0)

        def send_done(i, carry):
            for o in range(ranks):
                h = (mine + o) % ranks
                deliver(new_raw.at[h, i], got.at[sources, ranks * i + mine], R_GOT + sources, me, h)
            return carry

        lax.fori_loop(0, rows, send_done, 0)
        drain(mean_raw, recv.at[R_MRAW])
    for lv in range(sources):
        if ranks > 1:
            drain(mean_src.at[lv, pl.ds(0, ranks - 1)], recv.at[R_MEAN + lv])
    mean_src_out[...] = mean_src[...]
    mean_raw_out[...] = mean_raw[:, 0, :]
    note_out[...] = note_recv[:, 0, :]
    for lv in range(levels):
        drain(got.at[lv], recv.at[R_GOT + lv])
    own = my_side == mine
    drain(note_ref.at[pl.ds(0, groups - 1)], sent.at[R_NOTE])
    if ranks > 1:
        drain(props.at[pl.ds(0, ranks - 1)], sent.at[R_PROPS])
    for lv in range(sources):
        if ranks > 1:
            drain(ex_send.at[lv], sent.at[R_EX + lv])
            drain(mean_src.at[lv, pl.ds(0, ranks - 1)], sent.at[R_MEAN + lv])
        settle(got.at[lv, pl.ds(0, groups)], got.at[lv, pl.ds(0, groups - 1)], R_GOT + lv, own)
    if raws:
        settle(raw_send, raw_send.at[pl.ds(0, groups - 1)], R_RAW, own)
        settle(mean_raw, mean_raw.at[pl.ds(0, groups - 1)], R_MRAW, own)
        if ranks > 1:
            drain(got.at[sources, pl.ds(0, groups - rows)], sent.at[R_GOT + sources])


def exchange(source, notes, strains, state, moduli, tables, raws):
    groups, ranks = lax.axis_size("macro"), lax.axis_size("vox")
    rows = groups // ranks
    thickness = state.shape[2]
    sources = strains.shape[0]
    levels = sources + raws
    slab = (7, thickness, VOX_PLANE)
    vmem = pl.BlockSpec(memory_space=pltpu.VMEM)
    anywhere = pl.BlockSpec(memory_space=pl.ANY)
    f32 = jnp.float32
    kinds = 4 + 2 * sources + levels
    cells = levels * VOX_SIDE * rows * VOX_PLANE
    return pl.pallas_call(
        functools.partial(exchange_kernel, raws),
        out_shape=[
            jax.ShapeDtypeStruct((levels, groups) + slab, f32),
            jax.ShapeDtypeStruct((sources, ranks, rows, LANES), f32),
            jax.ShapeDtypeStruct((groups, LANES), f32),
            jax.ShapeDtypeStruct((groups, LANES), f32),
        ],
        in_specs=[pl.BlockSpec(memory_space=pltpu.SMEM), vmem, vmem] + [anywhere] * 4,
        out_specs=[anywhere, vmem, vmem, vmem],
        scratch_shapes=[
            pltpu.VMEM(state.shape, f32),
            pltpu.VMEM((groups,) + slab, f32),
            pltpu.VMEM((ranks, rows) + slab, f32),
            pltpu.VMEM((sources, max(ranks - 1, 1), rows) + slab, f32),
            pltpu.VMEM((sources, ranks, rows) + slab, f32),
            pltpu.VMEM((sources, ranks, rows) + slab, f32),
            pltpu.VMEM((ranks, rows) + slab, f32),
            pltpu.VMEM((ranks,) + moduli.shape, f32),
            pltpu.VMEM(tables[0].shape, f32),
            pltpu.VMEM(tables[1].shape, tables[1].dtype),
            pltpu.VMEM((7, VOX_SIDE, rows, VOX_PLANE), f32),
            pltpu.VMEM((6, VOX_SIDE, rows, VOX_PLANE), f32),
            pltpu.VMEM((6, VOX_SIDE, rows, VOX_PLANE), f32),
            pltpu.VMEM((6, HALF + 1, rows, VOX_PLANE), f32),
            pltpu.VMEM((6, HALF - 1, rows, VOX_PLANE), f32),
            pltpu.VMEM((groups, 8, LANES), f32),
            pltpu.VMEM((sources, ranks, rows, LANES), f32),
            pltpu.VMEM((groups, 8, LANES), f32),
            pltpu.VMEM((rows, 8, LANES), f32),
            pltpu.SemaphoreType.DMA((4,)),
            pltpu.SemaphoreType.DMA((kinds,)),
            pltpu.SemaphoreType.DMA((kinds,)),
        ],
        compiler_params=pltpu.CompilerParams(
            collective_id=0, has_side_effects=True, vmem_limit_bytes=48 * 2**20
        ),
        cost_estimate=pl.CostEstimate(
            flops=SWEEPS * 2 * 3 * 2 * 6 * cells * VOX_PLANE,
            bytes_accessed=4 * 7 * cells * 4,
            transcendentals=SWEEPS * cells,
        ),
    )(source, notes, strains, state, moduli, *tables)


def pick_kernel(order_ref, got, out, sem):
    count = out.shape[1]
    groups = got.shape[1]

    def place(j, carry):
        slot = order_ref[j]
        pltpu.make_async_copy(got.at[slot // groups, slot % groups], out.at[:, j], sem).start()
        return carry

    lax.fori_loop(0, count, place, 0)
    drain(out, sem)


def pick_rows(order, got):
    shape = (7, order.shape[0]) + got.shape[3:]
    return pl.pallas_call(
        pick_kernel,
        out_shape=jax.ShapeDtypeStruct(shape, jnp.float32),
        in_specs=[pl.BlockSpec(memory_space=pltpu.SMEM), pl.BlockSpec(memory_space=pl.ANY)],
        out_specs=pl.BlockSpec(memory_space=pltpu.VMEM),
        scratch_shapes=[pltpu.SemaphoreType.DMA],
        compiler_params=pltpu.CompilerParams(vmem_limit_bytes=16 * 2**20),
    )(order, got)


def strain_tensor(disp_el, grad_el):
    products = [[jnp.sum(disp_el[i] * grad_el[j], axis=0) for j in range(3)] for i in range(3)]
    return jnp.stack(
        [
            products[0][0],
            products[1][1],
            products[2][2],
            0.5 * (products[1][2] + products[2][1]),
            0.5 * (products[0][2] + products[2][0]),
            0.5 * (products[0][1] + products[1][0]),
        ]
    )


def full_tensor(voigt):
    return [
        [voigt[0], voigt[5], voigt[4]],
        [voigt[5], voigt[1], voigt[3]],
        [voigt[4], voigt[3], voigt[2]],
    ]


def nodal_forces(stress, grad_el, volume):
    tensor = full_tensor(stress)
    return jnp.stack(
        [
            volume
            * (tensor[i][0] * grad_el[0] + tensor[i][1] * grad_el[1] + tensor[i][2] * grad_el[2])
            for i in range(3)
        ]
    )


def elastic_stress(strain, moduli):
    lame_first = moduli[0]
    shear_mod = moduli[1]
    trace = strain[0] + strain[1] + strain[2]
    return jnp.stack(
        [lame_first * trace + 2.0 * shear_mod * strain[c] for c in range(3)]
        + [2.0 * shear_mod * strain[c] for c in range(3, 6)]
    )


def local(
    displacement,
    load,
    conn,
    halo_list,
    grad_ops,
    volume,
    elastic_moduli,
    plastic_mask,
    new_owner,
    state,
    micro_moduli,
):
    groups = lax.axis_size("macro")
    ranks = lax.axis_size("vox")
    me = lax.axis_index("vox")
    own_nodes = displacement.shape[1]
    elements = conn.shape[1]
    rows = groups // ranks
    tables = (jnp.asarray(green_tables()), plane_tables())
    capacity = (PLASTIC_MAX + groups - 1) // groups
    raws = 1 if capacity > 1 else 0
    sources = capacity - raws
    plastic = plastic_mask == 1
    point_ids = jnp.arange(elements, dtype=jnp.int32)
    same_owner = (
        (new_owner[:, None] == new_owner[None, :])
        & plastic[:, None]
        & plastic[None, :]
        & (point_ids[None, :] < point_ids[:, None])
    )
    owner_rank = jnp.sum(same_owner.astype(jnp.int32), axis=1)
    send_slot = jnp.where(plastic, owner_rank * groups + new_owner, -1)
    slot_ids = jnp.arange(groups * capacity, dtype=jnp.int32)
    slot_match = slot_ids[:, None] == send_slot[None, :]
    match_float = slot_match.astype(jnp.float32)
    slot_source = jnp.sum(jnp.where(slot_match, point_ids[None, :], 0), axis=1)
    node_ids = jnp.arange(own_nodes, dtype=jnp.int32)
    halo_match = (halo_list[:, None] == node_ids[None, :]).astype(jnp.float32)
    halo_out = jnp.dot(displacement, halo_match.T, precision=FULL_PREC)
    halo_disp = shifted(halo_out, "macro", 1)
    local_disp = jnp.concatenate([displacement, halo_disp], axis=1)
    all_ids = jnp.arange(local_disp.shape[1], dtype=jnp.int32)
    node_match = (conn[:, :, None] == all_ids[None, None, :]).astype(jnp.float32)
    disp_el = jnp.einsum("in,aen->iae", local_disp, node_match, precision=FULL_PREC)
    strain = strain_tensor(disp_el, grad_ops)
    slot_strain = jnp.dot(match_float, strain.T, precision=FULL_PREC).reshape(capacity, groups, 6)
    valid = jnp.sum(match_float, axis=1).reshape(capacity, groups)
    note = jnp.concatenate(
        [slot_strain[capacity - 1], jnp.zeros((groups, 2), jnp.float32), valid.T], axis=1
    )
    note = jnp.pad(note, ((0, 0), (0, LANES - note.shape[1])))
    notes = jnp.broadcast_to(note[:, None, :], (groups, 8, LANES))
    own = slot_strain[:sources].reshape(sources, rows, ranks, 6)
    own = lax.dynamic_index_in_dim(own, me, 2, keepdims=False)
    strains = jnp.pad(own, ((0, 0), (0, 0), (0, LANES - 6)))
    got, mean_src, mean_raw, note_got = exchange(slot_source, notes, strains, state, micro_moduli, tables, raws)
    full = note_got[:, 8 : 8 + capacity].reshape(ranks, rows, capacity)
    full = jnp.swapaxes(full, 0, 1).reshape(-1) > 0.5
    places = slot_ids % capacity * groups + slot_ids // capacity
    earlier = (slot_ids[:, None] < slot_ids[None, :]) & full[:, None]
    position = jnp.sum(earlier.astype(jnp.int32), axis=0)
    wanted = jnp.arange(RECV_AGG, dtype=jnp.int32)
    wanted_match = (wanted[:, None] == position[None, :]) & full[None, :]
    order = jnp.sum(jnp.where(wanted_match, places[None, :], 0), axis=1)
    means = jnp.swapaxes(mean_src, 1, 2).reshape(sources * groups, LANES)
    if raws:
        means = jnp.concatenate([means, mean_raw], axis=0)
    stress_plastic = jnp.dot(means[:, :6].T, match_float, precision=FULL_PREC)
    stress = jnp.where(plastic[None, :], stress_plastic, elastic_stress(strain, elastic_moduli))
    forces = nodal_forces(stress, grad_ops, volume)
    assembled = jnp.einsum("iae,aen->in", forces, node_match, precision=FULL_PREC)
    returned_force = shifted(assembled[:, own_nodes:], "macro", -1)
    residual = (
        assembled[:, :own_nodes] + jnp.dot(returned_force, halo_match, precision=FULL_PREC) - load
    )
    return (residual, pick_rows(order, got))


def solution(mesh):
    return jax.shard_map(
        local,
        mesh=mesh,
        in_specs=(
            P(None, "macro"),
            P(None, "macro"),
            P(None, "macro"),
            P("macro"),
            P(None, None, "macro"),
            P("macro"),
            P(None, "macro"),
            P("macro"),
            P("macro"),
            P(None, "macro", "vox", None),
            P(None, "vox", None),
        ),
        out_specs=(P(None, "macro"), P(None, "macro", "vox", None)),
        check_vma=False,
    )
```

```python
import functools
import math

import jax
import jax.numpy as jnp
import numpy as np
from jax import lax
from jax.experimental import pallas as pl
from jax.experimental.pallas import tpu as pltpu
from jax.sharding import PartitionSpec as P

RECV_AGG = 24
PLASTIC_MAX = 48
VOX_SIDE = 16
VOX_PLANE = 256
SWEEPS = 4
HALF = VOX_SIDE // 2
LANES = 128

LAM_REF = 3.0
MU_REF = 3.0

ROOT = math.sqrt(0.5)
COS1 = math.cos(math.pi / 8)
COS3 = math.cos(3 * math.pi / 8)
PAIRS = [(i, j) for i in range(6) for j in range(i, 6)]


def green_tables():
    line = np.arange(VOX_SIDE)
    signed = np.where(line < HALF, line, line - VOX_SIDE).astype(np.float64)
    freq = np.stack(np.meshgrid(signed, signed, signed, indexing="ij"))
    norm = np.sum(freq * freq, axis=0)
    inverse = np.where(norm > 0, 1.0 / np.maximum(norm, 1.0), 0.0)
    coupling = (LAM_REF + MU_REF) / (LAM_REF + 2.0 * MU_REF)
    spots = [(0, 0), (1, 1), (2, 2), (1, 2), (0, 2), (0, 1)]
    table = np.zeros((6, 6) + norm.shape)
    for j, (a, b) in enumerate(spots):
        tau = np.zeros((3, 3))
        tau[a, b] = tau[b, a] = 1.0
        trac = np.einsum("ij,jxyz->ixyz", tau, freq)
        along = np.sum(freq * trac, axis=0) * inverse
        wave = (trac - coupling * along * freq) * inverse / MU_REF
        for i, (c, d) in enumerate(spots):
            table[i, j] = 0.5 * (freq[c] * wave[d] + freq[d] * wave[c])
    back = -line % VOX_SIDE
    flipped = table[:, :, back][:, :, :, back][:, :, :, :, back]
    even = 0.5 * (table + flipped) / VOX_SIDE**3
    even[:, 3:] *= 0.5
    stacked = np.stack([even[i, j] for i, j in PAIRS])
    return stacked.reshape(len(PAIRS), VOX_SIDE, VOX_PLANE).astype(np.float32)


def plane_tables():
    plane = np.arange(VOX_PLANE)
    rows, cols = plane // VOX_SIDE, plane % VOX_SIDE
    phase = (rows[:, None] * rows[None, :] + cols[:, None] * cols[None, :]) % VOX_SIDE
    angle = phase * (2.0 * math.pi / VOX_SIDE)
    plus = jnp.asarray((np.cos(angle) + np.sin(angle)).astype(np.float32))
    minus = jnp.asarray((np.cos(angle) - np.sin(angle)).astype(np.float32))
    out = []
    for table in (plus, minus):
        high = table.astype(jnp.bfloat16)
        out += [high, (table - high.astype(jnp.float32)).astype(jnp.bfloat16)]
    return jnp.stack(out)


def cosine_line(a):
    sums = [None] + [a[x] + a[8 - x] for x in (1, 2, 3)]
    diffs = [None] + [a[x] - a[8 - x] for x in (1, 2, 3)]
    even0, odd0 = a[0] + a[8], a[0] - a[8]
    outer, inner = even0 + a[4], even0 - a[4]
    spread = sums[1] + sums[3]
    slant = ROOT * (sums[1] - sums[3])
    mid = ROOT * diffs[2]
    first = COS1 * diffs[1] + COS3 * diffs[3]
    second = COS3 * diffs[1] - COS1 * diffs[3]
    top, low = odd0 + mid, odd0 - mid
    core = outer + sums[2]
    return [
        core + spread,
        top + first,
        inner + slant,
        low + second,
        outer - sums[2],
        low - second,
        inner - slant,
        top - first,
        core - spread,
    ]


def sine_line(b):
    sums = [None] + [b[x] + b[8 - x] for x in (1, 2, 3)]
    diffs = [None] + [b[x] - b[8 - x] for x in (1, 2, 3)]
    slant = ROOT * (diffs[1] + diffs[3])
    mid = ROOT * sums[2]
    first = COS3 * sums[1] + COS1 * sums[3]
    second = COS1 * sums[1] - COS3 * sums[3]
    return [
        None,
        (first + mid) + b[4],
        slant + diffs[2],
        (second + mid) - b[4],
        diffs[1] - diffs[3],
        (second - mid) + b[4],
        slant - diffs[2],
        (first - mid) - b[4],
    ]


def split_dot(block, table_ref, first):
    high = block.astype(jnp.bfloat16)
    low = (block - high.astype(jnp.float32)).astype(jnp.bfloat16)
    dot = functools.partial(jnp.dot, preferred_element_type=jnp.float32)
    return dot(high, table_ref[first]) + (dot(high, table_ref[first + 1]) + dot(low, table_ref[first]))


def voxel_law(strain, state, props, row):
    lam, mu = props[0, row, :], props[1, row, :]
    yield_base, harden = props[2, row, :], props[3, row, :]
    two_mu, three_mu = 2.0 * mu, 3.0 * mu
    stiff_inv = 1.0 / (three_mu + harden)
    bulk = lam + two_mu * (1.0 / 3.0)
    elastic = [strain[c] - state[c] for c in range(6)]
    trace = elastic[0] + elastic[1] + elastic[2]
    third = trace * (1.0 / 3.0)
    shape = [elastic[c] - third for c in range(3)] + elastic[3:]
    normal = shape[0] * shape[0] + shape[1] * shape[1] + shape[2] * shape[2]
    shear = shape[3] * shape[3] + shape[4] * shape[4] + shape[5] * shape[5]
    equivalent = two_mu * jnp.sqrt(1.5 * (normal + 2.0 * shear))
    strength = yield_base + harden * state[6]
    gain = jnp.maximum(equivalent - strength, 0.0) * stiff_inv
    factor = gain / jnp.maximum(equivalent, strength)
    keep = two_mu * (1.0 - three_mu * factor)
    pressure = bulk * trace
    stress = [pressure + keep * shape[c] for c in range(3)] + [keep * shape[c] for c in range(3, 6)]
    return stress, shape, (1.5 * two_mu) * factor, gain


def solve_rows(pieces, strain, out, props, green, plane, buffers):
    stx, eps, work, cos_ref, sin_ref = buffers
    ranks, rows, _, thickness, _ = pieces.shape

    def bring(c, carry):
        for h in range(ranks):
            stx[c, h * thickness : (h + 1) * thickness] = jnp.swapaxes(pieces[h, :, c], 0, 1)
        return carry

    lax.fori_loop(0, 7, bring, 0)
    for c in range(6):
        eps[c] = jnp.broadcast_to(strain[:, c : c + 1][None], (VOX_SIDE, rows, VOX_PLANE))

    def sweep(step, carry):
        for h in range(ranks):

            def law(place, inner, h=h):
                x = h * thickness + place
                strain = [eps[c, x] for c in range(6)]
                state = [stx[c, x] for c in range(7)]
                stress = voxel_law(strain, state, props.at[h], pl.ds(place, 1))[0]
                for c in range(6):
                    work[c, x] = stress[c]
                return inner

            lax.fori_loop(0, thickness, law, 0)

        def forward(c, inner):
            field = [work[c, x] for x in range(VOX_SIDE)]
            sums = [field[0]] + [field[x] + field[VOX_SIDE - x] for x in range(1, HALF)] + [field[HALF]]
            diffs = [None] + [field[x] - field[VOX_SIDE - x] for x in range(1, HALF)]
            for k, value in enumerate(cosine_line(sums)):
                cos_ref[c, k] = value
            for k, value in enumerate(sine_line(diffs)):
                if k > 0:
                    sin_ref[c, k - 1] = value
            return inner

        lax.fori_loop(0, 6, forward, 0)

        def transform():
            for ref, first in ((cos_ref, 0), (sin_ref, 2)):
                flat = ref[...].reshape(6 * ref.shape[1] * rows, VOX_PLANE)
                ref[...] = split_dot(flat, plane, first).reshape(ref.shape)

        def apply(field, k):
            row = pl.ds(k, 1)
            field = field[:3] + [2.0 * field[c] for c in range(3, 6)]
            total = [None] * 6
            for n, (i, j) in enumerate(PAIRS):
                entry = green[n, row, :]
                for a, b in [(i, j), (j, i)][: 1 + (i != j)]:
                    term = entry * field[b]
                    total[a] = term if total[a] is None else total[a] + term
            return total

        transform()
        for k in (0, HALF):
            result = apply([cos_ref[c, k] for c in range(6)], k)
            for c in range(6):
                cos_ref[c, k] = result[c]

        def mix(k, inner):
            even = [cos_ref[c, k] for c in range(6)]
            odd = [sin_ref[c, k - 1] for c in range(6)]
            ahead = apply([even[c] + odd[c] for c in range(6)], k)
            behind = apply([even[c] - odd[c] for c in range(6)], VOX_SIDE - k)
            for c in range(6):
                cos_ref[c, k] = ahead[c] + behind[c]
                sin_ref[c, k - 1] = ahead[c] - behind[c]
            return inner

        lax.fori_loop(1, HALF, mix, 0)
        transform()

        def backward(c, inner):
            even = cosine_line([cos_ref[c, k] for k in range(HALF + 1)])
            odd = sine_line([None] + [sin_ref[c, k - 1] for k in range(1, HALF)])
            eps[c, 0] = eps[c, 0] - even[0]
            eps[c, HALF] = eps[c, HALF] - even[HALF]
            for x in range(1, HALF):
                eps[c, x] = eps[c, x] - (even[x] + odd[x])
                eps[c, VOX_SIDE - x] = eps[c, VOX_SIDE - x] - (even[x] - odd[x])
            return inner

        lax.fori_loop(0, 6, backward, 0)
        return carry

    lax.fori_loop(0, SWEEPS, sweep, 0)
    totals = (jnp.zeros((rows, VOX_PLANE), jnp.float32),) * 6
    for h in range(ranks):

        def finish(place, totals, h=h):
            x = h * thickness + place
            strain = [eps[c, x] for c in range(6)]
            state = [stx[c, x] for c in range(7)]
            stress, shape, scale, gain = voxel_law(strain, state, props.at[h], pl.ds(place, 1))
            for c in range(6):
                stx[c, x] = state[c] + scale * shape[c]
            stx[6, x] = state[6] + gain
            return tuple(totals[c] + stress[c] for c in range(6))

        totals = lax.fori_loop(0, thickness, finish, totals)

    def give(c, carry):
        for h in range(ranks):
            out[h, :, c] = jnp.swapaxes(stx[c, h * thickness : (h + 1) * thickness], 0, 1)
        return carry

    lax.fori_loop(0, 7, give, 0)
    lane = lax.broadcasted_iota(jnp.int32, (rows, LANES), 1)
    means = jnp.zeros((rows, LANES), jnp.float32)
    for c in range(6):
        total = jnp.sum(totals[c], axis=1, keepdims=True) / VOX_SIDE**3
        means = jnp.where(lane == c, total, means)
    return means


def drain(ref, sem):
    pltpu.make_async_copy(ref, ref, sem).wait()


def pieces_of(value):
    high = value.astype(jnp.bfloat16)
    rest = value - high.astype(jnp.float32)
    middle = rest.astype(jnp.bfloat16)
    low = (rest - middle.astype(jnp.float32)).astype(jnp.bfloat16)
    return high, middle, low


def select_dot(value, match, lanes):
    contract = (((1,), (1 if lanes else 0,)), ((), ()))
    parts = [
        lax.dot_general(piece, match, contract, preferred_element_type=jnp.float32)
        for piece in pieces_of(value)
    ]
    return parts[0] + (parts[1] + parts[2])


def count_up(shape, axis):
    return lax.broadcasted_iota(jnp.int32, shape, axis)


def to_column(row, size):
    spot = count_up((size, LANES), 0) == count_up((size, LANES), 1)
    return jnp.sum(jnp.where(spot, row, 0.0), axis=1, keepdims=True)


def exchange_kernel(raws, *refs):
    (disp_hbm, load_hbm, conn_hbm, halo_hbm, grad_hbm, volume_hbm, moduli_hbm, owner_hbm) = refs[:8]
    (state_hbm, props_hbm, green_hbm, plane_hbm) = refs[8:12]
    got, residual, order_out = refs[12:15]
    (st, raw_send, raw_recv, ex_send, ex_recv, new_src, new_raw, props, green, plane) = refs[15:25]
    buffers = refs[25:30]
    (note_send, note_recv, mean_src, mean_raw, mean_stage, mean_all) = refs[30:36]
    (halo_send, halo_recv, force_send, force_recv, strain_ref, onehot, forces, rows_i) = refs[36:44]
    (disp, load, conn, halo, grad, volume, moduli, owner, source_vec, source_ref) = refs[44:54]
    load_sem, recv, sent = refs[54:]
    levels, groups = got.shape[:2]
    ranks, rows = ex_recv.shape[1:3]
    own_nodes, elements, halos = disp.shape[1], conn.shape[1], halo.shape[1]
    sources = levels - raws
    me, mine = lax.axis_index("macro"), lax.axis_index("vox")
    my_row, my_side = me // ranks, me % ranks
    raw_side = (mine + ranks * groups - me) % ranks
    R_PROPS, R_NOTE, R_RAW, R_MRAW, R_HALO, R_FORCE, R_EX = range(7)
    R_MEAN, R_GOT = R_EX + sources, R_EX + 2 * sources
    f32 = jnp.float32

    def push(src, dst, kind, group, rank):
        pltpu.make_async_remote_copy(
            src_ref=src,
            dst_ref=dst,
            send_sem=sent.at[kind],
            recv_sem=recv.at[kind],
            device_id={"macro": group, "vox": rank},
            device_id_type=pl.DeviceIdType.MESH,
        ).start()

    def deliver(src, dst, kind, group, rank):
        here = (group == me) & (rank == mine)

        @pl.when(here)
        def _():
            pltpu.make_async_copy(src, dst, recv.at[kind]).start()

        @pl.when(jnp.logical_not(here))
        def _():
            push(src, dst, kind, group, rank)

    def settle(ref, kind, fewer):
        count = ref.shape[0]

        @pl.when(fewer)
        def _():
            drain(ref.at[pl.ds(0, count - 1)], sent.at[kind])

        @pl.when(jnp.logical_not(fewer))
        def _():
            drain(ref, sent.at[kind])

    def turn(step, count, block, spot):
        planes = count // block
        line, lane = spot // block, spot % block
        ring = step // block
        line = jnp.where(2 * line < planes, planes - 1 - ring, ring)
        return line * block + (lane + step) % block

    fetches = {}
    for n, (src, dst) in enumerate(
        (
            (owner_hbm, owner),
            (halo_hbm, halo),
            (disp_hbm, disp),
            (state_hbm, st),
            (conn_hbm, conn),
            (grad_hbm, grad),
            (props_hbm, props.at[mine]),
            (green_hbm, green),
            (plane_hbm, plane),
            (volume_hbm, volume),
            (moduli_hbm, moduli),
            (load_hbm, load),
        )
    ):
        fetches[n] = pltpu.make_async_copy(src, dst, load_sem.at[n])
        fetches[n].start()

    barrier = pltpu.get_barrier_semaphore()
    total = groups * ranks
    flat = me * ranks + mine

    def greet(k, carry):
        other = (flat + k) % total
        pl.semaphore_signal(
            barrier,
            inc=1,
            device_id={"macro": other // ranks, "vox": other % ranks},
            device_id_type=pl.DeviceIdType.MESH,
        )
        return carry

    lax.fori_loop(1, total, greet, 0)

    rows_i[...] = jnp.full(rows_i.shape, -1, jnp.int32)
    fetches[0].wait()
    rows_i[0:1, 0:elements] = owner[...]
    owner_row = rows_i[0:1, :].astype(f32)
    square = (LANES, LANES)
    owner_col = to_column(owner_row, LANES)
    before = count_up(square, 0) < count_up(square, 1)
    same = (owner_col == owner_row) & before
    rank_row = jnp.sum(jnp.where(same, 1.0, 0.0), axis=0, keepdims=True)
    slot_row = jnp.where(owner_row >= 0.0, rank_row * groups + owner_row, -1.0)
    slot_col = to_column(slot_row, LANES)
    hit = slot_col == count_up(square, 1).astype(f32)
    spots = jnp.where(hit, count_up(square, 0).astype(f32), 0.0)
    source_vec[...] = jnp.sum(spots, axis=0, keepdims=True).astype(jnp.int32)
    to_scalars = pltpu.make_async_copy(source_vec, source_ref, load_sem.at[12])
    to_scalars.start()

    fetches[1].wait()
    fetches[2].wait()
    rows_i[1:2, own_nodes : own_nodes + halos] = halo[...]
    halo_match = (count_up(square, 0) == rows_i[1:2, :]).astype(jnp.bfloat16)
    halo_send[...] = jnp.zeros(halo_send.shape, f32)
    halo_send[0:3, 0:own_nodes] = disp[...]
    own_disp = halo_send[...]
    halo_send[...] = select_dot(own_disp, halo_match, False)

    to_scalars.wait()
    fetches[3].wait()

    def slab_of(slot):
        return st[:, jnp.clip(source_ref[0, slot], 0, elements - 1)]

    def gather_trade(lv):
        for o in range(ranks):

            def gather(i, carry, o=o):
                slab = slab_of(lv * groups + ranks * i + (mine + o) % ranks)
                if o == 0:
                    ex_recv[lv, mine, i] = slab
                else:
                    ex_send[lv, o - 1, i] = slab
                return carry

            lax.fori_loop(0, rows, gather, 0)

    for lv in range(sources):
        gather_trade(lv)
    if raws:

        def gather_raw(d, carry):
            raw_send[d] = slab_of(sources * groups + d)
            return carry

        lax.fori_loop(0, groups, gather_raw, 0)
    pl.semaphore_wait(barrier, total - 1)

    row_block = math.gcd(rows, 2)

    def trade(lv):
        for o in range(1, ranks):
            push(ex_send.at[lv, o - 1], ex_recv.at[lv, mine], R_EX + lv, me, (mine + o) % ranks)

    def send_raw(o):
        side = (mine + o) % ranks

        def step(t, carry):
            d = ranks * turn(t, rows, row_block, my_row) + (side + ranks * groups - me) % ranks
            deliver(raw_send.at[d], raw_recv.at[mine, my_row], R_RAW, d, side)
            return carry

        lax.fori_loop(0, rows, step, 0)

    push(halo_send, halo_recv, R_HALO, (me + 1) % groups, mine)
    for o in range(1, ranks):
        push(props_hbm, props.at[mine], R_PROPS, me, (mine + o) % ranks)
    trade(0)
    if raws:
        send_raw(0)

    fetches[4].wait()
    fetches[5].wait()
    tall = (LANES, elements)
    for a in range(conn.shape[0]):
        onehot[a] = (count_up(tall, 0) == conn[a : a + 1, :]).astype(jnp.bfloat16)
    drain(halo_recv, recv.at[R_HALO])
    lane8 = count_up((8, LANES), 1)
    near = jnp.where(lane8 < own_nodes, own_disp, halo_recv[...])
    products = [jnp.zeros((8, elements), f32) for _ in range(3)]
    for a in range(conn.shape[0]):
        moved = select_dot(near, onehot[a], False)
        for j in range(3):
            products[j] = products[j] + moved * grad[j, a : a + 1, :]
    strain_ref[...] = jnp.zeros(strain_ref.shape, f32)
    strain_rows = [
        products[0][0:1],
        products[1][1:2],
        products[2][2:3],
        0.5 * (products[2][1:2] + products[1][2:3]),
        0.5 * (products[2][0:1] + products[0][2:3]),
        0.5 * (products[1][0:1] + products[0][1:2]),
    ]
    for c in range(6):
        strain_ref[c : c + 1, 0:elements] = strain_rows[c]
    all_strain = strain_ref[...]

    def matched(ids):
        return ids.astype(f32) == slot_row

    wide = (groups, LANES)
    note = jnp.zeros(wide, f32)
    if raws:
        hits = matched(count_up(wide, 0) + sources * groups)
        match = jnp.where(hits, 1.0, 0.0).astype(jnp.bfloat16)
        pieces = [
            lax.dot_general(match, piece, (((1,), (1,)), ((), ())), preferred_element_type=f32)
            for piece in pieces_of(all_strain)
        ]
        note = pieces[0] + (pieces[1] + pieces[2])
    for lv in range(levels):
        held = jnp.where(matched(count_up(wide, 0) + lv * groups), 1.0, 0.0)
        note = jnp.where(count_up(wide, 1) == 8 + lv, jnp.sum(held, axis=1, keepdims=True), note)
    for d in range(groups):
        note_send[d] = jnp.broadcast_to(note[d : d + 1, :], (8, LANES))

    def send_note(t, carry):
        d = turn(t, groups, math.gcd(groups, 4), me)
        deliver(note_send.at[d], note_recv.at[my_side * rows + my_row], R_NOTE, d, mine)
        return carry

    lax.fori_loop(0, groups, send_note, 0)
    for lv in range(1, sources):
        trade(lv)
    if raws:
        for o in range(1, ranks):
            send_raw(o)
    fetches[6].wait()
    fetches[7].wait()
    fetches[8].wait()
    if ranks > 1:
        drain(props.at[pl.ds(0, ranks - 1)], recv.at[R_PROPS])

    def send_new(lv, low, high):
        def step(t, carry):
            i = turn(t, rows, row_block, my_row)
            for o in range(ranks):
                h = (mine + o) % ranks
                deliver(new_src.at[lv, h, i], got.at[lv, me], R_GOT + lv, ranks * i + mine, h)
            return carry

        lax.fori_loop(low, high, step, 0)

    first, second = rows, rows
    if raws:
        first, second = rows // 4, rows - rows // 4
    for lv in range(sources):
        ids = lv * groups + ranks * count_up((rows, LANES), 0) + mine
        match = jnp.where(matched(ids), 1.0, 0.0).astype(jnp.bfloat16)
        pieces = [
            lax.dot_general(match, piece, (((1,), (1,)), ((), ())), preferred_element_type=f32)
            for piece in pieces_of(all_strain)
        ]
        strain = pieces[0] + (pieces[1] + pieces[2])
        if ranks > 1:
            drain(ex_recv.at[lv, pl.ds(0, ranks - 1)], recv.at[R_EX + lv])
        means = solve_rows(ex_recv.at[lv], strain, new_src.at[lv], props, green, plane, buffers)
        mean_src[lv, mine] = means
        for o in range(1, ranks):
            push(mean_src.at[lv, mine], mean_src.at[lv, mine], R_MEAN + lv, me, (mine + o) % ranks)
        send_new(lv, 0, rows if lv < sources - 1 else first)

    drain(note_recv, recv.at[R_NOTE])
    flags = note_recv[:, 0, :]
    spot = count_up(wide, 0)
    giver = (ranks * (spot % rows) + spot // rows).astype(f32)
    lane = count_up(wide, 1)
    counts = jnp.sum(jnp.where((lane >= 8) & (lane < 8 + levels), flags, 0.0), axis=1, keepdims=True)
    tall_count = jnp.sum(
        jnp.where(
            (count_up(wide, 0) == lane) & (lane < groups), jnp.broadcast_to(counts, wide), 0.0
        ),
        axis=0,
        keepdims=True,
    )
    lane_giver = (ranks * (lane % rows) + lane // rows).astype(f32)
    earlier = (lane_giver < giver) & (lane < groups)
    place = jnp.sum(jnp.where(earlier, tall_count, 0.0), axis=1, keepdims=True)
    picks = jnp.zeros((1, LANES), f32)
    for lv in range(levels):
        held = jnp.sum(jnp.where(lane == 8 + lv, flags, 0.0), axis=1, keepdims=True)
        chosen = (place == lane.astype(f32)) & (held > 0.5)
        picks = picks + jnp.sum(jnp.where(chosen, lv * groups + giver, 0.0), axis=0, keepdims=True)
        place = place + held
    order_out[...] = picks.astype(jnp.int32)

    if raws:
        drain(raw_recv, recv.at[R_RAW])
        strain = note_recv[pl.ds(raw_side * rows, rows), 0, :]
        means = solve_rows(raw_recv, strain, new_raw, props, green, plane, buffers)
        for i in range(rows):
            mean_stage[i] = jnp.broadcast_to(means[i : i + 1, :], (8, LANES))

        def send_back(t, carry):
            i = turn(t, rows, row_block, my_row)
            for h in range(ranks):
                deliver(mean_stage.at[i], mean_raw.at[me], R_MRAW, ranks * i + raw_side, h)
            return carry

        lax.fori_loop(0, rows, send_back, 0)

        def send_done(i, carry):
            for o in range(ranks):
                h = (mine + o) % ranks
                deliver(new_raw.at[h, i], got.at[sources, ranks * i + raw_side], R_GOT + sources, me, h)
            return carry

        lax.fori_loop(0, rows, send_done, 0)
        send_new(sources - 1, first, second)

    fetches[9].wait()
    fetches[10].wait()
    fetches[11].wait()
    for lv in range(sources):
        if ranks > 1:
            drain(mean_src.at[lv, pl.ds(0, ranks - 1)], recv.at[R_MEAN + lv])
        for y in range(ranks):
            mean_all[lv * groups + y * rows : lv * groups + (y + 1) * rows, :] = mean_src[lv, y]
    if raws:
        drain(mean_raw, recv.at[R_MRAW])
        mean_all[sources * groups :, :] = mean_raw[:, 0, :]
    deep = (levels * groups, LANES)
    k = count_up(deep, 0)
    inside = k % groups
    known = k - inside + jnp.where(
        k < sources * groups, ranks * (inside % rows) + inside // rows, inside
    )
    match = jnp.where(matched(known), 1.0, 0.0).astype(jnp.bfloat16)
    mean_t = jnp.transpose(mean_all[...])[0:8, :]
    averaged = select_dot(mean_t, match, False)[:, 0:elements]
    strain = all_strain[0:8, 0:elements]
    lame, shear = moduli[0:1, :], moduli[1:2, :]
    lateral = lame * (strain[0:1] + strain[1:2] + strain[2:3])
    plastic = owner[...] >= 0
    stress = []
    for c in range(6):
        plain = 2.0 * shear * strain[c : c + 1]
        plain = lateral + plain if c < 3 else plain
        stress.append(jnp.where(plastic, averaged[c : c + 1], plain))
    tensor = [[stress[0], stress[5], stress[4]], [stress[5], stress[1], stress[3]], [stress[4], stress[3], stress[2]]]
    forces[...] = jnp.zeros(forces.shape, f32)
    for i in range(3):
        force = volume[...] * (
            tensor[i][0] * grad[0] + tensor[i][1] * grad[1] + tensor[i][2] * grad[2]
        )
        for a in range(conn.shape[0]):
            forces[a, i : i + 1, :] = force[a : a + 1, :]
    assembled = jnp.zeros((8, LANES), f32)
    for a in range(conn.shape[0]):
        assembled = assembled + select_dot(forces[a], onehot[a], True)
    force_send[...] = assembled
    push(force_send, force_recv, R_FORCE, (me + groups - 1) % groups, mine)
    if raws:
        send_new(sources - 1, second, rows)
    drain(force_recv, recv.at[R_FORCE])
    lane8 = count_up((8, LANES), 1)
    beyond = (lane8 >= own_nodes) & (lane8 < own_nodes + halos)
    back = jnp.where(beyond, force_recv[...], 0.0)
    total_force = assembled + select_dot(back, halo_match, True)
    residual[...] = total_force[0:3, 0:own_nodes] - load[...]

    for lv in range(levels):
        drain(got.at[lv], recv.at[R_GOT + lv])
    drain(note_send.at[pl.ds(0, groups - 1)], sent.at[R_NOTE])
    drain(halo_send, sent.at[R_HALO])
    drain(force_send, sent.at[R_FORCE])
    if ranks > 1:
        drain(props.at[pl.ds(0, ranks - 1)], sent.at[R_PROPS])
    for lv in range(sources):
        if ranks > 1:
            drain(ex_send.at[lv], sent.at[R_EX + lv])
            drain(mean_src.at[lv, pl.ds(0, ranks - 1)], sent.at[R_MEAN + lv])
        settle(got.at[lv], R_GOT + lv, my_side == mine)
    if raws:
        own = (2 * me) % ranks == mine
        settle(raw_send, R_RAW, own)
        settle(mean_raw, R_MRAW, own)
        if ranks > 1:
            drain(got.at[sources, pl.ds(0, groups - rows)], sent.at[R_GOT + sources])


def exchange(smalls, state, moduli, tables, levels, raws):
    groups, ranks = lax.axis_size("macro"), lax.axis_size("vox")
    rows = groups // ranks
    thickness = state.shape[2]
    sources = levels - raws
    nodes, corners, elements = smalls[0].shape[1], smalls[2].shape[0], smalls[2].shape[1]
    slab = (7, thickness, VOX_PLANE)
    hbm = pl.BlockSpec(memory_space=pltpu.HBM)
    vmem = pl.BlockSpec(memory_space=pltpu.VMEM)
    f32 = jnp.float32
    kinds = 7 + 2 * sources + levels
    cells = levels * VOX_SIDE * rows * VOX_PLANE
    tile = pltpu.VMEM((8, LANES), f32)
    return pl.pallas_call(
        functools.partial(exchange_kernel, raws),
        out_shape=[
            jax.ShapeDtypeStruct((levels, groups) + slab, f32),
            jax.ShapeDtypeStruct((3, nodes), f32),
            jax.ShapeDtypeStruct((1, LANES), jnp.int32),
        ],
        in_specs=[hbm] * (len(smalls) + 2 + len(tables)),
        out_specs=[pl.BlockSpec(memory_space=pl.ANY), vmem, vmem],
        scratch_shapes=[
            pltpu.VMEM(state.shape, f32),
            pltpu.VMEM((groups,) + slab, f32),
            pltpu.VMEM((ranks, rows) + slab, f32),
            pltpu.VMEM((sources, max(ranks - 1, 1), rows) + slab, f32),
            pltpu.VMEM((sources, ranks, rows) + slab, f32),
            pltpu.VMEM((sources, ranks, rows) + slab, f32),
            pltpu.VMEM((ranks, rows) + slab, f32),
            pltpu.VMEM((ranks,) + moduli.shape, f32),
            pltpu.VMEM(tables[0].shape, f32),
            pltpu.VMEM(tables[1].shape, tables[1].dtype),
            pltpu.VMEM((7, VOX_SIDE, rows, VOX_PLANE), f32),
            pltpu.VMEM((6, VOX_SIDE, rows, VOX_PLANE), f32),
            pltpu.VMEM((6, VOX_SIDE, rows, VOX_PLANE), f32),
            pltpu.VMEM((6, HALF + 1, rows, VOX_PLANE), f32),
            pltpu.VMEM((6, HALF - 1, rows, VOX_PLANE), f32),
            pltpu.VMEM((groups, 8, LANES), f32),
            pltpu.VMEM((groups, 8, LANES), f32),
            pltpu.VMEM((sources, ranks, rows, LANES), f32),
            pltpu.VMEM((groups, 8, LANES), f32),
            pltpu.VMEM((rows, 8, LANES), f32),
            pltpu.VMEM((levels * groups, LANES), f32),
            tile,
            tile,
            tile,
            tile,
            pltpu.VMEM((LANES, LANES), f32),
            pltpu.VMEM((corners, LANES, elements), jnp.bfloat16),
            pltpu.VMEM((corners, 8, elements), f32),
            pltpu.VMEM((8, LANES), jnp.int32),
        ]
        + [pltpu.VMEM(small.shape, small.dtype) for small in smalls]
        + [
            pltpu.VMEM((1, LANES), jnp.int32),
            pltpu.SMEM((1, LANES), jnp.int32),
            pltpu.SemaphoreType.DMA((13,)),
            pltpu.SemaphoreType.DMA((kinds,)),
            pltpu.SemaphoreType.DMA((kinds,)),
        ],
        compiler_params=pltpu.CompilerParams(
            collective_id=0, has_side_effects=True, vmem_limit_bytes=48 * 2**20
        ),
        cost_estimate=pl.CostEstimate(
            flops=SWEEPS * 2 * 3 * 2 * 6 * cells * VOX_PLANE,
            bytes_accessed=4 * 7 * cells * 4,
            transcendentals=SWEEPS * cells,
        ),
    )(*smalls, state, moduli, *tables)


def pick_kernel(order_ref, got, out, sem):
    count = out.shape[1]
    groups = got.shape[1]

    def place(j, carry):
        slot = order_ref[0, j]
        pltpu.make_async_copy(got.at[slot // groups, slot % groups], out.at[:, j], sem).start()
        return carry

    lax.fori_loop(0, count, place, 0)
    drain(out, sem)


def pick_rows(order, got):
    return pl.pallas_call(
        pick_kernel,
        out_shape=jax.ShapeDtypeStruct((7, RECV_AGG) + got.shape[3:], jnp.float32),
        in_specs=[pl.BlockSpec(memory_space=pltpu.SMEM), pl.BlockSpec(memory_space=pl.ANY)],
        out_specs=pl.BlockSpec(memory_space=pltpu.VMEM),
        scratch_shapes=[pltpu.SemaphoreType.DMA],
        compiler_params=pltpu.CompilerParams(vmem_limit_bytes=16 * 2**20),
    )(order, got)


def local(
    displacement,
    load,
    conn,
    halo_list,
    grad_ops,
    volume,
    elastic_moduli,
    plastic_mask,
    new_owner,
    state,
    micro_moduli,
):
    groups = lax.axis_size("macro")
    tables = (jnp.asarray(green_tables()), plane_tables())
    levels = (PLASTIC_MAX + groups - 1) // groups
    raws = 1 if levels > 1 else 0
    smalls = (
        displacement,
        load,
        conn,
        halo_list[None, :],
        grad_ops,
        volume[None, :],
        elastic_moduli,
        new_owner[None, :],
    )
    got, residual, order = exchange(smalls, state, micro_moduli, tables, levels, raws)
    return (residual, pick_rows(order, got))


def solution(mesh):
    return jax.shard_map(
        local,
        mesh=mesh,
        in_specs=(
            P(None, "macro"),
            P(None, "macro"),
            P(None, "macro"),
            P("macro"),
            P(None, None, "macro"),
            P("macro"),
            P(None, "macro"),
            P("macro"),
            P("macro"),
            P(None, "macro", "vox", None),
            P(None, "vox", None),
        ),
        out_specs=(P(None, "macro"), P(None, "macro", "vox", None)),
        check_vma=False,
    )
```

```python
import functools
import math

import jax
import jax.numpy as jnp
import numpy as np
from jax import lax
from jax.experimental import pallas as pl
from jax.experimental.pallas import tpu as pltpu
from jax.sharding import PartitionSpec as P

RECV_AGG = 24
PLASTIC_MAX = 48
VOX_SIDE = 16
VOX_PLANE = 256
SWEEPS = 4
HALF = VOX_SIDE // 2
LANES = 128

LAM_REF = 3.0
MU_REF = 3.0

ROOT = math.sqrt(0.5)
COS1 = math.cos(math.pi / 8)
COS3 = math.cos(3 * math.pi / 8)
PAIRS = [(i, j) for i in range(6) for j in range(i, 6)]


def green_tables():
    line = np.arange(VOX_SIDE)
    signed = np.where(line < HALF, line, line - VOX_SIDE).astype(np.float64)
    freq = np.stack(np.meshgrid(signed, signed, signed, indexing="ij"))
    norm = np.sum(freq * freq, axis=0)
    inverse = np.where(norm > 0, 1.0 / np.maximum(norm, 1.0), 0.0)
    coupling = (LAM_REF + MU_REF) / (LAM_REF + 2.0 * MU_REF)
    spots = [(0, 0), (1, 1), (2, 2), (1, 2), (0, 2), (0, 1)]
    table = np.zeros((6, 6) + norm.shape)
    for j, (a, b) in enumerate(spots):
        tau = np.zeros((3, 3))
        tau[a, b] = tau[b, a] = 1.0
        trac = np.einsum("ij,jxyz->ixyz", tau, freq)
        along = np.sum(freq * trac, axis=0) * inverse
        wave = (trac - coupling * along * freq) * inverse / MU_REF
        for i, (c, d) in enumerate(spots):
            table[i, j] = 0.5 * (freq[c] * wave[d] + freq[d] * wave[c])
    back = -line % VOX_SIDE
    flipped = table[:, :, back][:, :, :, back][:, :, :, :, back]
    even = 0.5 * (table + flipped) / VOX_SIDE**3
    even[:, 3:] *= 0.5
    stacked = np.stack([even[i, j] for i, j in PAIRS])
    return stacked.reshape(len(PAIRS), VOX_SIDE, VOX_PLANE).astype(np.float32)


def plane_tables():
    plane = np.arange(VOX_PLANE)
    rows, cols = plane // VOX_SIDE, plane % VOX_SIDE
    phase = (rows[:, None] * rows[None, :] + cols[:, None] * cols[None, :]) % VOX_SIDE
    angle = phase * (2.0 * math.pi / VOX_SIDE)
    plus = jnp.asarray((np.cos(angle) + np.sin(angle)).astype(np.float32))
    minus = jnp.asarray((np.cos(angle) - np.sin(angle)).astype(np.float32))
    out = []
    for table in (plus, minus):
        high = table.astype(jnp.bfloat16)
        out += [high, (table - high.astype(jnp.float32)).astype(jnp.bfloat16)]
    return jnp.stack(out)


def cosine_line(a):
    sums = [None] + [a[x] + a[8 - x] for x in (1, 2, 3)]
    diffs = [None] + [a[x] - a[8 - x] for x in (1, 2, 3)]
    even0, odd0 = a[0] + a[8], a[0] - a[8]
    outer, inner = even0 + a[4], even0 - a[4]
    spread = sums[1] + sums[3]
    slant = ROOT * (sums[1] - sums[3])
    mid = ROOT * diffs[2]
    first = COS1 * diffs[1] + COS3 * diffs[3]
    second = COS3 * diffs[1] - COS1 * diffs[3]
    top, low = odd0 + mid, odd0 - mid
    core = outer + sums[2]
    return [
        core + spread,
        top + first,
        inner + slant,
        low + second,
        outer - sums[2],
        low - second,
        inner - slant,
        top - first,
        core - spread,
    ]


def sine_line(b):
    sums = [None] + [b[x] + b[8 - x] for x in (1, 2, 3)]
    diffs = [None] + [b[x] - b[8 - x] for x in (1, 2, 3)]
    slant = ROOT * (diffs[1] + diffs[3])
    mid = ROOT * sums[2]
    first = COS3 * sums[1] + COS1 * sums[3]
    second = COS1 * sums[1] - COS3 * sums[3]
    return [
        None,
        (first + mid) + b[4],
        slant + diffs[2],
        (second + mid) - b[4],
        diffs[1] - diffs[3],
        (second - mid) + b[4],
        slant - diffs[2],
        (first - mid) - b[4],
    ]


def split_dot(block, table_ref, first):
    high = block.astype(jnp.bfloat16)
    low = (block - high.astype(jnp.float32)).astype(jnp.bfloat16)
    dot = functools.partial(jnp.dot, preferred_element_type=jnp.float32)
    return dot(high, table_ref[first]) + (dot(high, table_ref[first + 1]) + dot(low, table_ref[first]))


def voxel_law(strain, state, props, row):
    lam, mu = props[0, row, :], props[1, row, :]
    yield_base, harden = props[2, row, :], props[3, row, :]
    two_mu, three_mu = 2.0 * mu, 3.0 * mu
    stiff_inv = 1.0 / (three_mu + harden)
    bulk = lam + two_mu * (1.0 / 3.0)
    elastic = [strain[c] - state[c] for c in range(6)]
    trace = elastic[0] + elastic[1] + elastic[2]
    third = trace * (1.0 / 3.0)
    shape = [elastic[c] - third for c in range(3)] + elastic[3:]
    normal = shape[0] * shape[0] + shape[1] * shape[1] + shape[2] * shape[2]
    shear = shape[3] * shape[3] + shape[4] * shape[4] + shape[5] * shape[5]
    equivalent = two_mu * jnp.sqrt(1.5 * (normal + 2.0 * shear))
    strength = yield_base + harden * state[6]
    gain = jnp.maximum(equivalent - strength, 0.0) * stiff_inv
    factor = gain / jnp.maximum(equivalent, strength)
    keep = two_mu * (1.0 - three_mu * factor)
    pressure = bulk * trace
    stress = [pressure + keep * shape[c] for c in range(3)] + [keep * shape[c] for c in range(3, 6)]
    return stress, shape, (1.5 * two_mu) * factor, gain


def solve_rows(pieces, strain, out, props, green, plane, buffers):
    stx, eps, work, cos_ref, sin_ref = buffers
    ranks, rows, _, thickness, _ = pieces.shape

    def bring(c, carry):
        for h in range(ranks):
            stx[c, h * thickness : (h + 1) * thickness] = jnp.swapaxes(pieces[h, :, c], 0, 1)
        return carry

    lax.fori_loop(0, 7, bring, 0)
    for c in range(6):
        eps[c] = jnp.broadcast_to(strain[:, c : c + 1][None], (VOX_SIDE, rows, VOX_PLANE))

    def sweep(step, carry):
        for h in range(ranks):

            def law(place, inner, h=h):
                x = h * thickness + place
                strain = [eps[c, x] for c in range(6)]
                state = [stx[c, x] for c in range(7)]
                stress = voxel_law(strain, state, props.at[h], pl.ds(place, 1))[0]
                for c in range(6):
                    work[c, x] = stress[c]
                return inner

            lax.fori_loop(0, thickness, law, 0)

        def forward(c, inner):
            field = [work[c, x] for x in range(VOX_SIDE)]
            sums = [field[0]] + [field[x] + field[VOX_SIDE - x] for x in range(1, HALF)] + [field[HALF]]
            diffs = [None] + [field[x] - field[VOX_SIDE - x] for x in range(1, HALF)]
            for k, value in enumerate(cosine_line(sums)):
                cos_ref[c, k] = value
            for k, value in enumerate(sine_line(diffs)):
                if k > 0:
                    sin_ref[c, k - 1] = value
            return inner

        lax.fori_loop(0, 6, forward, 0)

        def transform():
            for ref, first in ((cos_ref, 0), (sin_ref, 2)):
                flat = ref[...].reshape(6 * ref.shape[1] * rows, VOX_PLANE)
                ref[...] = split_dot(flat, plane, first).reshape(ref.shape)

        def apply(field, k):
            row = pl.ds(k, 1)
            field = field[:3] + [2.0 * field[c] for c in range(3, 6)]
            total = [None] * 6
            for n, (i, j) in enumerate(PAIRS):
                entry = green[n, row, :]
                for a, b in [(i, j), (j, i)][: 1 + (i != j)]:
                    term = entry * field[b]
                    total[a] = term if total[a] is None else total[a] + term
            return total

        transform()
        for k in (0, HALF):
            result = apply([cos_ref[c, k] for c in range(6)], k)
            for c in range(6):
                cos_ref[c, k] = result[c]

        def mix(k, inner):
            even = [cos_ref[c, k] for c in range(6)]
            odd = [sin_ref[c, k - 1] for c in range(6)]
            ahead = apply([even[c] + odd[c] for c in range(6)], k)
            behind = apply([even[c] - odd[c] for c in range(6)], VOX_SIDE - k)
            for c in range(6):
                cos_ref[c, k] = ahead[c] + behind[c]
                sin_ref[c, k - 1] = ahead[c] - behind[c]
            return inner

        lax.fori_loop(1, HALF, mix, 0)
        transform()

        def backward(c, inner):
            even = cosine_line([cos_ref[c, k] for k in range(HALF + 1)])
            odd = sine_line([None] + [sin_ref[c, k - 1] for k in range(1, HALF)])
            eps[c, 0] = eps[c, 0] - even[0]
            eps[c, HALF] = eps[c, HALF] - even[HALF]
            for x in range(1, HALF):
                eps[c, x] = eps[c, x] - (even[x] + odd[x])
                eps[c, VOX_SIDE - x] = eps[c, VOX_SIDE - x] - (even[x] - odd[x])
            return inner

        lax.fori_loop(0, 6, backward, 0)
        return carry

    lax.fori_loop(0, SWEEPS, sweep, 0)
    totals = (jnp.zeros((rows, VOX_PLANE), jnp.float32),) * 6
    for h in range(ranks):

        def finish(place, totals, h=h):
            x = h * thickness + place
            strain = [eps[c, x] for c in range(6)]
            state = [stx[c, x] for c in range(7)]
            stress, shape, scale, gain = voxel_law(strain, state, props.at[h], pl.ds(place, 1))
            for c in range(6):
                stx[c, x] = state[c] + scale * shape[c]
            stx[6, x] = state[6] + gain
            return tuple(totals[c] + stress[c] for c in range(6))

        totals = lax.fori_loop(0, thickness, finish, totals)

    def give(c, carry):
        for h in range(ranks):
            out[h, :, c] = jnp.swapaxes(stx[c, h * thickness : (h + 1) * thickness], 0, 1)
        return carry

    lax.fori_loop(0, 7, give, 0)
    lane = lax.broadcasted_iota(jnp.int32, (rows, LANES), 1)
    means = jnp.zeros((rows, LANES), jnp.float32)
    for c in range(6):
        total = jnp.sum(totals[c], axis=1, keepdims=True) / VOX_SIDE**3
        means = jnp.where(lane == c, total, means)
    return means


def drain(ref, sem):
    pltpu.make_async_copy(ref, ref, sem).wait()


def pieces_of(value):
    high = value.astype(jnp.bfloat16)
    rest = value - high.astype(jnp.float32)
    middle = rest.astype(jnp.bfloat16)
    low = (rest - middle.astype(jnp.float32)).astype(jnp.bfloat16)
    return high, middle, low


def select_dot(value, match, lanes):
    contract = (((1,), (1 if lanes else 0,)), ((), ()))
    parts = [
        lax.dot_general(piece, match, contract, preferred_element_type=jnp.float32)
        for piece in pieces_of(value)
    ]
    return parts[0] + (parts[1] + parts[2])


def count_up(shape, axis):
    return lax.broadcasted_iota(jnp.int32, shape, axis)


def to_column(row, size):
    spot = count_up((size, LANES), 0) == count_up((size, LANES), 1)
    return jnp.sum(jnp.where(spot, row, 0.0), axis=1, keepdims=True)


def exchange_kernel(raws, *refs):
    (disp_hbm, load_hbm, conn_hbm, halo_hbm, grad_hbm, volume_hbm, moduli_hbm, owner_hbm) = refs[:8]
    (state_hbm, props_hbm, green_hbm, plane_hbm) = refs[8:12]
    residual, moved_out = refs[12:14]
    (st, raw_send, raw_recv, ex_send, ex_recv, new_src, new_raw, props, green, plane) = refs[14:24]
    buffers = refs[24:29]
    (note_send, note_recv, mean_src, mean_raw, mean_stage, mean_all) = refs[29:35]
    (halo_send, halo_recv, force_send, force_recv, strain_ref, onehot, forces, rows_i) = refs[35:43]
    (disp, load, conn, halo, grad, volume, moduli, owner) = refs[43:51]
    (source_vec, source_ref, order_vec, order_ref, got, load_sem, recv, sent) = refs[51:]
    sources, ranks, rows = ex_recv.shape[:3]
    groups, levels = ranks * rows, sources + raws
    own_nodes, elements, halos = disp.shape[1], conn.shape[1], halo.shape[1]
    me, mine = lax.axis_index("macro"), lax.axis_index("vox")
    my_row, my_side = me // ranks, me % ranks
    raw_side = (mine + ranks * groups - me) % ranks
    R_PROPS, R_NOTE, R_HALO, R_FORCE, R_EX = range(5)
    R_MEAN, R_GOT = R_EX + sources, R_EX + 2 * sources
    R_RAW = R_GOT + levels
    R_MRAW = R_RAW + raws
    f32 = jnp.float32

    def push(src, dst, kind, group, rank):
        pltpu.make_async_remote_copy(
            src_ref=src,
            dst_ref=dst,
            send_sem=sent.at[kind],
            recv_sem=recv.at[kind],
            device_id={"macro": group, "vox": rank},
            device_id_type=pl.DeviceIdType.MESH,
        ).start()

    def deliver(src, dst, kind, group, rank):
        here = (group == me) & (rank == mine)

        @pl.when(here)
        def _():
            pltpu.make_async_copy(src, dst, recv.at[kind]).start()

        @pl.when(jnp.logical_not(here))
        def _():
            push(src, dst, kind, group, rank)

    def settle(ref, kind, fewer):
        count = ref.shape[0]

        @pl.when(fewer)
        def _():
            drain(ref.at[pl.ds(0, count - 1)], sent.at[kind])

        @pl.when(jnp.logical_not(fewer))
        def _():
            drain(ref, sent.at[kind])

    def turn(step, count, block, spot):
        planes = count // block
        line, lane = spot // block, spot % block
        ring = step // block
        line = jnp.where(2 * line < planes, planes - 1 - ring, ring)
        return line * block + (lane + step) % block

    fetches = {}
    for n, (src, dst) in enumerate(
        (
            (owner_hbm, owner),
            (halo_hbm, halo),
            (disp_hbm, disp),
            (state_hbm, st),
            (conn_hbm, conn),
            (grad_hbm, grad),
            (props_hbm, props.at[mine]),
            (green_hbm, green),
            (plane_hbm, plane),
            (volume_hbm, volume),
            (moduli_hbm, moduli),
            (load_hbm, load),
        )
    ):
        fetches[n] = pltpu.make_async_copy(src, dst, load_sem.at[n])
        fetches[n].start()

    barrier = pltpu.get_barrier_semaphore()
    total = groups * ranks
    flat = me * ranks + mine

    def greet(k, carry):
        other = (flat + k) % total
        pl.semaphore_signal(
            barrier,
            inc=1,
            device_id={"macro": other // ranks, "vox": other % ranks},
            device_id_type=pl.DeviceIdType.MESH,
        )
        return carry

    lax.fori_loop(1, total, greet, 0)

    rows_i[...] = jnp.full(rows_i.shape, -1, jnp.int32)
    fetches[0].wait()
    rows_i[0:1, 0:elements] = owner[...]
    owner_row = rows_i[0:1, :].astype(f32)
    square = (LANES, LANES)
    owner_col = to_column(owner_row, LANES)
    before = count_up(square, 0) < count_up(square, 1)
    same = (owner_col == owner_row) & before
    rank_row = jnp.sum(jnp.where(same, 1.0, 0.0), axis=0, keepdims=True)
    slot_row = jnp.where(owner_row >= 0.0, rank_row * groups + owner_row, -1.0)
    slot_col = to_column(slot_row, LANES)
    hit = slot_col == count_up(square, 1).astype(f32)
    spots = jnp.where(hit, count_up(square, 0).astype(f32), 0.0)
    source_vec[...] = jnp.sum(spots, axis=0, keepdims=True).astype(jnp.int32)
    to_scalars = pltpu.make_async_copy(source_vec, source_ref, load_sem.at[12])
    to_scalars.start()

    fetches[1].wait()
    fetches[2].wait()
    rows_i[1:2, own_nodes : own_nodes + halos] = halo[...]
    halo_match = (count_up(square, 0) == rows_i[1:2, :]).astype(jnp.bfloat16)
    halo_send[...] = jnp.zeros(halo_send.shape, f32)
    halo_send[0:3, 0:own_nodes] = disp[...]
    own_disp = halo_send[...]
    halo_send[...] = select_dot(own_disp, halo_match, False)

    to_scalars.wait()
    fetches[3].wait()

    def slab_of(slot):
        return st[:, jnp.clip(source_ref[0, slot], 0, elements - 1)]

    def gather_trade(lv):
        for o in range(ranks):

            def gather(i, carry, o=o):
                slab = slab_of(lv * groups + ranks * i + (mine + o) % ranks)
                if o == 0:
                    ex_recv[lv, mine, i] = slab
                else:
                    ex_send[lv, o - 1, i] = slab
                return carry

            lax.fori_loop(0, rows, gather, 0)

    for lv in range(sources):
        gather_trade(lv)
    for q in range(raws):

        def gather_raw(d, carry, q=q):
            raw_send[q, d] = slab_of((sources + q) * groups + d)
            return carry

        lax.fori_loop(0, groups, gather_raw, 0)
    pl.semaphore_wait(barrier, total - 1)

    row_block = math.gcd(rows, 2)

    def trade(lv):
        for o in range(1, ranks):
            push(ex_send.at[lv, o - 1], ex_recv.at[lv, mine], R_EX + lv, me, (mine + o) % ranks)

    def send_raw(q, o):
        side = (mine + o) % ranks

        def step(t, carry):
            d = ranks * turn(t, rows, row_block, my_row) + (side + ranks * groups - me) % ranks
            deliver(raw_send.at[q, d], raw_recv.at[q, mine, my_row], R_RAW + q, d, side)
            return carry

        lax.fori_loop(0, rows, step, 0)

    push(halo_send, halo_recv, R_HALO, (me + 1) % groups, mine)
    for o in range(1, ranks):
        push(props_hbm, props.at[mine], R_PROPS, me, (mine + o) % ranks)
    trade(0)
    if raws:
        send_raw(0, 0)

    fetches[4].wait()
    fetches[5].wait()
    tall = (LANES, elements)
    for a in range(conn.shape[0]):
        onehot[a] = (count_up(tall, 0) == conn[a : a + 1, :]).astype(jnp.bfloat16)
    drain(halo_recv, recv.at[R_HALO])
    lane8 = count_up((8, LANES), 1)
    near = jnp.where(lane8 < own_nodes, own_disp, halo_recv[...])
    products = [jnp.zeros((8, elements), f32) for _ in range(3)]
    for a in range(conn.shape[0]):
        moved = select_dot(near, onehot[a], False)
        for j in range(3):
            products[j] = products[j] + moved * grad[j, a : a + 1, :]
    strain_ref[...] = jnp.zeros(strain_ref.shape, f32)
    strain_rows = [
        products[0][0:1],
        products[1][1:2],
        products[2][2:3],
        0.5 * (products[2][1:2] + products[1][2:3]),
        0.5 * (products[2][0:1] + products[0][2:3]),
        0.5 * (products[1][0:1] + products[0][1:2]),
    ]
    for c in range(6):
        strain_ref[c : c + 1, 0:elements] = strain_rows[c]
    all_strain = strain_ref[...]

    def matched(ids):
        return ids.astype(f32) == slot_row

    wide = (groups, LANES)
    note = jnp.zeros(wide, f32)
    strain_pieces = pieces_of(all_strain)

    def strain_of(ids):
        match = jnp.where(matched(ids), 1.0, 0.0).astype(jnp.bfloat16)
        parts = [
            lax.dot_general(match, piece, (((1,), (1,)), ((), ())), preferred_element_type=f32)
            for piece in strain_pieces
        ]
        return parts[0] + (parts[1] + parts[2])

    for q in range(raws):
        held = strain_of(count_up(wide, 0) + (sources + q) * groups)
        note = note + (pltpu.roll(held, 16 * q, 1) if q else held)
    for lv in range(levels):
        held = jnp.where(matched(count_up(wide, 0) + lv * groups), 1.0, 0.0)
        note = jnp.where(count_up(wide, 1) == 8 + lv, jnp.sum(held, axis=1, keepdims=True), note)
    for d in range(groups):
        note_send[d] = jnp.broadcast_to(note[d : d + 1, :], (8, LANES))

    def send_note(t, carry):
        d = turn(t, groups, math.gcd(groups, 4), me)
        deliver(note_send.at[d], note_recv.at[my_side * rows + my_row], R_NOTE, d, mine)
        return carry

    lax.fori_loop(0, groups, send_note, 0)
    fetches[6].wait()
    fetches[7].wait()
    fetches[8].wait()
    if ranks > 1:
        drain(props.at[pl.ds(0, ranks - 1)], recv.at[R_PROPS])

    def send_new(lv, low, high, turns):
        def step(t, carry):
            i = turn(t, rows, row_block, my_row)
            for o in turns:
                h = (mine + o) % ranks
                deliver(new_src.at[lv, h, i], got.at[lv * groups + me], R_GOT + lv, ranks * i + mine, h)
            return carry

        lax.fori_loop(low, high, step, 0)

    near, far = range(1), range(1, ranks)
    early = rows // 2 if raws else rows
    for lv in range(sources):
        ids = lv * groups + ranks * count_up((rows, LANES), 0) + mine
        strain = strain_of(ids)
        if ranks > 1:
            drain(ex_recv.at[lv, pl.ds(0, ranks - 1)], recv.at[R_EX + lv])
        if lv == 0:
            for later in range(1, sources):
                trade(later)
            if raws:
                for o in range(1, ranks):
                    send_raw(0, o)
        means = solve_rows(ex_recv.at[lv], strain, new_src.at[lv], props, green, plane, buffers)
        mean_src[lv, mine] = means
        for o in range(1, ranks):
            push(mean_src.at[lv, mine], mean_src.at[lv, mine], R_MEAN + lv, me, (mine + o) % ranks)
        if not raws:
            send_new(lv, 0, rows, range(ranks))

    drain(note_recv, recv.at[R_NOTE])
    flags = note_recv[:, 0, :]
    spot = count_up(wide, 0)
    giver = (ranks * (spot % rows) + spot // rows).astype(f32)
    lane = count_up(wide, 1)
    counts = jnp.sum(jnp.where((lane >= 8) & (lane < 8 + levels), flags, 0.0), axis=1, keepdims=True)
    tall_count = jnp.sum(
        jnp.where(
            (count_up(wide, 0) == lane) & (lane < groups), jnp.broadcast_to(counts, wide), 0.0
        ),
        axis=0,
        keepdims=True,
    )
    lane_giver = (ranks * (lane % rows) + lane // rows).astype(f32)
    earlier = (lane_giver < giver) & (lane < groups)
    place = jnp.sum(jnp.where(earlier, tall_count, 0.0), axis=1, keepdims=True)
    picks = jnp.zeros((1, LANES), f32)
    for lv in range(levels):
        held = jnp.sum(jnp.where(lane == 8 + lv, flags, 0.0), axis=1, keepdims=True)
        chosen = (place == lane.astype(f32)) & (held > 0.5)
        picks = picks + jnp.sum(jnp.where(chosen, lv * groups + giver, 0.0), axis=0, keepdims=True)
        place = place + held
    order_vec[...] = picks.astype(jnp.int32)
    order_scalars = pltpu.make_async_copy(order_vec, order_ref, load_sem.at[12])
    order_scalars.start()

    for q in range(raws):
        drain(raw_recv.at[q], recv.at[R_RAW + q])
        if q + 1 < raws:
            for o in range(ranks):
                send_raw(q + 1, o)
        else:
            for lv in range(sources):
                send_new(lv, 0, rows, far)
                send_new(lv, 0, early, near)
        strain = pltpu.roll(note_recv[pl.ds(raw_side * rows, rows), 0, :], LANES - 16 * q, 1)
        means = solve_rows(raw_recv.at[q], strain, new_raw.at[q], props, green, plane, buffers)
        for i in range(rows):
            mean_stage[q, i] = jnp.broadcast_to(means[i : i + 1, :], (8, LANES))

        def send_back(t, carry, q=q):
            i = turn(t, rows, row_block, my_row)
            for h in range(ranks):
                deliver(mean_stage.at[q, i], mean_raw.at[q, me], R_MRAW + q, ranks * i + raw_side, h)
            return carry

        lax.fori_loop(0, rows, send_back, 0)

        def send_done(i, carry, q=q):
            for o in range(ranks):
                h = (mine + o) % ranks
                spot = (sources + q) * groups + ranks * i + raw_side
                deliver(new_raw.at[q, h, i], got.at[spot], R_GOT + sources + q, me, h)
            return carry

        lax.fori_loop(0, rows, send_done, 0)
    for lv in range(sources):
        send_new(lv, early, rows, near)

    fetches[9].wait()
    fetches[10].wait()
    fetches[11].wait()
    for lv in range(sources):
        if ranks > 1:
            drain(mean_src.at[lv, pl.ds(0, ranks - 1)], recv.at[R_MEAN + lv])
        for y in range(ranks):
            mean_all[lv * groups + y * rows : lv * groups + (y + 1) * rows, :] = mean_src[lv, y]
    for q in range(raws):
        drain(mean_raw.at[q], recv.at[R_MRAW + q])
        low = (sources + q) * groups
        mean_all[low : low + groups, :] = mean_raw[q, :, 0, :]
    deep = (levels * groups, LANES)
    k = count_up(deep, 0)
    inside = k % groups
    known = k - inside + jnp.where(
        k < sources * groups, ranks * (inside % rows) + inside // rows, inside
    )
    match = jnp.where(matched(known), 1.0, 0.0).astype(jnp.bfloat16)
    mean_t = jnp.transpose(mean_all[...])[0:8, :]
    averaged = select_dot(mean_t, match, False)[:, 0:elements]
    strain = all_strain[0:8, 0:elements]
    lame, shear = moduli[0:1, :], moduli[1:2, :]
    lateral = lame * (strain[0:1] + strain[1:2] + strain[2:3])
    plastic = owner[...] >= 0
    stress = []
    for c in range(6):
        plain = 2.0 * shear * strain[c : c + 1]
        plain = lateral + plain if c < 3 else plain
        stress.append(jnp.where(plastic, averaged[c : c + 1], plain))
    tensor = [[stress[0], stress[5], stress[4]], [stress[5], stress[1], stress[3]], [stress[4], stress[3], stress[2]]]
    forces[...] = jnp.zeros(forces.shape, f32)
    for i in range(3):
        force = volume[...] * (
            tensor[i][0] * grad[0] + tensor[i][1] * grad[1] + tensor[i][2] * grad[2]
        )
        for a in range(conn.shape[0]):
            forces[a, i : i + 1, :] = force[a : a + 1, :]
    assembled = jnp.zeros((8, LANES), f32)
    for a in range(conn.shape[0]):
        assembled = assembled + select_dot(forces[a], onehot[a], True)
    force_send[...] = assembled
    push(force_send, force_recv, R_FORCE, (me + groups - 1) % groups, mine)
    drain(force_recv, recv.at[R_FORCE])
    lane8 = count_up((8, LANES), 1)
    beyond = (lane8 >= own_nodes) & (lane8 < own_nodes + halos)
    back = jnp.where(beyond, force_recv[...], 0.0)
    total_force = assembled + select_dot(back, halo_match, True)
    residual[...] = total_force[0:3, 0:own_nodes] - load[...]

    for lv in range(levels):
        drain(got.at[pl.ds(lv * groups, groups)], recv.at[R_GOT + lv])
    order_scalars.wait()

    def place_row(j, carry):
        moved_out[:, j] = got[jnp.clip(order_ref[0, j], 0, levels * groups - 1)]
        return carry

    lax.fori_loop(0, moved_out.shape[1], place_row, 0)
    drain(note_send.at[pl.ds(0, groups - 1)], sent.at[R_NOTE])
    drain(halo_send, sent.at[R_HALO])
    drain(force_send, sent.at[R_FORCE])
    if ranks > 1:
        drain(props.at[pl.ds(0, ranks - 1)], sent.at[R_PROPS])
    for lv in range(sources):
        if ranks > 1:
            drain(ex_send.at[lv], sent.at[R_EX + lv])
            drain(mean_src.at[lv, pl.ds(0, ranks - 1)], sent.at[R_MEAN + lv])
        settle(got.at[pl.ds(0, groups)], R_GOT + lv, my_side == mine)
    own = (2 * me) % ranks == mine
    for q in range(raws):
        settle(raw_send.at[q], R_RAW + q, own)
        settle(mean_raw.at[q], R_MRAW + q, own)
        if ranks > 1:
            drain(got.at[pl.ds(0, groups - rows)], sent.at[R_GOT + sources + q])


def exchange(smalls, state, moduli, tables, levels, raws):
    groups, ranks = lax.axis_size("macro"), lax.axis_size("vox")
    rows = groups // ranks
    thickness = state.shape[2]
    sources = levels - raws
    nodes, corners, elements = smalls[0].shape[1], smalls[2].shape[0], smalls[2].shape[1]
    slab = (7, thickness, VOX_PLANE)
    hbm = pl.BlockSpec(memory_space=pltpu.HBM)
    vmem = pl.BlockSpec(memory_space=pltpu.VMEM)
    f32 = jnp.float32
    kinds = 5 + 2 * sources + levels + 2 * raws
    cells = levels * VOX_SIDE * rows * VOX_PLANE
    tile = pltpu.VMEM((8, LANES), f32)
    return pl.pallas_call(
        functools.partial(exchange_kernel, raws),
        out_shape=[
            jax.ShapeDtypeStruct((3, nodes), f32),
            jax.ShapeDtypeStruct((7, RECV_AGG) + slab[1:], f32),
        ],
        in_specs=[hbm] * (len(smalls) + 2 + len(tables)),
        out_specs=[vmem, vmem],
        scratch_shapes=[
            pltpu.VMEM(state.shape, f32),
            pltpu.VMEM((max(raws, 1), groups) + slab, f32),
            pltpu.VMEM((max(raws, 1), ranks, rows) + slab, f32),
            pltpu.VMEM((sources, max(ranks - 1, 1), rows) + slab, f32),
            pltpu.VMEM((sources, ranks, rows) + slab, f32),
            pltpu.VMEM((sources, ranks, rows) + slab, f32),
            pltpu.VMEM((max(raws, 1), ranks, rows) + slab, f32),
            pltpu.VMEM((ranks,) + moduli.shape, f32),
            pltpu.VMEM(tables[0].shape, f32),
            pltpu.VMEM(tables[1].shape, tables[1].dtype),
            pltpu.VMEM((7, VOX_SIDE, rows, VOX_PLANE), f32),
            pltpu.VMEM((6, VOX_SIDE, rows, VOX_PLANE), f32),
            pltpu.VMEM((6, VOX_SIDE, rows, VOX_PLANE), f32),
            pltpu.VMEM((6, HALF + 1, rows, VOX_PLANE), f32),
            pltpu.VMEM((6, HALF - 1, rows, VOX_PLANE), f32),
            pltpu.VMEM((groups, 8, LANES), f32),
            pltpu.VMEM((groups, 8, LANES), f32),
            pltpu.VMEM((sources, ranks, rows, LANES), f32),
            pltpu.VMEM((max(raws, 1), groups, 8, LANES), f32),
            pltpu.VMEM((max(raws, 1), rows, 8, LANES), f32),
            pltpu.VMEM((levels * groups, LANES), f32),
            tile,
            tile,
            tile,
            tile,
            pltpu.VMEM((LANES, LANES), f32),
            pltpu.VMEM((corners, LANES, elements), jnp.bfloat16),
            pltpu.VMEM((corners, 8, elements), f32),
            pltpu.VMEM((8, LANES), jnp.int32),
        ]
        + [pltpu.VMEM(small.shape, small.dtype) for small in smalls]
        + [
            pltpu.VMEM((1, LANES), jnp.int32),
            pltpu.SMEM((1, LANES), jnp.int32),
            pltpu.VMEM((1, LANES), jnp.int32),
            pltpu.SMEM((1, LANES), jnp.int32),
            pltpu.VMEM((levels * groups,) + slab, f32),
            pltpu.SemaphoreType.DMA((13,)),
            pltpu.SemaphoreType.DMA((kinds,)),
            pltpu.SemaphoreType.DMA((kinds,)),
        ],
        compiler_params=pltpu.CompilerParams(
            collective_id=0, has_side_effects=True, vmem_limit_bytes=63 * 2**20
        ),
        cost_estimate=pl.CostEstimate(
            flops=SWEEPS * 2 * 3 * 2 * 6 * cells * VOX_PLANE,
            bytes_accessed=4 * 7 * cells * 4,
            transcendentals=SWEEPS * cells,
        ),
    )(*smalls, state, moduli, *tables)


def local(
    displacement,
    load,
    conn,
    halo_list,
    grad_ops,
    volume,
    elastic_moduli,
    plastic_mask,
    new_owner,
    state,
    micro_moduli,
):
    groups = lax.axis_size("macro")
    tables = (jnp.asarray(green_tables()), plane_tables())
    levels = (PLASTIC_MAX + groups - 1) // groups
    raws = levels - 1
    smalls = (
        displacement,
        load,
        conn,
        halo_list[None, :],
        grad_ops,
        volume[None, :],
        elastic_moduli,
        new_owner[None, :],
    )
    return tuple(exchange(smalls, state, micro_moduli, tables, levels, raws))


def solution(mesh):
    return jax.shard_map(
        local,
        mesh=mesh,
        in_specs=(
            P(None, "macro"),
            P(None, "macro"),
            P(None, "macro"),
            P("macro"),
            P(None, None, "macro"),
            P("macro"),
            P(None, "macro"),
            P("macro"),
            P("macro"),
            P(None, "macro", "vox", None),
            P(None, "vox", None),
        ),
        out_specs=(P(None, "macro"), P(None, "macro", "vox", None)),
        check_vma=False,
    )
```

```python
import functools
import math

import jax
import jax.numpy as jnp
import numpy as np
from jax import lax
from jax.experimental import pallas as pl
from jax.experimental.pallas import tpu as pltpu
from jax.sharding import PartitionSpec as P

RECV_AGG = 24
PLASTIC_MAX = 48
VOX_SIDE = 16
VOX_PLANE = 256
SWEEPS = 4
HALF = VOX_SIDE // 2
LANES = 128

LAM_REF = 3.0
MU_REF = 3.0

ROOT = math.sqrt(0.5)
COS1 = math.cos(math.pi / 8)
COS3 = math.cos(3 * math.pi / 8)
PAIRS = [(i, j) for i in range(6) for j in range(i, 6)]


def green_tables():
    line = np.arange(VOX_SIDE)
    signed = np.where(line < HALF, line, line - VOX_SIDE).astype(np.float64)
    freq = np.stack(np.meshgrid(signed, signed, signed, indexing="ij"))
    norm = np.sum(freq * freq, axis=0)
    inverse = np.where(norm > 0, 1.0 / np.maximum(norm, 1.0), 0.0)
    coupling = (LAM_REF + MU_REF) / (LAM_REF + 2.0 * MU_REF)
    spots = [(0, 0), (1, 1), (2, 2), (1, 2), (0, 2), (0, 1)]
    table = np.zeros((6, 6) + norm.shape)
    for j, (a, b) in enumerate(spots):
        tau = np.zeros((3, 3))
        tau[a, b] = tau[b, a] = 1.0
        trac = np.einsum("ij,jxyz->ixyz", tau, freq)
        along = np.sum(freq * trac, axis=0) * inverse
        wave = (trac - coupling * along * freq) * inverse / MU_REF
        for i, (c, d) in enumerate(spots):
            table[i, j] = 0.5 * (freq[c] * wave[d] + freq[d] * wave[c])
    back = -line % VOX_SIDE
    flipped = table[:, :, back][:, :, :, back][:, :, :, :, back]
    even = 0.5 * (table + flipped) / VOX_SIDE**3
    even[:, 3:] *= 0.5
    stacked = np.stack([even[i, j] for i, j in PAIRS])
    return stacked.reshape(len(PAIRS), VOX_SIDE, VOX_PLANE).astype(np.float32)


def plane_tables():
    plane = np.arange(VOX_PLANE)
    rows, cols = plane // VOX_SIDE, plane % VOX_SIDE
    phase = (rows[:, None] * rows[None, :] + cols[:, None] * cols[None, :]) % VOX_SIDE
    angle = phase * (2.0 * math.pi / VOX_SIDE)
    plus = jnp.asarray((np.cos(angle) + np.sin(angle)).astype(np.float32))
    minus = jnp.asarray((np.cos(angle) - np.sin(angle)).astype(np.float32))
    out = []
    for table in (plus, minus):
        high = table.astype(jnp.bfloat16)
        out += [high, (table - high.astype(jnp.float32)).astype(jnp.bfloat16)]
    return jnp.stack(out)


def cosine_line(a):
    sums = [None] + [a[x] + a[8 - x] for x in (1, 2, 3)]
    diffs = [None] + [a[x] - a[8 - x] for x in (1, 2, 3)]
    even0, odd0 = a[0] + a[8], a[0] - a[8]
    outer, inner = even0 + a[4], even0 - a[4]
    spread = sums[1] + sums[3]
    slant = ROOT * (sums[1] - sums[3])
    mid = ROOT * diffs[2]
    first = COS1 * diffs[1] + COS3 * diffs[3]
    second = COS3 * diffs[1] - COS1 * diffs[3]
    top, low = odd0 + mid, odd0 - mid
    core = outer + sums[2]
    return [
        core + spread,
        top + first,
        inner + slant,
        low + second,
        outer - sums[2],
        low - second,
        inner - slant,
        top - first,
        core - spread,
    ]


def sine_line(b):
    sums = [None] + [b[x] + b[8 - x] for x in (1, 2, 3)]
    diffs = [None] + [b[x] - b[8 - x] for x in (1, 2, 3)]
    slant = ROOT * (diffs[1] + diffs[3])
    mid = ROOT * sums[2]
    first = COS3 * sums[1] + COS1 * sums[3]
    second = COS1 * sums[1] - COS3 * sums[3]
    return [
        None,
        (first + mid) + b[4],
        slant + diffs[2],
        (second + mid) - b[4],
        diffs[1] - diffs[3],
        (second - mid) + b[4],
        slant - diffs[2],
        (first - mid) - b[4],
    ]


def split_dot(block, table_ref, first):
    high = block.astype(jnp.bfloat16)
    low = (block - high.astype(jnp.float32)).astype(jnp.bfloat16)
    dot = functools.partial(jnp.dot, preferred_element_type=jnp.float32)
    return dot(high, table_ref[first]) + (dot(high, table_ref[first + 1]) + dot(low, table_ref[first]))


def voxel_law(strain, state, props, row):
    lam, mu = props[0, row, :], props[1, row, :]
    yield_base, harden = props[2, row, :], props[3, row, :]
    two_mu, three_mu = 2.0 * mu, 3.0 * mu
    stiff_inv = 1.0 / (three_mu + harden)
    bulk = lam + two_mu * (1.0 / 3.0)
    elastic = [strain[c] - state[c] for c in range(6)]
    trace = elastic[0] + elastic[1] + elastic[2]
    third = trace * (1.0 / 3.0)
    shape = [elastic[c] - third for c in range(3)] + elastic[3:]
    normal = shape[0] * shape[0] + shape[1] * shape[1] + shape[2] * shape[2]
    shear = shape[3] * shape[3] + shape[4] * shape[4] + shape[5] * shape[5]
    equivalent = two_mu * jnp.sqrt(1.5 * (normal + 2.0 * shear))
    strength = yield_base + harden * state[6]
    gain = jnp.maximum(equivalent - strength, 0.0) * stiff_inv
    factor = gain / jnp.maximum(equivalent, strength)
    keep = two_mu * (1.0 - three_mu * factor)
    pressure = bulk * trace
    stress = [pressure + keep * shape[c] for c in range(3)] + [keep * shape[c] for c in range(3, 6)]
    return stress, shape, (1.5 * two_mu) * factor, gain


def solve_rows(pieces, strain, base, out, props, green, plane, buffers):
    stx, eps, work, cos_ref, sin_ref = buffers
    ranks, rows, _, thickness, _ = pieces.shape

    def bring(c, carry):
        for h in range(ranks):
            stx[c, h * thickness : (h + 1) * thickness] = jnp.swapaxes(pieces[h, :, c], 0, 1)
        return carry

    lax.fori_loop(0, 7, bring, 0)
    for c in range(6):
        eps[c] = jnp.broadcast_to(strain[:, base + c : base + c + 1][None], (VOX_SIDE, rows, VOX_PLANE))

    def sweep(step, carry):
        for h in range(ranks):

            def law(place, inner, h=h):
                x = h * thickness + place
                strain = [eps[c, x] for c in range(6)]
                state = [stx[c, x] for c in range(7)]
                stress = voxel_law(strain, state, props.at[h], pl.ds(place, 1))[0]
                for c in range(6):
                    work[c, x] = stress[c]
                return inner

            lax.fori_loop(0, thickness, law, 0)

        def forward(c, inner):
            field = [work[c, x] for x in range(VOX_SIDE)]
            sums = [field[0]] + [field[x] + field[VOX_SIDE - x] for x in range(1, HALF)] + [field[HALF]]
            diffs = [None] + [field[x] - field[VOX_SIDE - x] for x in range(1, HALF)]
            for k, value in enumerate(cosine_line(sums)):
                cos_ref[c, k] = value
            for k, value in enumerate(sine_line(diffs)):
                if k > 0:
                    sin_ref[c, k - 1] = value
            return inner

        lax.fori_loop(0, 6, forward, 0)

        def transform():
            for ref, first in ((cos_ref, 0), (sin_ref, 2)):
                flat = ref[...].reshape(6 * ref.shape[1] * rows, VOX_PLANE)
                ref[...] = split_dot(flat, plane, first).reshape(ref.shape)

        def apply(field, k):
            row = pl.ds(k, 1)
            field = field[:3] + [2.0 * field[c] for c in range(3, 6)]
            total = [None] * 6
            for n, (i, j) in enumerate(PAIRS):
                entry = green[n, row, :]
                for a, b in [(i, j), (j, i)][: 1 + (i != j)]:
                    term = entry * field[b]
                    total[a] = term if total[a] is None else total[a] + term
            return total

        transform()
        for k in (0, HALF):
            result = apply([cos_ref[c, k] for c in range(6)], k)
            for c in range(6):
                cos_ref[c, k] = result[c]

        def mix(k, inner):
            even = [cos_ref[c, k] for c in range(6)]
            odd = [sin_ref[c, k - 1] for c in range(6)]
            ahead = apply([even[c] + odd[c] for c in range(6)], k)
            behind = apply([even[c] - odd[c] for c in range(6)], VOX_SIDE - k)
            for c in range(6):
                cos_ref[c, k] = ahead[c] + behind[c]
                sin_ref[c, k - 1] = ahead[c] - behind[c]
            return inner

        lax.fori_loop(1, HALF, mix, 0)
        transform()

        def backward(c, inner):
            even = cosine_line([cos_ref[c, k] for k in range(HALF + 1)])
            odd = sine_line([None] + [sin_ref[c, k - 1] for k in range(1, HALF)])
            eps[c, 0] = eps[c, 0] - even[0]
            eps[c, HALF] = eps[c, HALF] - even[HALF]
            for x in range(1, HALF):
                eps[c, x] = eps[c, x] - (even[x] + odd[x])
                eps[c, VOX_SIDE - x] = eps[c, VOX_SIDE - x] - (even[x] - odd[x])
            return inner

        lax.fori_loop(0, 6, backward, 0)
        return carry

    lax.fori_loop(0, SWEEPS, sweep, 0)
    totals = (jnp.zeros((rows, VOX_PLANE), jnp.float32),) * 6
    for h in range(ranks):

        def finish(place, totals, h=h):
            x = h * thickness + place
            strain = [eps[c, x] for c in range(6)]
            state = [stx[c, x] for c in range(7)]
            stress, shape, scale, gain = voxel_law(strain, state, props.at[h], pl.ds(place, 1))
            for c in range(6):
                stx[c, x] = state[c] + scale * shape[c]
            stx[6, x] = state[6] + gain
            return tuple(totals[c] + stress[c] for c in range(6))

        totals = lax.fori_loop(0, thickness, finish, totals)

    def give(c, carry):
        for h in range(ranks):
            out[h, :, c] = jnp.swapaxes(stx[c, h * thickness : (h + 1) * thickness], 0, 1)
        return carry

    lax.fori_loop(0, 7, give, 0)
    lane = lax.broadcasted_iota(jnp.int32, (rows, LANES), 1)
    means = jnp.zeros((rows, LANES), jnp.float32)
    for c in range(6):
        total = jnp.sum(totals[c], axis=1, keepdims=True) / VOX_SIDE**3
        means = jnp.where(lane == c, total, means)
    return means


def drain(ref, sem):
    pltpu.make_async_copy(ref, ref, sem).wait()


def pieces_of(value):
    high = value.astype(jnp.bfloat16)
    rest = value - high.astype(jnp.float32)
    middle = rest.astype(jnp.bfloat16)
    low = (rest - middle.astype(jnp.float32)).astype(jnp.bfloat16)
    return high, middle, low


def select_dot(value, match, lanes):
    contract = (((1,), (1 if lanes else 0,)), ((), ()))
    parts = [
        lax.dot_general(piece, match, contract, preferred_element_type=jnp.float32)
        for piece in pieces_of(value)
    ]
    return parts[0] + (parts[1] + parts[2])


def count_up(shape, axis):
    return lax.broadcasted_iota(jnp.int32, shape, axis)


def to_column(row, size):
    spot = count_up((size, LANES), 0) == count_up((size, LANES), 1)
    return jnp.sum(jnp.where(spot, row, 0.0), axis=1, keepdims=True)


def exchange_kernel(levels, *refs):
    (disp_hbm, load_hbm, conn_hbm, halo_hbm, grad_hbm, volume_hbm, moduli_hbm, owner_hbm) = refs[:8]
    (state_hbm, props_hbm, green_hbm, plane_hbm) = refs[8:12]
    residual, moved_out = refs[12:14]
    (st, trade_send, trade_recv, trade_new, raw_send, raw_recv, raw_new) = refs[14:21]
    (mix_trade, mix_send, mix_recv, mix_new, got, props, green, plane) = refs[21:29]
    buffers = refs[29:34]
    (note_send, note_recv, mean_src, mean_raw, mean_mix, mean_far, stage, mean_all) = refs[34:42]
    (halo_send, halo_recv, force_send, force_recv, mixed, strain_ref, onehot, forces, rows_i) = refs[42:51]
    (disp, load, conn, halo, grad, volume, moduli, owner) = refs[51:59]
    (source_vec, source_ref, order_vec, order_ref, load_sem, recv, sent) = refs[59:]
    ranks, rows = trade_recv.shape[:2]
    groups, half = ranks * rows, rows // 2
    own_nodes, elements, halos = disp.shape[1], conn.shape[1], halo.shape[1]
    me, mine = lax.axis_index("macro"), lax.axis_index("vox")
    my_row, my_side = me // ranks, me % ranks
    raw_side = (mine + ranks * groups - me) % ranks
    my_odd, my_pair = my_row % 2, my_row // 2
    R_PROPS, R_NOTE, R_HALO, R_FORCE, R_TRADE, R_MEAN, R_RAW, R_MRAW, R_MIXT, R_MIX, R_MMIX, R_MFAR, R_GOT = range(13)
    f32 = jnp.float32

    def push(src, dst, kind, group, rank):
        pltpu.make_async_remote_copy(
            src_ref=src,
            dst_ref=dst,
            send_sem=sent.at[kind],
            recv_sem=recv.at[kind],
            device_id={"macro": group, "vox": rank},
            device_id_type=pl.DeviceIdType.MESH,
        ).start()

    def deliver(src, dst, kind, group, rank):
        here = (group == me) & (rank == mine)

        @pl.when(here)
        def _():
            pltpu.make_async_copy(src, dst, recv.at[kind]).start()

        @pl.when(jnp.logical_not(here))
        def _():
            push(src, dst, kind, group, rank)

    def settle(ref, kind, fewer):
        count = ref.shape[0]

        @pl.when(fewer)
        def _():
            drain(ref.at[pl.ds(0, count - 1)], sent.at[kind])

        @pl.when(jnp.logical_not(fewer))
        def _():
            drain(ref, sent.at[kind])

    def turn(step, count, block, spot):
        planes = count // block
        line, lane = spot // block, spot % block
        ring = step // block
        line = jnp.where(2 * line < planes, planes - 1 - ring, ring)
        return line * block + (lane + step) % block

    fetches = {}
    for n, (src, dst) in enumerate(
        (
            (owner_hbm, owner),
            (halo_hbm, halo),
            (disp_hbm, disp),
            (state_hbm, st),
            (conn_hbm, conn),
            (grad_hbm, grad),
            (props_hbm, props.at[mine]),
            (green_hbm, green),
            (plane_hbm, plane),
            (volume_hbm, volume),
            (moduli_hbm, moduli),
            (load_hbm, load),
        )
    ):
        fetches[n] = pltpu.make_async_copy(src, dst, load_sem.at[n])
        fetches[n].start()

    barrier = pltpu.get_barrier_semaphore()
    total = groups * ranks
    flat = me * ranks + mine

    def greet(k, carry):
        other = (flat + k) % total
        pl.semaphore_signal(
            barrier,
            inc=1,
            device_id={"macro": other // ranks, "vox": other % ranks},
            device_id_type=pl.DeviceIdType.MESH,
        )
        return carry

    lax.fori_loop(1, total, greet, 0)

    rows_i[...] = jnp.full(rows_i.shape, -1, jnp.int32)
    fetches[0].wait()
    rows_i[0:1, 0:elements] = owner[...]
    owner_row = rows_i[0:1, :].astype(f32)
    square = (LANES, LANES)
    owner_col = to_column(owner_row, LANES)
    before = count_up(square, 0) < count_up(square, 1)
    same = (owner_col == owner_row) & before
    rank_row = jnp.sum(jnp.where(same, 1.0, 0.0), axis=0, keepdims=True)
    slot_row = jnp.where(owner_row >= 0.0, rank_row * groups + owner_row, -1.0)
    slot_col = to_column(slot_row, LANES)
    hit = slot_col == count_up(square, 1).astype(f32)
    spots = jnp.where(hit, count_up(square, 0).astype(f32), 0.0)
    source_vec[...] = jnp.sum(spots, axis=0, keepdims=True).astype(jnp.int32)
    to_scalars = pltpu.make_async_copy(source_vec, source_ref, load_sem.at[12])
    to_scalars.start()

    fetches[1].wait()
    fetches[2].wait()
    rows_i[1:2, own_nodes : own_nodes + halos] = halo[...]
    halo_match = (count_up(square, 0) == rows_i[1:2, :]).astype(jnp.bfloat16)
    halo_send[...] = jnp.zeros(halo_send.shape, f32)
    halo_send[0:3, 0:own_nodes] = disp[...]
    own_disp = halo_send[...]
    halo_send[...] = select_dot(own_disp, halo_match, False)

    to_scalars.wait()
    fetches[3].wait()

    def slab_of(slot):
        return st[:, jnp.clip(source_ref[0, slot], 0, elements - 1)]

    def expect(count, sem):
        drain(got.at[pl.ds(0, count)], sem)

    def gather_trade(low, stride, start, here, away):
        for o in range(ranks):

            def gather(i, carry, o=o):
                slab = slab_of(low + ranks * (stride * i + start) + (mine + o) % ranks)
                if o == 0:
                    here[mine, i] = slab
                else:
                    away[o - 1, i] = slab
                return carry

            lax.fori_loop(0, away.shape[1], gather, 0)

    gather_trade(0, 1, 0, trade_recv, trade_send)
    if levels > 1:

        def gather_raw(d, carry):
            raw_send[d] = slab_of(groups + d)
            return carry

        lax.fori_loop(0, groups, gather_raw, 0)
    if levels > 2:
        gather_trade(2 * groups, 2, 1 - my_odd, mix_recv, mix_trade)

        def gather_mix(v, carry):
            mix_send[v] = slab_of(2 * groups + ranks * (2 * (v // ranks) + my_odd) + v % ranks)
            return carry

        lax.fori_loop(0, groups // 2, gather_mix, 0)
    pl.semaphore_wait(barrier, total - 1)

    row_block = math.gcd(rows, 2)

    def side_of(o):
        side = (mine + o) % ranks
        return side, (side + ranks * groups - me) % ranks

    def send_raw(o):
        side, spot = side_of(o)

        def step(t, carry):
            d = ranks * turn(t, rows, row_block, my_row) + spot
            deliver(raw_send.at[d], raw_recv.at[mine, my_row], R_RAW, d, side)
            return carry

        lax.fori_loop(0, rows, step, 0)

    def send_mix(o):
        side, spot = side_of(o)

        def step(t, carry):
            u = turn(t, half, 1, my_pair)
            d = ranks * (2 * u + my_odd) + spot
            deliver(mix_send.at[u * ranks + spot], mix_recv.at[mine, half + my_pair], R_MIX, d, side)
            return carry

        lax.fori_loop(0, half, step, 0)

    push(halo_send, halo_recv, R_HALO, (me + 1) % groups, mine)
    for o in range(1, ranks):
        push(props_hbm, props.at[mine], R_PROPS, me, (mine + o) % ranks)
    for o in range(1, ranks):
        push(trade_send.at[o - 1], trade_recv.at[mine], R_TRADE, me, (mine + o) % ranks)
    if levels > 1:
        send_raw(0)

    fetches[4].wait()
    fetches[5].wait()
    tall = (LANES, elements)
    for a in range(conn.shape[0]):
        onehot[a] = (count_up(tall, 0) == conn[a : a + 1, :]).astype(jnp.bfloat16)
    drain(halo_recv, recv.at[R_HALO])
    lane8 = count_up((8, LANES), 1)
    near = jnp.where(lane8 < own_nodes, own_disp, halo_recv[...])
    products = [jnp.zeros((8, elements), f32) for _ in range(3)]
    for a in range(conn.shape[0]):
        moved = select_dot(near, onehot[a], False)
        for j in range(3):
            products[j] = products[j] + moved * grad[j, a : a + 1, :]
    strain_ref[...] = jnp.zeros(strain_ref.shape, f32)
    strain_rows = [
        products[0][0:1],
        products[1][1:2],
        products[2][2:3],
        0.5 * (products[2][1:2] + products[1][2:3]),
        0.5 * (products[2][0:1] + products[0][2:3]),
        0.5 * (products[1][0:1] + products[0][1:2]),
    ]
    for c in range(6):
        strain_ref[c : c + 1, 0:elements] = strain_rows[c]
    all_strain = strain_ref[...]

    def matched(ids):
        return ids.astype(f32) == slot_row

    wide = (groups, LANES)
    note = jnp.zeros(wide, f32)
    strain_pieces = pieces_of(all_strain)

    def strain_of(ids):
        match = jnp.where(matched(ids), 1.0, 0.0).astype(jnp.bfloat16)
        parts = [
            lax.dot_general(match, piece, (((1,), (1,)), ((), ())), preferred_element_type=f32)
            for piece in strain_pieces
        ]
        return parts[0] + (parts[1] + parts[2])

    for lv in range(1, levels):
        held = strain_of(count_up(wide, 0) + lv * groups)
        note = note + pltpu.roll(held, 16 * lv, 1)
    for lv in range(levels):
        held = jnp.where(matched(count_up(wide, 0) + lv * groups), 1.0, 0.0)
        note = jnp.where(count_up(wide, 1) == 8 + lv, jnp.sum(held, axis=1, keepdims=True), note)
    for d in range(groups):
        note_send[d] = jnp.broadcast_to(note[d : d + 1, :], (8, LANES))

    def send_note(t, carry):
        d = turn(t, groups, math.gcd(groups, 4), me)
        deliver(note_send.at[d], note_recv.at[my_side * rows + my_row], R_NOTE, d, mine)
        return carry

    lax.fori_loop(0, groups, send_note, 0)
    fetches[6].wait()
    fetches[7].wait()
    fetches[8].wait()
    if ranks > 1:
        drain(props.at[pl.ds(0, ranks - 1)], recv.at[R_PROPS])

    def send_new(low, high, turns):
        def step(t, carry):
            i = turn(t, rows, row_block, my_row)
            for o in turns:
                h = (mine + o) % ranks
                deliver(trade_new.at[h, i], got.at[me], R_GOT, ranks * i + mine, h)
            return carry

        lax.fori_loop(low, high, step, 0)

    def send_mixed(turns):
        def step(t, carry):
            u = turn(t, half, 1, my_pair)
            for o in turns:
                h = (mine + o) % ranks
                spot = ranks * (2 * u + 1 - my_odd) + mine
                push(mix_new.at[h, u], got.at[2 * groups + me], R_GOT + 2, spot, h)
            return carry

        lax.fori_loop(0, half, step, 0)

    def give_back(new, first, count, low, kind, stride, start):
        def step(i, carry):
            for o in range(ranks):
                h = (mine + o) % ranks
                giver = ranks * (stride * i + start) + raw_side
                deliver(new.at[h, first + i], got.at[low + giver], kind, me, h)
            return carry

        lax.fori_loop(0, count, step, 0)

    def send_means(means, first, count, dst, kind, stride, start):
        for i in range(count):
            stage[first + i if count < rows else rows + i] = jnp.broadcast_to(
                means[first + i : first + i + 1, :], (8, LANES)
            )

        def step(t, carry):
            i = turn(t, count, math.gcd(count, 2), my_row * count // rows)
            for h in range(ranks):
                src = stage.at[first + i if count < rows else rows + i]
                deliver(src, dst, kind, ranks * (stride * i + start) + raw_side, h)
            return carry

        lax.fori_loop(0, count, step, 0)

    near, far = range(1), range(1, ranks)
    early = rows // 2 if levels > 1 else rows
    strain = strain_of(ranks * count_up((rows, LANES), 0) + mine)
    if ranks > 1:
        expect((ranks - 1) * rows, recv.at[R_TRADE])
    if levels > 1:
        for o in far:
            send_raw(o)
    means = solve_rows(trade_recv, strain, 0, trade_new, props, green, plane, buffers)
    mean_src[mine] = means
    for o in far:
        push(mean_src.at[mine], mean_src.at[mine], R_MEAN, me, (mine + o) % ranks)
    if levels == 1:
        send_new(0, rows, range(ranks))

    drain(note_recv, recv.at[R_NOTE])
    flags = note_recv[:, 0, :]
    spot = count_up(wide, 0)
    giver = (ranks * (spot % rows) + spot // rows).astype(f32)
    lane = count_up(wide, 1)
    counts = jnp.sum(jnp.where((lane >= 8) & (lane < 8 + levels), flags, 0.0), axis=1, keepdims=True)
    tall_count = jnp.sum(
        jnp.where(
            (count_up(wide, 0) == lane) & (lane < groups), jnp.broadcast_to(counts, wide), 0.0
        ),
        axis=0,
        keepdims=True,
    )
    lane_giver = (ranks * (lane % rows) + lane // rows).astype(f32)
    earlier = (lane_giver < giver) & (lane < groups)
    place = jnp.sum(jnp.where(earlier, tall_count, 0.0), axis=1, keepdims=True)
    picks = jnp.zeros((1, LANES), f32)
    for lv in range(levels):
        held = jnp.sum(jnp.where(lane == 8 + lv, flags, 0.0), axis=1, keepdims=True)
        chosen = (place == lane.astype(f32)) & (held > 0.5)
        picks = picks + jnp.sum(jnp.where(chosen, lv * groups + giver, 0.0), axis=0, keepdims=True)
        place = place + held
    order_vec[...] = picks.astype(jnp.int32)
    order_scalars = pltpu.make_async_copy(order_vec, order_ref, load_sem.at[12])
    order_scalars.start()

    if levels > 1:
        expect(groups, recv.at[R_RAW])
        if levels > 2:
            for o in far:
                push(mix_trade.at[o - 1], mix_recv.at[mine, pl.ds(0, half)], R_MIXT, me, (mine + o) % ranks)
                send_mix(o)
            send_mix(0)
        strain = note_recv[pl.ds(raw_side * rows, rows), 0, :]
        means = solve_rows(raw_recv, strain, 16, raw_new, props, green, plane, buffers)
        send_means(means, 0, rows, mean_raw.at[me], R_MRAW, 1, 0)
        give_back(raw_new, 0, rows, groups, R_GOT + 1, 1, 0)
        send_new(0, rows, far)
        send_new(0, early, near)
    if levels > 2:
        mixed[...] = strain_of(2 * groups + ranks * (2 * count_up((8, LANES), 0) + 1 - my_odd) + mine)
        mixed[...] = pltpu.roll(mixed[...], 32, 1)
        for u in range(half):
            mixed[half + u : half + u + 1, :] = note_recv[raw_side * rows + 2 * u + my_odd][0:1, :]
        if ranks > 1:
            expect((ranks - 1) * half, recv.at[R_MIXT])
        expect(ranks * half, recv.at[R_MIX])
        means = solve_rows(mix_recv, mixed[0:rows, :], 32, mix_new, props, green, plane, buffers)
        mean_mix[mine] = means
        for o in far:
            push(mean_mix.at[mine], mean_mix.at[mine], R_MMIX, me, (mine + o) % ranks)
        send_means(means, half, half, mean_far.at[my_pair * ranks + my_side], R_MFAR, 2, my_odd)
        send_mixed(far)
        give_back(mix_new, half, half, 2 * groups, R_GOT + 2, 2, my_odd)
        send_mixed(near)
    if levels > 1:
        send_new(early, rows, near)

    fetches[9].wait()
    fetches[10].wait()
    fetches[11].wait()
    deep = (levels * groups, LANES)
    k = count_up(deep, 0)
    inside = k % groups
    known = ranks * (inside % rows) + inside // rows
    if ranks > 1:
        drain(mean_src.at[pl.ds(0, ranks - 1)], recv.at[R_MEAN])
    for y in range(ranks):
        mean_all[y * rows : (y + 1) * rows, :] = mean_src[y]
    if levels > 1:
        drain(mean_raw, recv.at[R_MRAW])
        mean_all[groups : 2 * groups, :] = mean_raw[:, 0, :]
        known = jnp.where(k < groups, known, k)
    if levels > 2:
        if ranks > 1:
            drain(mean_mix.at[pl.ds(0, ranks - 1)], recv.at[R_MMIX])
        drain(mean_far, recv.at[R_MFAR])
        middle = 2 * groups + groups // 2
        for y in range(ranks):
            low = 2 * groups + y * half
            mean_all[low : low + half, :] = mean_mix[y, 0:half, :]
        mean_all[middle:, :] = mean_far[:, 0, :]
        from_src = 2 * groups + ranks * (2 * (inside % half) + 1 - my_odd) + inside // half
        v = inside - groups // 2
        from_raw = 2 * groups + ranks * (2 * (v // ranks) + my_odd) + v % ranks
        known = jnp.where(k < 2 * groups, known, jnp.where(k < middle, from_src, from_raw))
    match = jnp.where(matched(known), 1.0, 0.0).astype(jnp.bfloat16)
    mean_t = jnp.transpose(mean_all[...])[0:8, :]
    averaged = select_dot(mean_t, match, False)[:, 0:elements]
    strain = all_strain[0:8, 0:elements]
    lame, shear = moduli[0:1, :], moduli[1:2, :]
    lateral = lame * (strain[0:1] + strain[1:2] + strain[2:3])
    plastic = owner[...] >= 0
    stress = []
    for c in range(6):
        plain = 2.0 * shear * strain[c : c + 1]
        plain = lateral + plain if c < 3 else plain
        stress.append(jnp.where(plastic, averaged[c : c + 1], plain))
    tensor = [[stress[0], stress[5], stress[4]], [stress[5], stress[1], stress[3]], [stress[4], stress[3], stress[2]]]
    forces[...] = jnp.zeros(forces.shape, f32)
    for i in range(3):
        force = volume[...] * (
            tensor[i][0] * grad[0] + tensor[i][1] * grad[1] + tensor[i][2] * grad[2]
        )
        for a in range(conn.shape[0]):
            forces[a, i : i + 1, :] = force[a : a + 1, :]
    assembled = jnp.zeros((8, LANES), f32)
    for a in range(conn.shape[0]):
        assembled = assembled + select_dot(forces[a], onehot[a], True)
    force_send[...] = assembled
    push(force_send, force_recv, R_FORCE, (me + groups - 1) % groups, mine)
    drain(force_recv, recv.at[R_FORCE])
    lane8 = count_up((8, LANES), 1)
    beyond = (lane8 >= own_nodes) & (lane8 < own_nodes + halos)
    back = jnp.where(beyond, force_recv[...], 0.0)
    total_force = assembled + select_dot(back, halo_match, True)
    residual[...] = total_force[0:3, 0:own_nodes] - load[...]

    for lv in range(levels):
        drain(got.at[pl.ds(lv * groups, groups)], recv.at[R_GOT + lv])
    order_scalars.wait()

    def place_row(j, carry):
        moved_out[:, j] = got[jnp.clip(order_ref[0, j], 0, levels * groups - 1)]
        return carry

    lax.fori_loop(0, moved_out.shape[1], place_row, 0)
    drain(note_send.at[pl.ds(0, groups - 1)], sent.at[R_NOTE])
    drain(halo_send, sent.at[R_HALO])
    drain(force_send, sent.at[R_FORCE])
    if ranks > 1:
        drain(props.at[pl.ds(0, ranks - 1)], sent.at[R_PROPS])
    if ranks > 1:
        drain(trade_send, sent.at[R_TRADE])
        drain(mean_src.at[pl.ds(0, ranks - 1)], sent.at[R_MEAN])
    settle(got.at[pl.ds(0, groups)], R_GOT, my_side == mine)
    own = (2 * me) % ranks == mine
    if levels > 1:
        settle(raw_send, R_RAW, own)
        settle(mean_raw, R_MRAW, own)
        if ranks > 1:
            expect((ranks - 1) * rows, sent.at[R_GOT + 1])
    if levels > 2:
        settle(mix_send, R_MIX, own)
        settle(mean_far, R_MFAR, own)
        if ranks > 1:
            drain(mix_trade, sent.at[R_MIXT])
            drain(mean_mix.at[pl.ds(0, ranks - 1)], sent.at[R_MMIX])
        expect(ranks * half + (ranks - 1) * half, sent.at[R_GOT + 2])


def exchange(smalls, state, moduli, tables, levels):
    groups, ranks = lax.axis_size("macro"), lax.axis_size("vox")
    rows = groups // ranks
    thickness = state.shape[2]
    half, extra, mix = rows // 2, min(levels - 1, 1), 1 if levels > 2 else 0
    nodes, corners, elements = smalls[0].shape[1], smalls[2].shape[0], smalls[2].shape[1]
    slab = (7, thickness, VOX_PLANE)
    hbm = pl.BlockSpec(memory_space=pltpu.HBM)
    vmem = pl.BlockSpec(memory_space=pltpu.VMEM)
    f32 = jnp.float32
    kinds = 13 + levels
    cells = levels * VOX_SIDE * rows * VOX_PLANE
    tile = pltpu.VMEM((8, LANES), f32)
    return pl.pallas_call(
        functools.partial(exchange_kernel, levels),
        out_shape=[
            jax.ShapeDtypeStruct((3, nodes), f32),
            jax.ShapeDtypeStruct((7, RECV_AGG) + slab[1:], f32),
        ],
        in_specs=[hbm] * (len(smalls) + 2 + len(tables)),
        out_specs=[vmem, vmem],
        scratch_shapes=[
            pltpu.VMEM(state.shape, f32),
            pltpu.VMEM((max(ranks - 1, 1), rows) + slab, f32),
            pltpu.VMEM((ranks, rows) + slab, f32),
            pltpu.VMEM((ranks, rows) + slab, f32),
            pltpu.VMEM((groups if extra else 1,) + slab, f32),
            pltpu.VMEM((ranks, rows if extra else 1) + slab, f32),
            pltpu.VMEM((ranks, rows if extra else 1) + slab, f32),
            pltpu.VMEM((max(ranks - 1, 1), half if mix else 1) + slab, f32),
            pltpu.VMEM((groups // 2 if mix else 1,) + slab, f32),
            pltpu.VMEM((ranks, rows if mix else 1) + slab, f32),
            pltpu.VMEM((ranks, rows if mix else 1) + slab, f32),
            pltpu.VMEM((levels * groups,) + slab, f32),
            pltpu.VMEM((ranks,) + moduli.shape, f32),
            pltpu.VMEM(tables[0].shape, f32),
            pltpu.VMEM(tables[1].shape, tables[1].dtype),
            pltpu.VMEM((7, VOX_SIDE, rows, VOX_PLANE), f32),
            pltpu.VMEM((6, VOX_SIDE, rows, VOX_PLANE), f32),
            pltpu.VMEM((6, VOX_SIDE, rows, VOX_PLANE), f32),
            pltpu.VMEM((6, HALF + 1, rows, VOX_PLANE), f32),
            pltpu.VMEM((6, HALF - 1, rows, VOX_PLANE), f32),
            pltpu.VMEM((groups, 8, LANES), f32),
            pltpu.VMEM((groups, 8, LANES), f32),
            pltpu.VMEM((ranks, rows, LANES), f32),
            pltpu.VMEM((groups, 8, LANES), f32),
            pltpu.VMEM((ranks, rows, LANES), f32),
            pltpu.VMEM((groups // 2, 8, LANES), f32),
            pltpu.VMEM((2 * rows, 8, LANES), f32),
            pltpu.VMEM((levels * groups, LANES), f32),
            tile,
            tile,
            tile,
            tile,
            tile,
            pltpu.VMEM((LANES, LANES), f32),
            pltpu.VMEM((corners, LANES, elements), jnp.bfloat16),
            pltpu.VMEM((corners, 8, elements), f32),
            pltpu.VMEM((8, LANES), jnp.int32),
        ]
        + [pltpu.VMEM(small.shape, small.dtype) for small in smalls]
        + [
            pltpu.VMEM((1, LANES), jnp.int32),
            pltpu.SMEM((1, LANES), jnp.int32),
            pltpu.VMEM((1, LANES), jnp.int32),
            pltpu.SMEM((1, LANES), jnp.int32),
            pltpu.SemaphoreType.DMA((13,)),
            pltpu.SemaphoreType.DMA((kinds,)),
            pltpu.SemaphoreType.DMA((kinds,)),
        ],
        compiler_params=pltpu.CompilerParams(
            collective_id=0, has_side_effects=True, vmem_limit_bytes=63 * 2**20
        ),
        cost_estimate=pl.CostEstimate(
            flops=SWEEPS * 2 * 3 * 2 * 6 * cells * VOX_PLANE,
            bytes_accessed=4 * 7 * cells * 4,
            transcendentals=SWEEPS * cells,
        ),
    )(*smalls, state, moduli, *tables)


def local(
    displacement,
    load,
    conn,
    halo_list,
    grad_ops,
    volume,
    elastic_moduli,
    plastic_mask,
    new_owner,
    state,
    micro_moduli,
):
    groups = lax.axis_size("macro")
    tables = (jnp.asarray(green_tables()), plane_tables())
    levels = (PLASTIC_MAX + groups - 1) // groups
    assert levels <= 3
    smalls = (
        displacement,
        load,
        conn,
        halo_list[None, :],
        grad_ops,
        volume[None, :],
        elastic_moduli,
        new_owner[None, :],
    )
    return tuple(exchange(smalls, state, micro_moduli, tables, levels))


def solution(mesh):
    return jax.shard_map(
        local,
        mesh=mesh,
        in_specs=(
            P(None, "macro"),
            P(None, "macro"),
            P(None, "macro"),
            P("macro"),
            P(None, None, "macro"),
            P("macro"),
            P(None, "macro"),
            P("macro"),
            P("macro"),
            P(None, "macro", "vox", None),
            P(None, "vox", None),
        ),
        out_specs=(P(None, "macro"), P(None, "macro", "vox", None)),
        check_vma=False,
    )
```

```python
import functools
import math

import jax
import jax.numpy as jnp
import numpy as np
from jax import lax
from jax.experimental import pallas as pl
from jax.experimental.pallas import tpu as pltpu
from jax.sharding import PartitionSpec as P

RECV_AGG = 24
PLASTIC_MAX = 48
VOX_SIDE = 16
VOX_PLANE = 256
SWEEPS = 4
HALF = VOX_SIDE // 2
LANES = 128

LAM_REF = 3.0
MU_REF = 3.0

ROOT = math.sqrt(0.5)
COS1 = math.cos(math.pi / 8)
COS3 = math.cos(3 * math.pi / 8)
PAIRS = [(i, j) for i in range(6) for j in range(i, 6)]


def green_tables():
    line = np.arange(VOX_SIDE)
    signed = np.where(line < HALF, line, line - VOX_SIDE).astype(np.float64)
    freq = np.stack(np.meshgrid(signed, signed, signed, indexing="ij"))
    norm = np.sum(freq * freq, axis=0)
    inverse = np.where(norm > 0, 1.0 / np.maximum(norm, 1.0), 0.0)
    coupling = (LAM_REF + MU_REF) / (LAM_REF + 2.0 * MU_REF)
    spots = [(0, 0), (1, 1), (2, 2), (1, 2), (0, 2), (0, 1)]
    table = np.zeros((6, 6) + norm.shape)
    for j, (a, b) in enumerate(spots):
        tau = np.zeros((3, 3))
        tau[a, b] = tau[b, a] = 1.0
        trac = np.einsum("ij,jxyz->ixyz", tau, freq)
        along = np.sum(freq * trac, axis=0) * inverse
        wave = (trac - coupling * along * freq) * inverse / MU_REF
        for i, (c, d) in enumerate(spots):
            table[i, j] = 0.5 * (freq[c] * wave[d] + freq[d] * wave[c])
    back = -line % VOX_SIDE
    flipped = table[:, :, back][:, :, :, back][:, :, :, :, back]
    even = 0.5 * (table + flipped) / VOX_SIDE**3
    even[:, 3:] *= 0.5
    stacked = np.stack([even[i, j] for i, j in PAIRS])
    return stacked.reshape(len(PAIRS), VOX_SIDE, VOX_PLANE).astype(np.float32)


def plane_tables():
    plane = np.arange(VOX_PLANE)
    rows, cols = plane // VOX_SIDE, plane % VOX_SIDE
    phase = (rows[:, None] * rows[None, :] + cols[:, None] * cols[None, :]) % VOX_SIDE
    angle = phase * (2.0 * math.pi / VOX_SIDE)
    plus = jnp.asarray((np.cos(angle) + np.sin(angle)).astype(np.float32))
    minus = jnp.asarray((np.cos(angle) - np.sin(angle)).astype(np.float32))
    out = []
    for table in (plus, minus):
        high = table.astype(jnp.bfloat16)
        out += [high, (table - high.astype(jnp.float32)).astype(jnp.bfloat16)]
    return jnp.stack(out)


def cosine_line(a):
    sums = [None] + [a[x] + a[8 - x] for x in (1, 2, 3)]
    diffs = [None] + [a[x] - a[8 - x] for x in (1, 2, 3)]
    even0, odd0 = a[0] + a[8], a[0] - a[8]
    outer, inner = even0 + a[4], even0 - a[4]
    spread = sums[1] + sums[3]
    slant = ROOT * (sums[1] - sums[3])
    mid = ROOT * diffs[2]
    first = COS1 * diffs[1] + COS3 * diffs[3]
    second = COS3 * diffs[1] - COS1 * diffs[3]
    top, low = odd0 + mid, odd0 - mid
    core = outer + sums[2]
    return [
        core + spread,
        top + first,
        inner + slant,
        low + second,
        outer - sums[2],
        low - second,
        inner - slant,
        top - first,
        core - spread,
    ]


def sine_line(b):
    sums = [None] + [b[x] + b[8 - x] for x in (1, 2, 3)]
    diffs = [None] + [b[x] - b[8 - x] for x in (1, 2, 3)]
    slant = ROOT * (diffs[1] + diffs[3])
    mid = ROOT * sums[2]
    first = COS3 * sums[1] + COS1 * sums[3]
    second = COS1 * sums[1] - COS3 * sums[3]
    return [
        None,
        (first + mid) + b[4],
        slant + diffs[2],
        (second + mid) - b[4],
        diffs[1] - diffs[3],
        (second - mid) + b[4],
        slant - diffs[2],
        (first - mid) - b[4],
    ]


def split_dot(block, table_ref, first):
    high = block.astype(jnp.bfloat16)
    low = (block - high.astype(jnp.float32)).astype(jnp.bfloat16)
    dot = functools.partial(jnp.dot, preferred_element_type=jnp.float32)
    return dot(high, table_ref[first]) + (dot(high, table_ref[first + 1]) + dot(low, table_ref[first]))


def voxel_law(strain, state, props, row):
    lam, mu = props[0, row, :], props[1, row, :]
    yield_base, harden = props[2, row, :], props[3, row, :]
    two_mu, three_mu = 2.0 * mu, 3.0 * mu
    stiff_inv = 1.0 / (three_mu + harden)
    bulk = lam + two_mu * (1.0 / 3.0)
    elastic = [strain[c] - state[c] for c in range(6)]
    trace = elastic[0] + elastic[1] + elastic[2]
    third = trace * (1.0 / 3.0)
    shape = [elastic[c] - third for c in range(3)] + elastic[3:]
    normal = shape[0] * shape[0] + shape[1] * shape[1] + shape[2] * shape[2]
    shear = shape[3] * shape[3] + shape[4] * shape[4] + shape[5] * shape[5]
    equivalent = two_mu * jnp.sqrt(1.5 * (normal + 2.0 * shear))
    strength = yield_base + harden * state[6]
    gain = jnp.maximum(equivalent - strength, 0.0) * stiff_inv
    factor = gain / jnp.maximum(equivalent, strength)
    keep = two_mu * (1.0 - three_mu * factor)
    pressure = bulk * trace
    stress = [pressure + keep * shape[c] for c in range(3)] + [keep * shape[c] for c in range(3, 6)]
    return stress, shape, (1.5 * two_mu) * factor, gain


def solve_rows(pieces, strain, base, out, props, green, plane, buffers, hook):
    stx, eps, work, cos_ref, sin_ref = buffers
    ranks, rows, _, thickness, _ = pieces.shape

    def bring(c, carry):
        for h in range(ranks):
            stx[c, h * thickness : (h + 1) * thickness] = jnp.swapaxes(pieces[h, :, c], 0, 1)
        return carry

    lax.fori_loop(0, 7, bring, 0)
    for c in range(6):
        eps[c] = jnp.broadcast_to(strain[:, base + c : base + c + 1][None], (VOX_SIDE, rows, VOX_PLANE))

    def sweep(step, carry):
        hook(step)
        for h in range(ranks):

            def law(place, inner, h=h):
                x = h * thickness + place
                strain = [eps[c, x] for c in range(6)]
                state = [stx[c, x] for c in range(7)]
                stress = voxel_law(strain, state, props.at[h], pl.ds(place, 1))[0]
                for c in range(6):
                    work[c, x] = stress[c]
                return inner

            lax.fori_loop(0, thickness, law, 0)

        def forward(c, inner):
            field = [work[c, x] for x in range(VOX_SIDE)]
            sums = [field[0]] + [field[x] + field[VOX_SIDE - x] for x in range(1, HALF)] + [field[HALF]]
            diffs = [None] + [field[x] - field[VOX_SIDE - x] for x in range(1, HALF)]
            for k, value in enumerate(cosine_line(sums)):
                cos_ref[c, k] = value
            for k, value in enumerate(sine_line(diffs)):
                if k > 0:
                    sin_ref[c, k - 1] = value
            return inner

        lax.fori_loop(0, 6, forward, 0)

        def transform():
            for ref, first in ((cos_ref, 0), (sin_ref, 2)):
                flat = ref[...].reshape(6 * ref.shape[1] * rows, VOX_PLANE)
                ref[...] = split_dot(flat, plane, first).reshape(ref.shape)

        def apply(field, k):
            row = pl.ds(k, 1)
            field = field[:3] + [2.0 * field[c] for c in range(3, 6)]
            total = [None] * 6
            for n, (i, j) in enumerate(PAIRS):
                entry = green[n, row, :]
                for a, b in [(i, j), (j, i)][: 1 + (i != j)]:
                    term = entry * field[b]
                    total[a] = term if total[a] is None else total[a] + term
            return total

        transform()
        for k in (0, HALF):
            result = apply([cos_ref[c, k] for c in range(6)], k)
            for c in range(6):
                cos_ref[c, k] = result[c]

        def mix(k, inner):
            even = [cos_ref[c, k] for c in range(6)]
            odd = [sin_ref[c, k - 1] for c in range(6)]
            ahead = apply([even[c] + odd[c] for c in range(6)], k)
            behind = apply([even[c] - odd[c] for c in range(6)], VOX_SIDE - k)
            for c in range(6):
                cos_ref[c, k] = ahead[c] + behind[c]
                sin_ref[c, k - 1] = ahead[c] - behind[c]
            return inner

        lax.fori_loop(1, HALF, mix, 0)
        transform()

        def backward(c, inner):
            even = cosine_line([cos_ref[c, k] for k in range(HALF + 1)])
            odd = sine_line([None] + [sin_ref[c, k - 1] for k in range(1, HALF)])
            eps[c, 0] = eps[c, 0] - even[0]
            eps[c, HALF] = eps[c, HALF] - even[HALF]
            for x in range(1, HALF):
                eps[c, x] = eps[c, x] - (even[x] + odd[x])
                eps[c, VOX_SIDE - x] = eps[c, VOX_SIDE - x] - (even[x] - odd[x])
            return inner

        lax.fori_loop(0, 6, backward, 0)
        return carry

    lax.fori_loop(0, SWEEPS, sweep, 0)
    totals = (jnp.zeros((rows, VOX_PLANE), jnp.float32),) * 6
    for h in range(ranks):

        def finish(place, totals, h=h):
            x = h * thickness + place
            strain = [eps[c, x] for c in range(6)]
            state = [stx[c, x] for c in range(7)]
            stress, shape, scale, gain = voxel_law(strain, state, props.at[h], pl.ds(place, 1))
            for c in range(6):
                stx[c, x] = state[c] + scale * shape[c]
            stx[6, x] = state[6] + gain
            return tuple(totals[c] + stress[c] for c in range(6))

        totals = lax.fori_loop(0, thickness, finish, totals)

    def give(c, carry):
        for h in range(ranks):
            out[h, :, c] = jnp.swapaxes(stx[c, h * thickness : (h + 1) * thickness], 0, 1)
        return carry

    lax.fori_loop(0, 7, give, 0)
    lane = lax.broadcasted_iota(jnp.int32, (rows, LANES), 1)
    means = jnp.zeros((rows, LANES), jnp.float32)
    for c in range(6):
        total = jnp.sum(totals[c], axis=1, keepdims=True) / VOX_SIDE**3
        means = jnp.where(lane == c, total, means)
    return means


def drain(ref, sem):
    pltpu.make_async_copy(ref, ref, sem).wait()


def pieces_of(value):
    high = value.astype(jnp.bfloat16)
    rest = value - high.astype(jnp.float32)
    middle = rest.astype(jnp.bfloat16)
    low = (rest - middle.astype(jnp.float32)).astype(jnp.bfloat16)
    return high, middle, low


def select_dot(value, match, lanes):
    contract = (((1,), (1 if lanes else 0,)), ((), ()))
    parts = [
        lax.dot_general(piece, match, contract, preferred_element_type=jnp.float32)
        for piece in pieces_of(value)
    ]
    return parts[0] + (parts[1] + parts[2])


def count_up(shape, axis):
    return lax.broadcasted_iota(jnp.int32, shape, axis)


def to_column(row, size):
    spot = count_up((size, LANES), 0) == count_up((size, LANES), 1)
    return jnp.sum(jnp.where(spot, row, 0.0), axis=1, keepdims=True)


def exchange_kernel(levels, *refs):
    (disp_hbm, load_hbm, conn_hbm, halo_hbm, grad_hbm, volume_hbm, moduli_hbm, owner_hbm) = refs[:8]
    (state_hbm, props_hbm, green_hbm, plane_hbm) = refs[8:12]
    residual_out, got, order_out = refs[12:15]
    (st, trade_send, trade_recv, trade_new, raw_send, raw_recv, raw_new) = refs[15:22]
    (mix_trade, mix_send, mix_recv, mix_new, props, green, plane) = refs[22:29]
    buffers = refs[29:34]
    (note_send, note_recv, mean_src, mean_raw, mean_mix, mean_far, stage, mean_all) = refs[34:42]
    (halo_send, halo_recv, force_send, force_recv, mixed, strain_ref, onehot, forces, rows_i) = refs[42:51]
    (disp, load, conn, halo, grad, volume, moduli, owner) = refs[51:59]
    (source_vec, source_ref, order_vec, residual, load_sem, recv, sent) = refs[59:]
    ranks, rows = trade_recv.shape[:2]
    groups, half = ranks * rows, rows // 2
    own_nodes, elements, halos = disp.shape[1], conn.shape[1], halo.shape[1]
    me, mine = lax.axis_index("macro"), lax.axis_index("vox")
    my_row, my_side = me // ranks, me % ranks
    raw_side = (mine + ranks * groups - me) % ranks
    my_odd, my_pair = my_row % 2, my_row // 2
    R_PROPS, R_NOTE, R_HALO, R_FORCE, R_TRADE, R_MEAN, R_RAW, R_MRAW, R_MIXT, R_MIX, R_MMIX, R_MFAR, R_GOT = range(13)
    f32 = jnp.float32

    def push(src, dst, kind, group, rank):
        pltpu.make_async_remote_copy(
            src_ref=src,
            dst_ref=dst,
            send_sem=sent.at[kind],
            recv_sem=recv.at[kind],
            device_id={"macro": group, "vox": rank},
            device_id_type=pl.DeviceIdType.MESH,
        ).start()

    def deliver(src, dst, kind, group, rank):
        here = (group == me) & (rank == mine)

        @pl.when(here)
        def _():
            pltpu.make_async_copy(src, dst, recv.at[kind]).start()

        @pl.when(jnp.logical_not(here))
        def _():
            push(src, dst, kind, group, rank)

    def settle(ref, kind, fewer):
        count = ref.shape[0]

        @pl.when(fewer)
        def _():
            drain(ref.at[pl.ds(0, count - 1)], sent.at[kind])

        @pl.when(jnp.logical_not(fewer))
        def _():
            drain(ref, sent.at[kind])

    def turn(step, count, block, spot):
        planes = count // block
        line, lane = spot // block, spot % block
        ring = step // block
        line = jnp.where(2 * line < planes, planes - 1 - ring, ring)
        return line * block + (lane + step) % block

    fetches = {}
    for n, (src, dst) in enumerate(
        (
            (owner_hbm, owner),
            (halo_hbm, halo),
            (disp_hbm, disp),
            (state_hbm, st),
            (conn_hbm, conn),
            (grad_hbm, grad),
            (props_hbm, props.at[mine]),
            (green_hbm, green),
            (plane_hbm, plane),
            (volume_hbm, volume),
            (moduli_hbm, moduli),
            (load_hbm, load),
        )
    ):
        fetches[n] = pltpu.make_async_copy(src, dst, load_sem.at[n])
        fetches[n].start()

    barrier = pltpu.get_barrier_semaphore()
    total = groups * ranks
    flat = me * ranks + mine

    def greet(k, carry):
        other = (flat + k) % total
        pl.semaphore_signal(
            barrier,
            inc=1,
            device_id={"macro": other // ranks, "vox": other % ranks},
            device_id_type=pl.DeviceIdType.MESH,
        )
        return carry

    lax.fori_loop(1, total, greet, 0)

    rows_i[...] = jnp.full(rows_i.shape, -1, jnp.int32)
    fetches[0].wait()
    rows_i[0:1, 0:elements] = owner[...]
    owner_row = rows_i[0:1, :].astype(f32)
    square = (LANES, LANES)
    owner_col = to_column(owner_row, LANES)
    before = count_up(square, 0) < count_up(square, 1)
    same = (owner_col == owner_row) & before
    rank_row = jnp.sum(jnp.where(same, 1.0, 0.0), axis=0, keepdims=True)
    slot_row = jnp.where(owner_row >= 0.0, rank_row * groups + owner_row, -1.0)
    slot_col = to_column(slot_row, LANES)
    hit = slot_col == count_up(square, 1).astype(f32)
    spots = jnp.where(hit, count_up(square, 0).astype(f32), 0.0)
    source_vec[...] = jnp.sum(spots, axis=0, keepdims=True).astype(jnp.int32)
    to_scalars = pltpu.make_async_copy(source_vec, source_ref, load_sem.at[12])
    to_scalars.start()

    fetches[1].wait()
    fetches[2].wait()
    rows_i[1:2, own_nodes : own_nodes + halos] = halo[...]
    halo_match = (count_up(square, 0) == rows_i[1:2, :]).astype(jnp.bfloat16)
    halo_send[...] = jnp.zeros(halo_send.shape, f32)
    halo_send[0:3, 0:own_nodes] = disp[...]
    own_disp = halo_send[...]
    halo_send[...] = select_dot(own_disp, halo_match, False)

    to_scalars.wait()
    fetches[3].wait()

    def slab_of(slot):
        return st[:, jnp.clip(source_ref[0, slot], 0, elements - 1)]

    def expect(count, sem):
        drain(got.at[pl.ds(0, count)], sem)

    def gather_trade(low, stride, start, here, away):
        for o in range(ranks):

            def gather(i, carry, o=o):
                slab = slab_of(low + ranks * (stride * i + start) + (mine + o) % ranks)
                if o == 0:
                    here[mine, i] = slab
                else:
                    away[o - 1, i] = slab
                return carry

            lax.fori_loop(0, away.shape[1], gather, 0)

    gather_trade(0, 1, 0, trade_recv, trade_send)
    if levels > 1:

        def gather_raw(d, carry):
            raw_send[d] = slab_of(groups + d)
            return carry

        lax.fori_loop(0, groups, gather_raw, 0)
    if levels > 2:
        gather_trade(2 * groups, 2, 1 - my_odd, mix_recv, mix_trade)

        def gather_mix(v, carry):
            mix_send[v] = slab_of(2 * groups + ranks * (2 * (v // ranks) + my_odd) + v % ranks)
            return carry

        lax.fori_loop(0, groups // 2, gather_mix, 0)
    pl.semaphore_wait(barrier, total - 1)

    row_block = math.gcd(rows, 2)

    def side_of(o):
        side = (mine + o) % ranks
        return side, (side + ranks * groups - me) % ranks

    def send_raw(o):
        side, spot = side_of(o)

        def step(t, carry):
            d = ranks * turn(t, rows, row_block, my_row) + spot
            deliver(raw_send.at[d], raw_recv.at[mine, my_row], R_RAW, d, side)
            return carry

        lax.fori_loop(0, rows, step, 0)

    def send_mix(o):
        side, spot = side_of(o)

        def step(t, carry):
            u = turn(t, half, 1, my_pair)
            d = ranks * (2 * u + my_odd) + spot
            deliver(mix_send.at[u * ranks + spot], mix_recv.at[mine, half + my_pair], R_MIX, d, side)
            return carry

        lax.fori_loop(0, half, step, 0)

    push(halo_send, halo_recv, R_HALO, (me + 1) % groups, mine)
    for o in range(1, ranks):
        push(props_hbm, props.at[mine], R_PROPS, me, (mine + o) % ranks)
    for o in range(1, ranks):
        push(trade_send.at[o - 1], trade_recv.at[mine], R_TRADE, me, (mine + o) % ranks)
    if levels > 1:
        send_raw(0)

    fetches[4].wait()
    fetches[5].wait()
    tall = (LANES, elements)
    for a in range(conn.shape[0]):
        onehot[a] = (count_up(tall, 0) == conn[a : a + 1, :]).astype(jnp.bfloat16)
    drain(halo_recv, recv.at[R_HALO])
    lane8 = count_up((8, LANES), 1)
    near = jnp.where(lane8 < own_nodes, own_disp, halo_recv[...])
    products = [jnp.zeros((8, elements), f32) for _ in range(3)]
    for a in range(conn.shape[0]):
        moved = select_dot(near, onehot[a], False)
        for j in range(3):
            products[j] = products[j] + moved * grad[j, a : a + 1, :]
    strain_ref[...] = jnp.zeros(strain_ref.shape, f32)
    strain_rows = [
        products[0][0:1],
        products[1][1:2],
        products[2][2:3],
        0.5 * (products[2][1:2] + products[1][2:3]),
        0.5 * (products[2][0:1] + products[0][2:3]),
        0.5 * (products[1][0:1] + products[0][1:2]),
    ]
    for c in range(6):
        strain_ref[c : c + 1, 0:elements] = strain_rows[c]
    all_strain = strain_ref[...]

    def matched(ids):
        return ids.astype(f32) == slot_row

    wide = (groups, LANES)
    note = jnp.zeros(wide, f32)
    strain_pieces = pieces_of(all_strain)

    def strain_of(ids):
        match = jnp.where(matched(ids), 1.0, 0.0).astype(jnp.bfloat16)
        parts = [
            lax.dot_general(match, piece, (((1,), (1,)), ((), ())), preferred_element_type=f32)
            for piece in strain_pieces
        ]
        return parts[0] + (parts[1] + parts[2])

    for lv in range(1, levels):
        held = strain_of(count_up(wide, 0) + lv * groups)
        note = note + pltpu.roll(held, 16 * lv, 1)
    for lv in range(levels):
        held = jnp.where(matched(count_up(wide, 0) + lv * groups), 1.0, 0.0)
        note = jnp.where(count_up(wide, 1) == 8 + lv, jnp.sum(held, axis=1, keepdims=True), note)
    for d in range(groups):
        note_send[d] = jnp.broadcast_to(note[d : d + 1, :], (8, LANES))

    def send_note(t, carry):
        d = turn(t, groups, math.gcd(groups, 4), me)
        deliver(note_send.at[d], note_recv.at[my_side * rows + my_row], R_NOTE, d, mine)
        return carry

    lax.fori_loop(0, groups, send_note, 0)
    fetches[6].wait()
    fetches[7].wait()
    fetches[8].wait()
    if ranks > 1:
        drain(props.at[pl.ds(0, ranks - 1)], recv.at[R_PROPS])

    def send_row(t, turns):
        i = turn(t, rows, row_block, my_row)
        for o in turns:
            h = (mine + o) % ranks
            deliver(trade_new.at[h, i], got.at[me], R_GOT, ranks * i + mine, h)

    def send_new(low, high, turns):
        def step(t, carry):
            send_row(t, turns)
            return carry

        lax.fori_loop(low, high, step, 0)

    def send_mixed(turns):
        def step(t, carry):
            u = turn(t, half, 1, my_pair)
            for o in turns:
                h = (mine + o) % ranks
                spot = ranks * (2 * u + 1 - my_odd) + mine
                push(mix_new.at[h, u], got.at[2 * groups + me], R_GOT + 2, spot, h)
            return carry

        lax.fori_loop(0, half, step, 0)

    def give_back(new, first, count, low, kind, stride, start):
        def step(i, carry):
            for o in range(ranks):
                h = (mine + o) % ranks
                giver = ranks * (stride * i + start) + raw_side
                deliver(new.at[h, first + i], got.at[low + giver], kind, me, h)
            return carry

        lax.fori_loop(0, count, step, 0)

    def send_means(means, first, count, dst, kind, stride, start):
        for i in range(count):
            stage[first + i if count < rows else rows + i] = jnp.broadcast_to(
                means[first + i : first + i + 1, :], (8, LANES)
            )

        def step(t, carry):
            i = turn(t, count, math.gcd(count, 2), my_row * count // rows)
            for h in range(ranks):
                src = stage.at[first + i if count < rows else rows + i]
                deliver(src, dst, kind, ranks * (stride * i + start) + raw_side, h)
            return carry

        lax.fori_loop(0, count, step, 0)

    near, far = range(1), range(1, ranks)

    def trade_mix():
        for o in far:
            push(mix_trade.at[o - 1], mix_recv.at[mine, pl.ds(0, half)], R_MIXT, me, (mine + o) % ranks)

    def first_hook(step):
        if levels > 2:
            pl.when(step == SWEEPS - 1)(trade_mix)

    def second_hook(step):
        if levels > 2:

            @pl.when(step >= SWEEPS - 2)
            def _():
                low = 2 * (step - (SWEEPS - 2))
                send_row(low, far)
                send_row(low + 1, far)

    def third_hook(step):
        send_row(2 * step, near)
        send_row(2 * step + 1, near)

    strain = strain_of(ranks * count_up((rows, LANES), 0) + mine)
    if ranks > 1:
        expect((ranks - 1) * rows, recv.at[R_TRADE])
    if levels > 1:
        for o in far:
            send_raw(o)
    means = solve_rows(trade_recv, strain, 0, trade_new, props, green, plane, buffers, first_hook)
    mean_src[mine] = means
    for o in far:
        push(mean_src.at[mine], mean_src.at[mine], R_MEAN, me, (mine + o) % ranks)
    if levels == 1:
        send_new(0, rows, range(ranks))

    drain(note_recv, recv.at[R_NOTE])
    flags = note_recv[:, 0, :]
    spot = count_up(wide, 0)
    giver = (ranks * (spot % rows) + spot // rows).astype(f32)
    lane = count_up(wide, 1)
    counts = jnp.sum(jnp.where((lane >= 8) & (lane < 8 + levels), flags, 0.0), axis=1, keepdims=True)
    tall_count = jnp.sum(
        jnp.where(
            (count_up(wide, 0) == lane) & (lane < groups), jnp.broadcast_to(counts, wide), 0.0
        ),
        axis=0,
        keepdims=True,
    )
    lane_giver = (ranks * (lane % rows) + lane // rows).astype(f32)
    earlier = (lane_giver < giver) & (lane < groups)
    place = jnp.sum(jnp.where(earlier, tall_count, 0.0), axis=1, keepdims=True)
    picks = jnp.zeros((1, LANES), f32)
    for lv in range(levels):
        held = jnp.sum(jnp.where(lane == 8 + lv, flags, 0.0), axis=1, keepdims=True)
        chosen = (place == lane.astype(f32)) & (held > 0.5)
        picks = picks + jnp.sum(jnp.where(chosen, lv * groups + giver, 0.0), axis=0, keepdims=True)
        place = place + held
    order_vec[...] = picks.astype(jnp.int32)
    give_order = pltpu.make_async_copy(order_vec, order_out, load_sem.at[12])
    give_order.start()

    if levels > 1:
        expect(groups, recv.at[R_RAW])
        if levels > 2:
            for o in range(ranks - 1, -1, -1):
                send_mix(o)
        strain = note_recv[pl.ds(raw_side * rows, rows), 0, :]
        means = solve_rows(raw_recv, strain, 16, raw_new, props, green, plane, buffers, second_hook)
        send_means(means, 0, rows, mean_raw.at[me], R_MRAW, 1, 0)
        give_back(raw_new, 0, rows, groups, R_GOT + 1, 1, 0)
        if levels > 2:
            send_new(half, rows, far)
        else:
            send_new(0, rows, range(ranks))
    if levels > 2:
        mixed[...] = strain_of(2 * groups + ranks * (2 * count_up((8, LANES), 0) + 1 - my_odd) + mine)
        mixed[...] = pltpu.roll(mixed[...], 32, 1)
        for u in range(half):
            mixed[half + u : half + u + 1, :] = note_recv[raw_side * rows + 2 * u + my_odd][0:1, :]
        if ranks > 1:
            expect((ranks - 1) * half, recv.at[R_MIXT])
        expect(ranks * half, recv.at[R_MIX])
        means = solve_rows(mix_recv, mixed[0:rows, :], 32, mix_new, props, green, plane, buffers, third_hook)
        mean_mix[mine] = means
        for o in far:
            push(mean_mix.at[mine], mean_mix.at[mine], R_MMIX, me, (mine + o) % ranks)
        send_means(means, half, half, mean_far.at[my_pair * ranks + my_side], R_MFAR, 2, my_odd)
        send_mixed(far)
        give_back(mix_new, half, half, 2 * groups, R_GOT + 2, 2, my_odd)
    fetches[9].wait()
    fetches[10].wait()
    fetches[11].wait()
    deep = (levels * groups, LANES)
    k = count_up(deep, 0)
    inside = k % groups
    known = ranks * (inside % rows) + inside // rows
    if ranks > 1:
        drain(mean_src.at[pl.ds(0, ranks - 1)], recv.at[R_MEAN])
    for y in range(ranks):
        mean_all[y * rows : (y + 1) * rows, :] = mean_src[y]
    if levels > 1:
        drain(mean_raw, recv.at[R_MRAW])
        mean_all[groups : 2 * groups, :] = mean_raw[:, 0, :]
        known = jnp.where(k < groups, known, k)
    if levels > 2:
        if ranks > 1:
            drain(mean_mix.at[pl.ds(0, ranks - 1)], recv.at[R_MMIX])
        drain(mean_far, recv.at[R_MFAR])
        middle = 2 * groups + groups // 2
        for y in range(ranks):
            low = 2 * groups + y * half
            mean_all[low : low + half, :] = mean_mix[y, 0:half, :]
        mean_all[middle:, :] = mean_far[:, 0, :]
        from_src = 2 * groups + ranks * (2 * (inside % half) + 1 - my_odd) + inside // half
        v = inside - groups // 2
        from_raw = 2 * groups + ranks * (2 * (v // ranks) + my_odd) + v % ranks
        known = jnp.where(k < 2 * groups, known, jnp.where(k < middle, from_src, from_raw))
    match = jnp.where(matched(known), 1.0, 0.0).astype(jnp.bfloat16)
    mean_t = jnp.transpose(mean_all[...])[0:8, :]
    averaged = select_dot(mean_t, match, False)[:, 0:elements]
    strain = all_strain[0:8, 0:elements]
    lame, shear = moduli[0:1, :], moduli[1:2, :]
    lateral = lame * (strain[0:1] + strain[1:2] + strain[2:3])
    plastic = owner[...] >= 0
    stress = []
    for c in range(6):
        plain = 2.0 * shear * strain[c : c + 1]
        plain = lateral + plain if c < 3 else plain
        stress.append(jnp.where(plastic, averaged[c : c + 1], plain))
    tensor = [[stress[0], stress[5], stress[4]], [stress[5], stress[1], stress[3]], [stress[4], stress[3], stress[2]]]
    forces[...] = jnp.zeros(forces.shape, f32)
    for i in range(3):
        force = volume[...] * (
            tensor[i][0] * grad[0] + tensor[i][1] * grad[1] + tensor[i][2] * grad[2]
        )
        for a in range(conn.shape[0]):
            forces[a, i : i + 1, :] = force[a : a + 1, :]
    assembled = jnp.zeros((8, LANES), f32)
    for a in range(conn.shape[0]):
        assembled = assembled + select_dot(forces[a], onehot[a], True)
    force_send[...] = assembled
    push(force_send, force_recv, R_FORCE, (me + groups - 1) % groups, mine)
    if levels > 2:
        send_mixed(near)
    drain(force_recv, recv.at[R_FORCE])
    lane8 = count_up((8, LANES), 1)
    beyond = (lane8 >= own_nodes) & (lane8 < own_nodes + halos)
    back = jnp.where(beyond, force_recv[...], 0.0)
    total_force = assembled + select_dot(back, halo_match, True)
    residual[...] = total_force[0:3, 0:own_nodes] - load[...]
    give_residual = pltpu.make_async_copy(residual, residual_out, load_sem.at[13])
    give_residual.start()

    for lv in range(levels):
        drain(got.at[pl.ds(lv * groups, groups)], recv.at[R_GOT + lv])
    give_order.wait()
    give_residual.wait()
    drain(note_send.at[pl.ds(0, groups - 1)], sent.at[R_NOTE])
    drain(halo_send, sent.at[R_HALO])
    drain(force_send, sent.at[R_FORCE])
    if ranks > 1:
        drain(props.at[pl.ds(0, ranks - 1)], sent.at[R_PROPS])
    if ranks > 1:
        drain(trade_send, sent.at[R_TRADE])
        drain(mean_src.at[pl.ds(0, ranks - 1)], sent.at[R_MEAN])
    settle(got.at[pl.ds(0, groups)], R_GOT, my_side == mine)
    own = (2 * me) % ranks == mine
    if levels > 1:
        settle(raw_send, R_RAW, own)
        settle(mean_raw, R_MRAW, own)
        if ranks > 1:
            expect((ranks - 1) * rows, sent.at[R_GOT + 1])
    if levels > 2:
        settle(mix_send, R_MIX, own)
        settle(mean_far, R_MFAR, own)
        if ranks > 1:
            drain(mix_trade, sent.at[R_MIXT])
            drain(mean_mix.at[pl.ds(0, ranks - 1)], sent.at[R_MMIX])
        expect(ranks * half + (ranks - 1) * half, sent.at[R_GOT + 2])


def exchange(smalls, state, moduli, tables, levels):
    groups, ranks = lax.axis_size("macro"), lax.axis_size("vox")
    rows = groups // ranks
    thickness = state.shape[2]
    half, extra, mix = rows // 2, min(levels - 1, 1), 1 if levels > 2 else 0
    nodes, corners, elements = smalls[0].shape[1], smalls[2].shape[0], smalls[2].shape[1]
    slab = (7, thickness, VOX_PLANE)
    hbm = pl.BlockSpec(memory_space=pltpu.HBM)
    f32 = jnp.float32
    kinds = 13 + levels
    cells = levels * VOX_SIDE * rows * VOX_PLANE
    tile = pltpu.VMEM((8, LANES), f32)
    return pl.pallas_call(
        functools.partial(exchange_kernel, levels),
        out_shape=[
            jax.ShapeDtypeStruct((3, nodes), f32),
            jax.ShapeDtypeStruct((levels * groups,) + slab, f32),
            jax.ShapeDtypeStruct((1, LANES), jnp.int32),
        ],
        in_specs=[hbm] * (len(smalls) + 2 + len(tables)),
        out_specs=[hbm] * 3,
        scratch_shapes=[
            pltpu.VMEM(state.shape, f32),
            pltpu.VMEM((max(ranks - 1, 1), rows) + slab, f32),
            pltpu.VMEM((ranks, rows) + slab, f32),
            pltpu.VMEM((ranks, rows) + slab, f32),
            pltpu.VMEM((groups if extra else 1,) + slab, f32),
            pltpu.VMEM((ranks, rows if extra else 1) + slab, f32),
            pltpu.VMEM((ranks, rows if extra else 1) + slab, f32),
            pltpu.VMEM((max(ranks - 1, 1), half if mix else 1) + slab, f32),
            pltpu.VMEM((groups // 2 if mix else 1,) + slab, f32),
            pltpu.VMEM((ranks, rows if mix else 1) + slab, f32),
            pltpu.VMEM((ranks, rows if mix else 1) + slab, f32),
            pltpu.VMEM((ranks,) + moduli.shape, f32),
            pltpu.VMEM(tables[0].shape, f32),
            pltpu.VMEM(tables[1].shape, tables[1].dtype),
            pltpu.VMEM((7, VOX_SIDE, rows, VOX_PLANE), f32),
            pltpu.VMEM((6, VOX_SIDE, rows, VOX_PLANE), f32),
            pltpu.VMEM((6, VOX_SIDE, rows, VOX_PLANE), f32),
            pltpu.VMEM((6, HALF + 1, rows, VOX_PLANE), f32),
            pltpu.VMEM((6, HALF - 1, rows, VOX_PLANE), f32),
            pltpu.VMEM((groups, 8, LANES), f32),
            pltpu.VMEM((groups, 8, LANES), f32),
            pltpu.VMEM((ranks, rows, LANES), f32),
            pltpu.VMEM((groups, 8, LANES), f32),
            pltpu.VMEM((ranks, rows, LANES), f32),
            pltpu.VMEM((groups // 2, 8, LANES), f32),
            pltpu.VMEM((2 * rows, 8, LANES), f32),
            pltpu.VMEM((levels * groups, LANES), f32),
            tile,
            tile,
            tile,
            tile,
            tile,
            pltpu.VMEM((LANES, LANES), f32),
            pltpu.VMEM((corners, LANES, elements), jnp.bfloat16),
            pltpu.VMEM((corners, 8, elements), f32),
            pltpu.VMEM((8, LANES), jnp.int32),
        ]
        + [pltpu.VMEM(small.shape, small.dtype) for small in smalls]
        + [
            pltpu.VMEM((1, LANES), jnp.int32),
            pltpu.SMEM((1, LANES), jnp.int32),
            pltpu.VMEM((1, LANES), jnp.int32),
            pltpu.VMEM((3, nodes), f32),
            pltpu.SemaphoreType.DMA((14,)),
            pltpu.SemaphoreType.DMA((kinds,)),
            pltpu.SemaphoreType.DMA((kinds,)),
        ],
        compiler_params=pltpu.CompilerParams(
            collective_id=0, has_side_effects=True, vmem_limit_bytes=63 * 2**20
        ),
        cost_estimate=pl.CostEstimate(
            flops=SWEEPS * 2 * 3 * 2 * 6 * cells * VOX_PLANE,
            bytes_accessed=4 * 7 * cells * 4,
            transcendentals=SWEEPS * cells,
        ),
    )(*smalls, state, moduli, *tables)


def pick_kernel(order_hbm, got, residual, residual_out, moved, order_ref, held, load_sem, slot_sem, out_sem):
    count, slots = held.shape[0], got.shape[0]
    fetch = pltpu.make_async_copy(order_hbm, order_ref, load_sem.at[0])
    fetch.start()
    keep = pltpu.make_async_copy(residual, residual_out, load_sem.at[1])
    keep.start()
    fetch.wait()

    def take(j):
        slot = jnp.clip(order_ref[0, j], 0, slots - 1)
        return pltpu.make_async_copy(got.at[slot], held.at[j], slot_sem.at[j])

    for j in range(count):
        take(j).start()
    for j in range(count):
        drain(held.at[j], slot_sem.at[j])
        pltpu.make_async_copy(held.at[j], moved.at[:, j], out_sem).start()
    keep.wait()
    drain(held, out_sem)


def pick_rows(order, got, residual):
    slab = got.shape[1:]
    hbm = pl.BlockSpec(memory_space=pltpu.HBM)
    return pl.pallas_call(
        pick_kernel,
        out_shape=[
            jax.ShapeDtypeStruct(residual.shape, jnp.float32),
            jax.ShapeDtypeStruct(slab[:1] + (RECV_AGG,) + slab[1:], jnp.float32),
        ],
        in_specs=[hbm] * 3,
        out_specs=[hbm] * 2,
        scratch_shapes=[
            pltpu.SMEM(order.shape, jnp.int32),
            pltpu.VMEM((RECV_AGG,) + slab, jnp.float32),
            pltpu.SemaphoreType.DMA((2,)),
            pltpu.SemaphoreType.DMA((RECV_AGG,)),
            pltpu.SemaphoreType.DMA,
        ],
        compiler_params=pltpu.CompilerParams(vmem_limit_bytes=63 * 2**20),
    )(order, got, residual)


def local(
    displacement,
    load,
    conn,
    halo_list,
    grad_ops,
    volume,
    elastic_moduli,
    plastic_mask,
    new_owner,
    state,
    micro_moduli,
):
    groups = lax.axis_size("macro")
    tables = (jnp.asarray(green_tables()), plane_tables())
    levels = (PLASTIC_MAX + groups - 1) // groups
    assert levels <= 3 and groups // lax.axis_size("vox") == 2 * SWEEPS
    smalls = (
        displacement,
        load,
        conn,
        halo_list[None, :],
        grad_ops,
        volume[None, :],
        elastic_moduli,
        new_owner[None, :],
    )
    residual, got, order = exchange(smalls, state, micro_moduli, tables, levels)
    return tuple(pick_rows(order, got, residual))


def solution(mesh):
    return jax.shard_map(
        local,
        mesh=mesh,
        in_specs=(
            P(None, "macro"),
            P(None, "macro"),
            P(None, "macro"),
            P("macro"),
            P(None, None, "macro"),
            P("macro"),
            P(None, "macro"),
            P("macro"),
            P("macro"),
            P(None, "macro", "vox", None),
            P(None, "vox", None),
        ),
        out_specs=(P(None, "macro"), P(None, "macro", "vox", None)),
        check_vma=False,
    )
```

```python
import functools
import math

import jax
import jax.numpy as jnp
import numpy as np
from jax import lax
from jax.experimental import pallas as pl
from jax.experimental.pallas import tpu as pltpu
from jax.sharding import PartitionSpec as P

RECV_AGG = 24
PLASTIC_MAX = 48
VOX_SIDE = 16
VOX_PLANE = 256
SWEEPS = 4
HALF = VOX_SIDE // 2
LANES = 128

LAM_REF = 3.0
MU_REF = 3.0

ROOT = math.sqrt(0.5)
COS1 = math.cos(math.pi / 8)
COS3 = math.cos(3 * math.pi / 8)
PAIRS = [(i, j) for i in range(6) for j in range(i, 6)]


def green_tables():
    line = np.arange(VOX_SIDE)
    signed = np.where(line < HALF, line, line - VOX_SIDE).astype(np.float64)
    freq = np.stack(np.meshgrid(signed, signed, signed, indexing="ij"))
    norm = np.sum(freq * freq, axis=0)
    inverse = np.where(norm > 0, 1.0 / np.maximum(norm, 1.0), 0.0)
    coupling = (LAM_REF + MU_REF) / (LAM_REF + 2.0 * MU_REF)
    spots = [(0, 0), (1, 1), (2, 2), (1, 2), (0, 2), (0, 1)]
    table = np.zeros((6, 6) + norm.shape)
    for j, (a, b) in enumerate(spots):
        tau = np.zeros((3, 3))
        tau[a, b] = tau[b, a] = 1.0
        trac = np.einsum("ij,jxyz->ixyz", tau, freq)
        along = np.sum(freq * trac, axis=0) * inverse
        wave = (trac - coupling * along * freq) * inverse / MU_REF
        for i, (c, d) in enumerate(spots):
            table[i, j] = 0.5 * (freq[c] * wave[d] + freq[d] * wave[c])
    back = -line % VOX_SIDE
    flipped = table[:, :, back][:, :, :, back][:, :, :, :, back]
    even = 0.5 * (table + flipped) / VOX_SIDE**3
    even[:, 3:] *= 0.5
    stacked = np.stack([even[i, j] for i, j in PAIRS])
    return stacked.reshape(len(PAIRS), VOX_SIDE, VOX_PLANE).astype(np.float32)


def plane_tables():
    plane = np.arange(VOX_PLANE)
    rows, cols = plane // VOX_SIDE, plane % VOX_SIDE
    phase = (rows[:, None] * rows[None, :] + cols[:, None] * cols[None, :]) % VOX_SIDE
    angle = phase * (2.0 * math.pi / VOX_SIDE)
    plus = jnp.asarray((np.cos(angle) + np.sin(angle)).astype(np.float32))
    minus = jnp.asarray((np.cos(angle) - np.sin(angle)).astype(np.float32))
    out = []
    for table in (plus, minus):
        high = table.astype(jnp.bfloat16)
        out += [high, (table - high.astype(jnp.float32)).astype(jnp.bfloat16)]
    return jnp.stack(out)


def cosine_line(a):
    sums = [None] + [a[x] + a[8 - x] for x in (1, 2, 3)]
    diffs = [None] + [a[x] - a[8 - x] for x in (1, 2, 3)]
    even0, odd0 = a[0] + a[8], a[0] - a[8]
    outer, inner = even0 + a[4], even0 - a[4]
    spread = sums[1] + sums[3]
    slant = ROOT * (sums[1] - sums[3])
    mid = ROOT * diffs[2]
    first = COS1 * diffs[1] + COS3 * diffs[3]
    second = COS3 * diffs[1] - COS1 * diffs[3]
    top, low = odd0 + mid, odd0 - mid
    core = outer + sums[2]
    return [
        core + spread,
        top + first,
        inner + slant,
        low + second,
        outer - sums[2],
        low - second,
        inner - slant,
        top - first,
        core - spread,
    ]


def sine_line(b):
    sums = [None] + [b[x] + b[8 - x] for x in (1, 2, 3)]
    diffs = [None] + [b[x] - b[8 - x] for x in (1, 2, 3)]
    slant = ROOT * (diffs[1] + diffs[3])
    mid = ROOT * sums[2]
    first = COS3 * sums[1] + COS1 * sums[3]
    second = COS1 * sums[1] - COS3 * sums[3]
    return [
        None,
        (first + mid) + b[4],
        slant + diffs[2],
        (second + mid) - b[4],
        diffs[1] - diffs[3],
        (second - mid) + b[4],
        slant - diffs[2],
        (first - mid) - b[4],
    ]


def split_dot(block, table_ref, first):
    high = block.astype(jnp.bfloat16)
    low = (block - high.astype(jnp.float32)).astype(jnp.bfloat16)
    dot = functools.partial(jnp.dot, preferred_element_type=jnp.float32)
    return dot(high, table_ref[first]) + (dot(high, table_ref[first + 1]) + dot(low, table_ref[first]))


def prepare_law(props, laws):
    for h in range(props.shape[0]):
        lam, mu, yield_base, harden = [props[h, n] for n in range(4)]
        stiff_inv = 1.0 / (3.0 * mu + harden)
        laws[h, 0] = 2.0 * mu
        laws[h, 1] = lam + 2.0 * mu * (1.0 / 3.0)
        laws[h, 2] = yield_base * (0.5 / mu)
        laws[h, 3] = harden * (0.5 / mu)
        laws[h, 4] = stiff_inv
        laws[h, 5] = 3.0 * mu * stiff_inv


def voxel_law(strain, state, laws, row):
    two_mu, bulk, yield_base, harden, stiff_inv, soften = [laws[n, row, :] for n in range(6)]
    elastic = [strain[c] - state[c] for c in range(6)]
    trace = elastic[0] + elastic[1] + elastic[2]
    third = trace * (1.0 / 3.0)
    shape = [elastic[c] - third for c in range(3)] + elastic[3:]
    normal = shape[0] * shape[0] + shape[1] * shape[1] + shape[2] * shape[2]
    shear = shape[3] * shape[3] + shape[4] * shape[4] + shape[5] * shape[5]
    squared = jnp.maximum(1.5 * normal + 3.0 * shear, 1e-30)
    inverse = lax.rsqrt(squared)
    strength = yield_base + harden * state[6]
    share = jnp.maximum(1.0 - strength * inverse, 0.0)
    keep = two_mu * (1.0 - soften * share)
    pressure = bulk * trace
    stress = [pressure + keep * shape[c] for c in range(3)] + [keep * shape[c] for c in range(3, 6)]
    return stress, shape, (two_mu * stiff_inv) * share, squared * inverse


def solve_rows(pieces, strain, base, out, laws, green, plane, buffers, hook):
    stx, eps, work, cos_ref, sin_ref = buffers
    ranks, rows, _, thickness, _ = pieces.shape
    batch = math.gcd(thickness, 4)

    def bring(c, carry):
        for h in range(ranks):
            stx[c, h * thickness : (h + 1) * thickness] = jnp.swapaxes(pieces[h, :, c], 0, 1)
        return carry

    lax.fori_loop(0, 7, bring, 0)
    for c in range(6):
        eps[c] = jnp.broadcast_to(strain[:, base + c : base + c + 1][None], (VOX_SIDE, rows, VOX_PLANE))

    def sweep(step, carry):
        hook(step)
        for h in range(ranks):

            def law(step, inner, h=h):
                for part in range(batch):
                    place = step * batch + part
                    x = h * thickness + place
                    strain = [eps[c, x] for c in range(6)]
                    state = [stx[c, x] for c in range(7)]
                    stress = voxel_law(strain, state, laws.at[h], pl.ds(place, 1))[0]
                    for c in range(6):
                        work[c, x] = stress[c]
                return inner

            lax.fori_loop(0, thickness // batch, law, 0)

        def forward(c, inner):
            field = [work[c, x] for x in range(VOX_SIDE)]
            sums = [field[0]] + [field[x] + field[VOX_SIDE - x] for x in range(1, HALF)] + [field[HALF]]
            diffs = [None] + [field[x] - field[VOX_SIDE - x] for x in range(1, HALF)]
            for k, value in enumerate(cosine_line(sums)):
                cos_ref[c, k] = value
            for k, value in enumerate(sine_line(diffs)):
                if k > 0:
                    sin_ref[c, k - 1] = value
            return inner

        lax.fori_loop(0, 6, forward, 0)

        def transform():
            for ref, first in ((cos_ref, 0), (sin_ref, 2)):
                flat = ref[...].reshape(6 * ref.shape[1] * rows, VOX_PLANE)
                ref[...] = split_dot(flat, plane, first).reshape(ref.shape)

        def apply(field, k):
            row = pl.ds(k, 1)
            field = field[:3] + [2.0 * field[c] for c in range(3, 6)]
            total = [None] * 6
            for n, (i, j) in enumerate(PAIRS):
                entry = green[n, row, :]
                for a, b in [(i, j), (j, i)][: 1 + (i != j)]:
                    term = entry * field[b]
                    total[a] = term if total[a] is None else total[a] + term
            return total

        transform()
        for k in (0, HALF):
            result = apply([cos_ref[c, k] for c in range(6)], k)
            for c in range(6):
                cos_ref[c, k] = result[c]

        def mix(k, inner):
            even = [cos_ref[c, k] for c in range(6)]
            odd = [sin_ref[c, k - 1] for c in range(6)]
            ahead = apply([even[c] + odd[c] for c in range(6)], k)
            behind = apply([even[c] - odd[c] for c in range(6)], VOX_SIDE - k)
            for c in range(6):
                cos_ref[c, k] = ahead[c] + behind[c]
                sin_ref[c, k - 1] = ahead[c] - behind[c]
            return inner

        lax.fori_loop(1, HALF, mix, 0)
        transform()

        def backward(c, inner):
            even = cosine_line([cos_ref[c, k] for k in range(HALF + 1)])
            odd = sine_line([None] + [sin_ref[c, k - 1] for k in range(1, HALF)])
            eps[c, 0] = eps[c, 0] - even[0]
            eps[c, HALF] = eps[c, HALF] - even[HALF]
            for x in range(1, HALF):
                eps[c, x] = eps[c, x] - (even[x] + odd[x])
                eps[c, VOX_SIDE - x] = eps[c, VOX_SIDE - x] - (even[x] - odd[x])
            return inner

        lax.fori_loop(0, 6, backward, 0)
        return carry

    lax.fori_loop(0, SWEEPS, sweep, 0)
    totals = (jnp.zeros((rows, VOX_PLANE), jnp.float32),) * 6
    for h in range(ranks):

        def finish(place, totals, h=h):
            x = h * thickness + place
            strain = [eps[c, x] for c in range(6)]
            state = [stx[c, x] for c in range(7)]
            stress, shape, gain, size = voxel_law(strain, state, laws.at[h], pl.ds(place, 1))
            for c in range(6):
                stx[c, x] = state[c] + (1.5 * gain) * shape[c]
            stx[6, x] = state[6] + gain * size
            return tuple(totals[c] + stress[c] for c in range(6))

        totals = lax.fori_loop(0, thickness, finish, totals)

    def give(c, carry):
        for h in range(ranks):
            out[h, :, c] = jnp.swapaxes(stx[c, h * thickness : (h + 1) * thickness], 0, 1)
        return carry

    lax.fori_loop(0, 7, give, 0)
    lane = lax.broadcasted_iota(jnp.int32, (rows, LANES), 1)
    means = jnp.zeros((rows, LANES), jnp.float32)
    for c in range(6):
        total = jnp.sum(totals[c], axis=1, keepdims=True) / VOX_SIDE**3
        means = jnp.where(lane == c, total, means)
    return means


def drain(ref, sem):
    pltpu.make_async_copy(ref, ref, sem).wait()


def pieces_of(value):
    high = value.astype(jnp.bfloat16)
    rest = value - high.astype(jnp.float32)
    middle = rest.astype(jnp.bfloat16)
    low = (rest - middle.astype(jnp.float32)).astype(jnp.bfloat16)
    return high, middle, low


def select_dot(value, match, lanes):
    contract = (((1,), (1 if lanes else 0,)), ((), ()))
    parts = [
        lax.dot_general(piece, match, contract, preferred_element_type=jnp.float32)
        for piece in pieces_of(value)
    ]
    return parts[0] + (parts[1] + parts[2])


def count_up(shape, axis):
    return lax.broadcasted_iota(jnp.int32, shape, axis)


def to_column(row, size):
    spot = count_up((size, LANES), 0) == count_up((size, LANES), 1)
    return jnp.sum(jnp.where(spot, row, 0.0), axis=1, keepdims=True)


def exchange_kernel(levels, *refs):
    (disp_hbm, load_hbm, conn_hbm, halo_hbm, grad_hbm, volume_hbm, moduli_hbm, owner_hbm) = refs[:8]
    (state_hbm, props_hbm, green_hbm, plane_hbm) = refs[8:12]
    residual_out, got, order_out = refs[12:15]
    (st, trade_send, trade_recv, trade_new, raw_send, raw_recv, raw_new) = refs[15:22]
    (mix_trade, mix_send, mix_recv, mix_new, props, green, plane) = refs[22:29]
    buffers = refs[29:34]
    (note_send, note_recv, mean_src, mean_raw, mean_mix, mean_far, stage, mean_all) = refs[34:42]
    (halo_send, halo_recv, force_send, force_recv, mixed, strain_ref, onehot, forces, rows_i) = refs[42:51]
    (disp, load, conn, halo, grad, volume, moduli, owner) = refs[51:59]
    (source_vec, source_ref, order_vec, residual, laws, load_sem, recv, sent) = refs[59:]
    ranks, rows = trade_recv.shape[:2]
    groups, half = ranks * rows, rows // 2
    own_nodes, elements, halos = disp.shape[1], conn.shape[1], halo.shape[1]
    me, mine = lax.axis_index("macro"), lax.axis_index("vox")
    my_row, my_side = me // ranks, me % ranks
    raw_side = (mine + ranks * groups - me) % ranks
    my_odd, my_pair = my_row % 2, my_row // 2
    R_PROPS, R_NOTE, R_HALO, R_FORCE, R_TRADE, R_MEAN, R_RAW, R_MRAW, R_MIXT, R_MIX, R_MMIX, R_MFAR, R_GOT = range(13)
    f32 = jnp.float32

    def push(src, dst, kind, group, rank):
        pltpu.make_async_remote_copy(
            src_ref=src,
            dst_ref=dst,
            send_sem=sent.at[kind],
            recv_sem=recv.at[kind],
            device_id={"macro": group, "vox": rank},
            device_id_type=pl.DeviceIdType.MESH,
        ).start()

    def deliver(src, dst, kind, group, rank):
        here = (group == me) & (rank == mine)

        @pl.when(here)
        def _():
            pltpu.make_async_copy(src, dst, recv.at[kind]).start()

        @pl.when(jnp.logical_not(here))
        def _():
            push(src, dst, kind, group, rank)

    def settle(ref, kind, fewer):
        count = ref.shape[0]

        @pl.when(fewer)
        def _():
            drain(ref.at[pl.ds(0, count - 1)], sent.at[kind])

        @pl.when(jnp.logical_not(fewer))
        def _():
            drain(ref, sent.at[kind])

    def turn(step, count, block, spot):
        planes = count // block
        line, lane = spot // block, spot % block
        ring = step // block
        line = jnp.where(2 * line < planes, planes - 1 - ring, ring)
        return line * block + (lane + step) % block

    fetches = {}
    for n, (src, dst) in enumerate(
        (
            (owner_hbm, owner),
            (halo_hbm, halo),
            (disp_hbm, disp),
            (state_hbm, st),
            (conn_hbm, conn),
            (grad_hbm, grad),
            (props_hbm, props.at[mine]),
            (green_hbm, green),
            (plane_hbm, plane),
            (volume_hbm, volume),
            (moduli_hbm, moduli),
            (load_hbm, load),
        )
    ):
        fetches[n] = pltpu.make_async_copy(src, dst, load_sem.at[n])
        fetches[n].start()

    barrier = pltpu.get_barrier_semaphore()
    total = groups * ranks
    flat = me * ranks + mine

    def greet(k, carry):
        other = (flat + k) % total
        pl.semaphore_signal(
            barrier,
            inc=1,
            device_id={"macro": other // ranks, "vox": other % ranks},
            device_id_type=pl.DeviceIdType.MESH,
        )
        return carry

    lax.fori_loop(1, total, greet, 0)

    rows_i[...] = jnp.full(rows_i.shape, -1, jnp.int32)
    fetches[0].wait()
    rows_i[0:1, 0:elements] = owner[...]
    owner_row = rows_i[0:1, :].astype(f32)
    square = (LANES, LANES)
    owner_col = to_column(owner_row, LANES)
    before = count_up(square, 0) < count_up(square, 1)
    same = (owner_col == owner_row) & before
    rank_row = jnp.sum(jnp.where(same, 1.0, 0.0), axis=0, keepdims=True)
    slot_row = jnp.where(owner_row >= 0.0, rank_row * groups + owner_row, -1.0)
    slot_col = to_column(slot_row, LANES)
    hit = slot_col == count_up(square, 1).astype(f32)
    spots = jnp.where(hit, count_up(square, 0).astype(f32), 0.0)
    source_vec[...] = jnp.sum(spots, axis=0, keepdims=True).astype(jnp.int32)
    to_scalars = pltpu.make_async_copy(source_vec, source_ref, load_sem.at[12])
    to_scalars.start()

    fetches[1].wait()
    fetches[2].wait()
    rows_i[1:2, own_nodes : own_nodes + halos] = halo[...]
    halo_match = (count_up(square, 0) == rows_i[1:2, :]).astype(jnp.bfloat16)
    halo_send[...] = jnp.zeros(halo_send.shape, f32)
    halo_send[0:3, 0:own_nodes] = disp[...]
    own_disp = halo_send[...]
    halo_send[...] = select_dot(own_disp, halo_match, False)

    to_scalars.wait()
    fetches[3].wait()

    def slab_of(slot):
        return st[:, jnp.clip(source_ref[0, slot], 0, elements - 1)]

    def expect(count, sem):
        drain(got.at[pl.ds(0, count)], sem)

    def gather_trade(low, stride, start, here, away, turns):
        for o in turns:

            def gather(i, carry, o=o):
                slab = slab_of(low + ranks * (stride * i + start) + (mine + o) % ranks)
                if o == 0:
                    here[mine, i] = slab
                else:
                    away[o - 1, i] = slab
                return carry

            lax.fori_loop(0, away.shape[1], gather, 0)

    gather_trade(0, 1, 0, trade_recv, trade_send, range(1, ranks))
    if levels > 1:

        def gather_raw(d, carry):
            raw_send[d] = slab_of(groups + d)
            return carry

        lax.fori_loop(0, groups, gather_raw, 0)
    pl.semaphore_wait(barrier, total - 1)

    row_block = math.gcd(rows, 2)

    def side_of(o):
        side = (mine + o) % ranks
        return side, (side + ranks * groups - me) % ranks

    def send_raw(o):
        side, spot = side_of(o)

        def step(t, carry):
            d = ranks * turn(t, rows, row_block, my_row) + spot
            deliver(raw_send.at[d], raw_recv.at[mine, my_row], R_RAW, d, side)
            return carry

        lax.fori_loop(0, rows, step, 0)

    def send_mix(o):
        side, spot = side_of(o)

        def step(t, carry):
            u = turn(t, half, 1, my_pair)
            d = ranks * (2 * u + my_odd) + spot
            deliver(mix_send.at[u * ranks + spot], mix_recv.at[mine, half + my_pair], R_MIX, d, side)
            return carry

        lax.fori_loop(0, half, step, 0)

    push(halo_send, halo_recv, R_HALO, (me + 1) % groups, mine)
    for o in range(1, ranks):
        push(props_hbm, props.at[mine], R_PROPS, me, (mine + o) % ranks)
    for o in range(1, ranks):
        push(trade_send.at[o - 1], trade_recv.at[mine], R_TRADE, me, (mine + o) % ranks)
    if levels > 1:
        send_raw(0)
    gather_trade(0, 1, 0, trade_recv, trade_send, range(1))
    if levels > 2:
        gather_trade(2 * groups, 2, 1 - my_odd, mix_recv, mix_trade, range(ranks))

        def gather_mix(v, carry):
            mix_send[v] = slab_of(2 * groups + ranks * (2 * (v // ranks) + my_odd) + v % ranks)
            return carry

        lax.fori_loop(0, groups // 2, gather_mix, 0)

    fetches[4].wait()
    fetches[5].wait()
    tall = (LANES, elements)
    for a in range(conn.shape[0]):
        onehot[a] = (count_up(tall, 0) == conn[a : a + 1, :]).astype(jnp.bfloat16)
    drain(halo_recv, recv.at[R_HALO])
    lane8 = count_up((8, LANES), 1)
    near = jnp.where(lane8 < own_nodes, own_disp, halo_recv[...])
    products = [jnp.zeros((8, elements), f32) for _ in range(3)]
    for a in range(conn.shape[0]):
        moved = select_dot(near, onehot[a], False)
        for j in range(3):
            products[j] = products[j] + moved * grad[j, a : a + 1, :]
    strain_ref[...] = jnp.zeros(strain_ref.shape, f32)
    strain_rows = [
        products[0][0:1],
        products[1][1:2],
        products[2][2:3],
        0.5 * (products[2][1:2] + products[1][2:3]),
        0.5 * (products[2][0:1] + products[0][2:3]),
        0.5 * (products[1][0:1] + products[0][1:2]),
    ]
    for c in range(6):
        strain_ref[c : c + 1, 0:elements] = strain_rows[c]
    all_strain = strain_ref[...]

    def matched(ids):
        return ids.astype(f32) == slot_row

    wide = (groups, LANES)
    note = jnp.zeros(wide, f32)
    strain_pieces = pieces_of(all_strain)

    def strain_of(ids):
        match = jnp.where(matched(ids), 1.0, 0.0).astype(jnp.bfloat16)
        parts = [
            lax.dot_general(match, piece, (((1,), (1,)), ((), ())), preferred_element_type=f32)
            for piece in strain_pieces
        ]
        return parts[0] + (parts[1] + parts[2])

    for lv in range(1, levels):
        held = strain_of(count_up(wide, 0) + lv * groups)
        note = note + pltpu.roll(held, 16 * lv, 1)
    for lv in range(levels):
        held = jnp.where(matched(count_up(wide, 0) + lv * groups), 1.0, 0.0)
        note = jnp.where(count_up(wide, 1) == 8 + lv, jnp.sum(held, axis=1, keepdims=True), note)
    for d in range(groups):
        note_send[d] = jnp.broadcast_to(note[d : d + 1, :], (8, LANES))

    def send_note(t, carry):
        d = turn(t, groups, math.gcd(groups, 4), me)
        deliver(note_send.at[d], note_recv.at[my_side * rows + my_row], R_NOTE, d, mine)
        return carry

    lax.fori_loop(0, groups, send_note, 0)
    fetches[6].wait()
    fetches[7].wait()
    fetches[8].wait()
    if ranks > 1:
        drain(props.at[pl.ds(0, ranks - 1)], recv.at[R_PROPS])
    prepare_law(props, laws)

    def send_row(t, turns):
        i = turn(t, rows, row_block, my_row)
        for o in turns:
            h = (mine + o) % ranks
            deliver(trade_new.at[h, i], got.at[me], R_GOT, ranks * i + mine, h)

    def send_new(low, high, turns):
        def step(t, carry):
            send_row(t, turns)
            return carry

        lax.fori_loop(low, high, step, 0)

    def send_mixed(turns):
        def step(t, carry):
            u = turn(t, half, 1, my_pair)
            for o in turns:
                h = (mine + o) % ranks
                spot = ranks * (2 * u + 1 - my_odd) + mine
                push(mix_new.at[h, u], got.at[2 * groups + me], R_GOT + 2, spot, h)
            return carry

        lax.fori_loop(0, half, step, 0)

    def give_back(new, first, count, low, kind, stride, start):
        def step(i, carry):
            for o in range(ranks):
                h = (mine + o) % ranks
                giver = ranks * (stride * i + start) + raw_side
                deliver(new.at[h, first + i], got.at[low + giver], kind, me, h)
            return carry

        lax.fori_loop(0, count, step, 0)

    def send_means(means, first, count, dst, kind, stride, start):
        for i in range(count):
            stage[first + i if count < rows else rows + i] = jnp.broadcast_to(
                means[first + i : first + i + 1, :], (8, LANES)
            )

        def step(t, carry):
            i = turn(t, count, math.gcd(count, 2), my_row * count // rows)
            for h in range(ranks):
                src = stage.at[first + i if count < rows else rows + i]
                deliver(src, dst, kind, ranks * (stride * i + start) + raw_side, h)
            return carry

        lax.fori_loop(0, count, step, 0)

    near, far = range(1), range(1, ranks)

    def trade_mix():
        for o in far:
            push(mix_trade.at[o - 1], mix_recv.at[mine, pl.ds(0, half)], R_MIXT, me, (mine + o) % ranks)

    def first_hook(step):
        if levels > 2:
            pl.when(step == SWEEPS - 2)(lambda: send_mix(0))
            pl.when(step == SWEEPS - 1)(trade_mix)

    def second_hook(step):
        if levels > 2:

            @pl.when(step >= SWEEPS - 2)
            def _():
                low = 2 * (step - (SWEEPS - 2))
                send_row(low, far)
                send_row(low + 1, far)

    def third_hook(step):
        @pl.when(step < SWEEPS // 2)
        def _():
            send_new(half * step, half * step + half, near)

    strain = strain_of(ranks * count_up((rows, LANES), 0) + mine)
    if ranks > 1:
        expect((ranks - 1) * rows, recv.at[R_TRADE])
    if levels > 1:
        for o in far:
            send_raw(o)
    means = solve_rows(trade_recv, strain, 0, trade_new, laws, green, plane, buffers, first_hook)
    mean_src[mine] = means
    for o in far:
        push(mean_src.at[mine], mean_src.at[mine], R_MEAN, me, (mine + o) % ranks)
    if levels == 1:
        send_new(0, rows, range(ranks))

    drain(note_recv, recv.at[R_NOTE])
    flags = note_recv[:, 0, :]
    spot = count_up(wide, 0)
    giver = (ranks * (spot % rows) + spot // rows).astype(f32)
    lane = count_up(wide, 1)
    counts = jnp.sum(jnp.where((lane >= 8) & (lane < 8 + levels), flags, 0.0), axis=1, keepdims=True)
    tall_count = jnp.sum(
        jnp.where(
            (count_up(wide, 0) == lane) & (lane < groups), jnp.broadcast_to(counts, wide), 0.0
        ),
        axis=0,
        keepdims=True,
    )
    lane_giver = (ranks * (lane % rows) + lane // rows).astype(f32)
    earlier = (lane_giver < giver) & (lane < groups)
    place = jnp.sum(jnp.where(earlier, tall_count, 0.0), axis=1, keepdims=True)
    picks = jnp.zeros((1, LANES), f32)
    for lv in range(levels):
        held = jnp.sum(jnp.where(lane == 8 + lv, flags, 0.0), axis=1, keepdims=True)
        chosen = (place == lane.astype(f32)) & (held > 0.5)
        picks = picks + jnp.sum(jnp.where(chosen, lv * groups + giver, 0.0), axis=0, keepdims=True)
        place = place + held
    order_vec[...] = picks.astype(jnp.int32)
    give_order = pltpu.make_async_copy(order_vec, order_out, load_sem.at[12])
    give_order.start()

    if levels > 1:
        expect(groups, recv.at[R_RAW])
        if levels > 2:
            for o in far:
                send_mix(o)
        strain = note_recv[pl.ds(raw_side * rows, rows), 0, :]
        means = solve_rows(raw_recv, strain, 16, raw_new, laws, green, plane, buffers, second_hook)
        send_means(means, 0, rows, mean_raw.at[me], R_MRAW, 1, 0)
        give_back(raw_new, 0, rows, groups, R_GOT + 1, 1, 0)
        if levels > 2:
            send_new(half, rows, far)
        else:
            send_new(0, rows, range(ranks))
    if levels > 2:
        mixed[...] = strain_of(2 * groups + ranks * (2 * count_up((8, LANES), 0) + 1 - my_odd) + mine)
        mixed[...] = pltpu.roll(mixed[...], 32, 1)
        for u in range(half):
            mixed[half + u : half + u + 1, :] = note_recv[raw_side * rows + 2 * u + my_odd][0:1, :]
        if ranks > 1:
            expect((ranks - 1) * half, recv.at[R_MIXT])
        expect(ranks * half, recv.at[R_MIX])
        means = solve_rows(mix_recv, mixed[0:rows, :], 32, mix_new, laws, green, plane, buffers, third_hook)
        mean_mix[mine] = means
        for o in far:
            push(mean_mix.at[mine], mean_mix.at[mine], R_MMIX, me, (mine + o) % ranks)
        send_means(means, half, half, mean_far.at[my_pair * ranks + my_side], R_MFAR, 2, my_odd)
        send_mixed(far)
        give_back(mix_new, half, half, 2 * groups, R_GOT + 2, 2, my_odd)
        send_mixed(near)
    fetches[9].wait()
    fetches[10].wait()
    fetches[11].wait()
    deep = (levels * groups, LANES)
    k = count_up(deep, 0)
    inside = k % groups
    known = ranks * (inside % rows) + inside // rows
    if ranks > 1:
        drain(mean_src.at[pl.ds(0, ranks - 1)], recv.at[R_MEAN])
    for y in range(ranks):
        mean_all[y * rows : (y + 1) * rows, :] = mean_src[y]
    if levels > 1:
        drain(mean_raw, recv.at[R_MRAW])
        mean_all[groups : 2 * groups, :] = mean_raw[:, 0, :]
        known = jnp.where(k < groups, known, k)
    if levels > 2:
        if ranks > 1:
            drain(mean_mix.at[pl.ds(0, ranks - 1)], recv.at[R_MMIX])
        drain(mean_far, recv.at[R_MFAR])
        middle = 2 * groups + groups // 2
        for y in range(ranks):
            low = 2 * groups + y * half
            mean_all[low : low + half, :] = mean_mix[y, 0:half, :]
        mean_all[middle:, :] = mean_far[:, 0, :]
        from_src = 2 * groups + ranks * (2 * (inside % half) + 1 - my_odd) + inside // half
        v = inside - groups // 2
        from_raw = 2 * groups + ranks * (2 * (v // ranks) + my_odd) + v % ranks
        known = jnp.where(k < 2 * groups, known, jnp.where(k < middle, from_src, from_raw))
    match = jnp.where(matched(known), 1.0, 0.0).astype(jnp.bfloat16)
    mean_t = jnp.transpose(mean_all[...])[0:8, :]
    averaged = select_dot(mean_t, match, False)[:, 0:elements]
    strain = all_strain[0:8, 0:elements]
    lame, shear = moduli[0:1, :], moduli[1:2, :]
    lateral = lame * (strain[0:1] + strain[1:2] + strain[2:3])
    plastic = owner[...] >= 0
    stress = []
    for c in range(6):
        plain = 2.0 * shear * strain[c : c + 1]
        plain = lateral + plain if c < 3 else plain
        stress.append(jnp.where(plastic, averaged[c : c + 1], plain))
    tensor = [[stress[0], stress[5], stress[4]], [stress[5], stress[1], stress[3]], [stress[4], stress[3], stress[2]]]
    forces[...] = jnp.zeros(forces.shape, f32)
    for i in range(3):
        force = volume[...] * (
            tensor[i][0] * grad[0] + tensor[i][1] * grad[1] + tensor[i][2] * grad[2]
        )
        for a in range(conn.shape[0]):
            forces[a, i : i + 1, :] = force[a : a + 1, :]
    assembled = jnp.zeros((8, LANES), f32)
    for a in range(conn.shape[0]):
        assembled = assembled + select_dot(forces[a], onehot[a], True)
    force_send[...] = assembled
    push(force_send, force_recv, R_FORCE, (me + groups - 1) % groups, mine)
    drain(force_recv, recv.at[R_FORCE])
    lane8 = count_up((8, LANES), 1)
    beyond = (lane8 >= own_nodes) & (lane8 < own_nodes + halos)
    back = jnp.where(beyond, force_recv[...], 0.0)
    total_force = assembled + select_dot(back, halo_match, True)
    residual[...] = total_force[0:3, 0:own_nodes] - load[...]
    give_residual = pltpu.make_async_copy(residual, residual_out, load_sem.at[13])
    give_residual.start()

    for lv in range(levels):
        drain(got.at[pl.ds(lv * groups, groups)], recv.at[R_GOT + lv])
    give_order.wait()
    give_residual.wait()
    drain(note_send.at[pl.ds(0, groups - 1)], sent.at[R_NOTE])
    drain(halo_send, sent.at[R_HALO])
    drain(force_send, sent.at[R_FORCE])
    if ranks > 1:
        drain(props.at[pl.ds(0, ranks - 1)], sent.at[R_PROPS])
    if ranks > 1:
        drain(trade_send, sent.at[R_TRADE])
        drain(mean_src.at[pl.ds(0, ranks - 1)], sent.at[R_MEAN])
    settle(got.at[pl.ds(0, groups)], R_GOT, my_side == mine)
    own = (2 * me) % ranks == mine
    if levels > 1:
        settle(raw_send, R_RAW, own)
        settle(mean_raw, R_MRAW, own)
        if ranks > 1:
            expect((ranks - 1) * rows, sent.at[R_GOT + 1])
    if levels > 2:
        settle(mix_send, R_MIX, own)
        settle(mean_far, R_MFAR, own)
        if ranks > 1:
            drain(mix_trade, sent.at[R_MIXT])
            drain(mean_mix.at[pl.ds(0, ranks - 1)], sent.at[R_MMIX])
        expect(ranks * half + (ranks - 1) * half, sent.at[R_GOT + 2])


def exchange(smalls, state, moduli, tables, levels):
    groups, ranks = lax.axis_size("macro"), lax.axis_size("vox")
    rows = groups // ranks
    thickness = state.shape[2]
    half, extra, mix = rows // 2, min(levels - 1, 1), 1 if levels > 2 else 0
    nodes, corners, elements = smalls[0].shape[1], smalls[2].shape[0], smalls[2].shape[1]
    slab = (7, thickness, VOX_PLANE)
    hbm = pl.BlockSpec(memory_space=pltpu.HBM)
    f32 = jnp.float32
    kinds = 13 + levels
    cells = levels * VOX_SIDE * rows * VOX_PLANE
    tile = pltpu.VMEM((8, LANES), f32)
    return pl.pallas_call(
        functools.partial(exchange_kernel, levels),
        out_shape=[
            jax.ShapeDtypeStruct((3, nodes), f32),
            jax.ShapeDtypeStruct((levels * groups,) + slab, f32),
            jax.ShapeDtypeStruct((1, LANES), jnp.int32),
        ],
        in_specs=[hbm] * (len(smalls) + 2 + len(tables)),
        out_specs=[hbm] * 3,
        scratch_shapes=[
            pltpu.VMEM(state.shape, f32),
            pltpu.VMEM((max(ranks - 1, 1), rows) + slab, f32),
            pltpu.VMEM((ranks, rows) + slab, f32),
            pltpu.VMEM((ranks, rows) + slab, f32),
            pltpu.VMEM((groups if extra else 1,) + slab, f32),
            pltpu.VMEM((ranks, rows if extra else 1) + slab, f32),
            pltpu.VMEM((ranks, rows if extra else 1) + slab, f32),
            pltpu.VMEM((max(ranks - 1, 1), half if mix else 1) + slab, f32),
            pltpu.VMEM((groups // 2 if mix else 1,) + slab, f32),
            pltpu.VMEM((ranks, rows if mix else 1) + slab, f32),
            pltpu.VMEM((ranks, rows if mix else 1) + slab, f32),
            pltpu.VMEM((ranks,) + moduli.shape, f32),
            pltpu.VMEM(tables[0].shape, f32),
            pltpu.VMEM(tables[1].shape, tables[1].dtype),
            pltpu.VMEM((7, VOX_SIDE, rows, VOX_PLANE), f32),
            pltpu.VMEM((6, VOX_SIDE, rows, VOX_PLANE), f32),
            pltpu.VMEM((6, VOX_SIDE, rows, VOX_PLANE), f32),
            pltpu.VMEM((6, HALF + 1, rows, VOX_PLANE), f32),
            pltpu.VMEM((6, HALF - 1, rows, VOX_PLANE), f32),
            pltpu.VMEM((groups, 8, LANES), f32),
            pltpu.VMEM((groups, 8, LANES), f32),
            pltpu.VMEM((ranks, rows, LANES), f32),
            pltpu.VMEM((groups, 8, LANES), f32),
            pltpu.VMEM((ranks, rows, LANES), f32),
            pltpu.VMEM((groups // 2, 8, LANES), f32),
            pltpu.VMEM((2 * rows, 8, LANES), f32),
            pltpu.VMEM((levels * groups, LANES), f32),
            tile,
            tile,
            tile,
            tile,
            tile,
            pltpu.VMEM((LANES, LANES), f32),
            pltpu.VMEM((corners, LANES, elements), jnp.bfloat16),
            pltpu.VMEM((corners, 8, elements), f32),
            pltpu.VMEM((8, LANES), jnp.int32),
        ]
        + [pltpu.VMEM(small.shape, small.dtype) for small in smalls]
        + [
            pltpu.VMEM((1, LANES), jnp.int32),
            pltpu.SMEM((1, LANES), jnp.int32),
            pltpu.VMEM((1, LANES), jnp.int32),
            pltpu.VMEM((3, nodes), f32),
            pltpu.VMEM((ranks, 6) + moduli.shape[1:], f32),
            pltpu.SemaphoreType.DMA((14,)),
            pltpu.SemaphoreType.DMA((kinds,)),
            pltpu.SemaphoreType.DMA((kinds,)),
        ],
        compiler_params=pltpu.CompilerParams(
            collective_id=0, has_side_effects=True, vmem_limit_bytes=63 * 2**20
        ),
        cost_estimate=pl.CostEstimate(
            flops=SWEEPS * 2 * 3 * 2 * 6 * cells * VOX_PLANE,
            bytes_accessed=4 * 7 * cells * 4,
            transcendentals=SWEEPS * cells,
        ),
    )(*smalls, state, moduli, *tables)


def pick_kernel(order_hbm, got, residual, residual_out, moved, order_ref, held, load_sem, slot_sem, out_sem):
    count, slots = held.shape[0], got.shape[0]
    fetch = pltpu.make_async_copy(order_hbm, order_ref, load_sem.at[0])
    fetch.start()
    keep = pltpu.make_async_copy(residual, residual_out, load_sem.at[1])
    keep.start()
    fetch.wait()

    def take(j):
        slot = jnp.clip(order_ref[0, j], 0, slots - 1)
        return pltpu.make_async_copy(got.at[slot], held.at[j], slot_sem.at[j])

    for j in range(count):
        take(j).start()
    for j in range(count):
        drain(held.at[j], slot_sem.at[j])
        pltpu.make_async_copy(held.at[j], moved.at[:, j], out_sem).start()
    keep.wait()
    drain(held, out_sem)


def pick_rows(order, got, residual):
    slab = got.shape[1:]
    hbm = pl.BlockSpec(memory_space=pltpu.HBM)
    return pl.pallas_call(
        pick_kernel,
        out_shape=[
            jax.ShapeDtypeStruct(residual.shape, jnp.float32),
            jax.ShapeDtypeStruct(slab[:1] + (RECV_AGG,) + slab[1:], jnp.float32),
        ],
        in_specs=[hbm] * 3,
        out_specs=[hbm] * 2,
        scratch_shapes=[
            pltpu.SMEM(order.shape, jnp.int32),
            pltpu.VMEM((RECV_AGG,) + slab, jnp.float32),
            pltpu.SemaphoreType.DMA((2,)),
            pltpu.SemaphoreType.DMA((RECV_AGG,)),
            pltpu.SemaphoreType.DMA,
        ],
        compiler_params=pltpu.CompilerParams(vmem_limit_bytes=63 * 2**20),
    )(order, got, residual)


def local(
    displacement,
    load,
    conn,
    halo_list,
    grad_ops,
    volume,
    elastic_moduli,
    plastic_mask,
    new_owner,
    state,
    micro_moduli,
):
    groups = lax.axis_size("macro")
    tables = (jnp.asarray(green_tables()), plane_tables())
    levels = (PLASTIC_MAX + groups - 1) // groups
    assert levels <= 3 and groups // lax.axis_size("vox") == 2 * SWEEPS
    smalls = (
        displacement,
        load,
        conn,
        halo_list[None, :],
        grad_ops,
        volume[None, :],
        elastic_moduli,
        new_owner[None, :],
    )
    residual, got, order = exchange(smalls, state, micro_moduli, tables, levels)
    return tuple(pick_rows(order, got, residual))


def solution(mesh):
    return jax.shard_map(
        local,
        mesh=mesh,
        in_specs=(
            P(None, "macro"),
            P(None, "macro"),
            P(None, "macro"),
            P("macro"),
            P(None, None, "macro"),
            P("macro"),
            P(None, "macro"),
            P("macro"),
            P("macro"),
            P(None, "macro", "vox", None),
            P(None, "vox", None),
        ),
        out_specs=(P(None, "macro"), P(None, "macro", "vox", None)),
        check_vma=False,
    )
```

```python
import functools
import math

import jax
import jax.numpy as jnp
import numpy as np
from jax import lax
from jax.experimental import pallas as pl
from jax.experimental.pallas import tpu as pltpu
from jax.sharding import PartitionSpec as P

RECV_AGG = 24
PLASTIC_MAX = 48
VOX_SIDE = 16
VOX_PLANE = 256
SWEEPS = 4
HALF = VOX_SIDE // 2
LANES = 128

LAM_REF = 3.0
MU_REF = 3.0

ROOT = math.sqrt(0.5)
COS1 = math.cos(math.pi / 8)
COS3 = math.cos(3 * math.pi / 8)
PAIRS = [(i, j) for i in range(6) for j in range(i, 6)]


def green_tables():
    line = np.arange(VOX_SIDE)
    signed = np.where(line < HALF, line, line - VOX_SIDE).astype(np.float64)
    freq = np.stack(np.meshgrid(signed, signed, signed, indexing="ij"))
    norm = np.sum(freq * freq, axis=0)
    inverse = np.where(norm > 0, 1.0 / np.maximum(norm, 1.0), 0.0)
    coupling = (LAM_REF + MU_REF) / (LAM_REF + 2.0 * MU_REF)
    spots = [(0, 0), (1, 1), (2, 2), (1, 2), (0, 2), (0, 1)]
    table = np.zeros((6, 6) + norm.shape)
    for j, (a, b) in enumerate(spots):
        tau = np.zeros((3, 3))
        tau[a, b] = tau[b, a] = 1.0
        trac = np.einsum("ij,jxyz->ixyz", tau, freq)
        along = np.sum(freq * trac, axis=0) * inverse
        wave = (trac - coupling * along * freq) * inverse / MU_REF
        for i, (c, d) in enumerate(spots):
            table[i, j] = 0.5 * (freq[c] * wave[d] + freq[d] * wave[c])
    back = -line % VOX_SIDE
    flipped = table[:, :, back][:, :, :, back][:, :, :, :, back]
    even = 0.5 * (table + flipped) / VOX_SIDE**3
    even[:, 3:] *= 0.5
    stacked = np.stack([even[i, j] for i, j in PAIRS])
    return stacked.reshape(len(PAIRS), VOX_SIDE, VOX_PLANE).astype(np.float32)


def plane_tables():
    plane = np.arange(VOX_PLANE)
    rows, cols = plane // VOX_SIDE, plane % VOX_SIDE
    phase = (rows[:, None] * rows[None, :] + cols[:, None] * cols[None, :]) % VOX_SIDE
    angle = phase * (2.0 * math.pi / VOX_SIDE)
    plus = jnp.asarray((np.cos(angle) + np.sin(angle)).astype(np.float32))
    minus = jnp.asarray((np.cos(angle) - np.sin(angle)).astype(np.float32))
    out = []
    for table in (plus, minus):
        high = table.astype(jnp.bfloat16)
        out += [high, (table - high.astype(jnp.float32)).astype(jnp.bfloat16)]
    return jnp.stack(out)


def cosine_line(a):
    sums = [None] + [a[x] + a[8 - x] for x in (1, 2, 3)]
    diffs = [None] + [a[x] - a[8 - x] for x in (1, 2, 3)]
    even0, odd0 = a[0] + a[8], a[0] - a[8]
    outer, inner = even0 + a[4], even0 - a[4]
    spread = sums[1] + sums[3]
    slant = ROOT * (sums[1] - sums[3])
    mid = ROOT * diffs[2]
    first = COS1 * diffs[1] + COS3 * diffs[3]
    second = COS3 * diffs[1] - COS1 * diffs[3]
    top, low = odd0 + mid, odd0 - mid
    core = outer + sums[2]
    return [
        core + spread,
        top + first,
        inner + slant,
        low + second,
        outer - sums[2],
        low - second,
        inner - slant,
        top - first,
        core - spread,
    ]


def sine_line(b):
    sums = [None] + [b[x] + b[8 - x] for x in (1, 2, 3)]
    diffs = [None] + [b[x] - b[8 - x] for x in (1, 2, 3)]
    slant = ROOT * (diffs[1] + diffs[3])
    mid = ROOT * sums[2]
    first = COS3 * sums[1] + COS1 * sums[3]
    second = COS1 * sums[1] - COS3 * sums[3]
    return [
        None,
        (first + mid) + b[4],
        slant + diffs[2],
        (second + mid) - b[4],
        diffs[1] - diffs[3],
        (second - mid) + b[4],
        slant - diffs[2],
        (first - mid) - b[4],
    ]


def split_dot(block, table_ref, first):
    high = block.astype(jnp.bfloat16)
    low = (block - high.astype(jnp.float32)).astype(jnp.bfloat16)
    dot = functools.partial(jnp.dot, preferred_element_type=jnp.float32)
    return dot(high, table_ref[first]) + (dot(high, table_ref[first + 1]) + dot(low, table_ref[first]))


def prepare_law(props, laws):
    for h in range(props.shape[0]):
        lam, mu, yield_base, harden = [props[h, n] for n in range(4)]
        stiff_inv = 1.0 / (3.0 * mu + harden)
        laws[h, 0] = 2.0 * mu
        laws[h, 1] = lam + 2.0 * mu * (1.0 / 3.0)
        laws[h, 2] = yield_base * (0.5 / mu)
        laws[h, 3] = harden * (0.5 / mu)
        laws[h, 4] = stiff_inv
        laws[h, 5] = 3.0 * mu * stiff_inv


def voxel_law(strain, state, laws, row):
    two_mu, bulk, yield_base, harden, stiff_inv, soften = [laws[n, row, :] for n in range(6)]
    elastic = [strain[c] - state[c] for c in range(6)]
    trace = elastic[0] + elastic[1] + elastic[2]
    third = trace * (1.0 / 3.0)
    shape = [elastic[c] - third for c in range(3)] + elastic[3:]
    normal = shape[0] * shape[0] + shape[1] * shape[1] + shape[2] * shape[2]
    shear = shape[3] * shape[3] + shape[4] * shape[4] + shape[5] * shape[5]
    squared = jnp.maximum(1.5 * normal + 3.0 * shear, 1e-30)
    inverse = lax.rsqrt(squared)
    strength = yield_base + harden * state[6]
    share = jnp.maximum(1.0 - strength * inverse, 0.0)
    keep = two_mu * (1.0 - soften * share)
    pressure = bulk * trace
    stress = [pressure + keep * shape[c] for c in range(3)] + [keep * shape[c] for c in range(3, 6)]
    return stress, shape, (two_mu * stiff_inv) * share, squared * inverse


def solve_rows(pieces, strain, base, out, laws, green, plane, buffers, hook):
    stx, eps, work, cos_ref, sin_ref = buffers
    ranks, rows, _, thickness, _ = pieces.shape
    batch = math.gcd(thickness, 4)

    def bring(c, carry):
        for h in range(ranks):
            stx[c, h * thickness : (h + 1) * thickness] = jnp.swapaxes(pieces[h, :, c], 0, 1)
        return carry

    lax.fori_loop(0, 7, bring, 0)
    for c in range(6):
        eps[c] = jnp.broadcast_to(strain[:, base + c : base + c + 1][None], (VOX_SIDE, rows, VOX_PLANE))

    def sweep(step, carry):
        hook(step)
        for h in range(ranks):

            def law(step, inner, h=h):
                for part in range(batch):
                    place = step * batch + part
                    x = h * thickness + place
                    strain = [eps[c, x] for c in range(6)]
                    state = [stx[c, x] for c in range(7)]
                    stress = voxel_law(strain, state, laws.at[h], pl.ds(place, 1))[0]
                    for c in range(6):
                        work[c, x] = stress[c]
                return inner

            lax.fori_loop(0, thickness // batch, law, 0)

        def forward(c, inner):
            field = [work[c, x] for x in range(VOX_SIDE)]
            sums = [field[0]] + [field[x] + field[VOX_SIDE - x] for x in range(1, HALF)] + [field[HALF]]
            diffs = [None] + [field[x] - field[VOX_SIDE - x] for x in range(1, HALF)]
            for k, value in enumerate(cosine_line(sums)):
                cos_ref[c, k] = value
            for k, value in enumerate(sine_line(diffs)):
                if k > 0:
                    sin_ref[c, k - 1] = value
            return inner

        lax.fori_loop(0, 6, forward, 0)

        def transform():
            for ref, first in ((cos_ref, 0), (sin_ref, 2)):
                flat = ref[...].reshape(6 * ref.shape[1] * rows, VOX_PLANE)
                ref[...] = split_dot(flat, plane, first).reshape(ref.shape)

        def apply(field, k):
            row = pl.ds(k, 1)
            field = field[:3] + [2.0 * field[c] for c in range(3, 6)]
            total = [None] * 6
            for n, (i, j) in enumerate(PAIRS):
                entry = green[n, row, :]
                for a, b in [(i, j), (j, i)][: 1 + (i != j)]:
                    term = entry * field[b]
                    total[a] = term if total[a] is None else total[a] + term
            return total

        transform()
        for k in (0, HALF):
            result = apply([cos_ref[c, k] for c in range(6)], k)
            for c in range(6):
                cos_ref[c, k] = result[c]

        def mix(k, inner):
            even = [cos_ref[c, k] for c in range(6)]
            odd = [sin_ref[c, k - 1] for c in range(6)]
            ahead = apply([even[c] + odd[c] for c in range(6)], k)
            behind = apply([even[c] - odd[c] for c in range(6)], VOX_SIDE - k)
            for c in range(6):
                cos_ref[c, k] = ahead[c] + behind[c]
                sin_ref[c, k - 1] = ahead[c] - behind[c]
            return inner

        lax.fori_loop(1, HALF, mix, 0)
        transform()

        def backward(c, inner):
            even = cosine_line([cos_ref[c, k] for k in range(HALF + 1)])
            odd = sine_line([None] + [sin_ref[c, k - 1] for k in range(1, HALF)])
            eps[c, 0] = eps[c, 0] - even[0]
            eps[c, HALF] = eps[c, HALF] - even[HALF]
            for x in range(1, HALF):
                eps[c, x] = eps[c, x] - (even[x] + odd[x])
                eps[c, VOX_SIDE - x] = eps[c, VOX_SIDE - x] - (even[x] - odd[x])
            return inner

        lax.fori_loop(0, 6, backward, 0)
        return carry

    lax.fori_loop(0, SWEEPS, sweep, 0)
    totals = (jnp.zeros((rows, VOX_PLANE), jnp.float32),) * 6
    for h in range(ranks):

        def finish(place, totals, h=h):
            x = h * thickness + place
            strain = [eps[c, x] for c in range(6)]
            state = [stx[c, x] for c in range(7)]
            stress, shape, gain, size = voxel_law(strain, state, laws.at[h], pl.ds(place, 1))
            for c in range(6):
                stx[c, x] = state[c] + (1.5 * gain) * shape[c]
            stx[6, x] = state[6] + gain * size
            return tuple(totals[c] + stress[c] for c in range(6))

        totals = lax.fori_loop(0, thickness, finish, totals)

    def give(c, carry):
        for h in range(ranks):
            out[h, :, c] = jnp.swapaxes(stx[c, h * thickness : (h + 1) * thickness], 0, 1)
        return carry

    lax.fori_loop(0, 7, give, 0)
    lane = lax.broadcasted_iota(jnp.int32, (rows, LANES), 1)
    means = jnp.zeros((rows, LANES), jnp.float32)
    for c in range(6):
        total = jnp.sum(totals[c], axis=1, keepdims=True) / VOX_SIDE**3
        means = jnp.where(lane == c, total, means)
    return means


def drain(ref, sem):
    pltpu.make_async_copy(ref, ref, sem).wait()


def pieces_of(value):
    high = value.astype(jnp.bfloat16)
    rest = value - high.astype(jnp.float32)
    middle = rest.astype(jnp.bfloat16)
    low = (rest - middle.astype(jnp.float32)).astype(jnp.bfloat16)
    return high, middle, low


def select_dot(value, match, lanes):
    contract = (((1,), (1 if lanes else 0,)), ((), ()))
    parts = [
        lax.dot_general(piece, match, contract, preferred_element_type=jnp.float32)
        for piece in pieces_of(value)
    ]
    return parts[0] + (parts[1] + parts[2])


def count_up(shape, axis):
    return lax.broadcasted_iota(jnp.int32, shape, axis)


def to_column(row, size):
    spot = count_up((size, LANES), 0) == count_up((size, LANES), 1)
    return jnp.sum(jnp.where(spot, row, 0.0), axis=1, keepdims=True)


def exchange_kernel(levels, *refs):
    (disp_hbm, load_hbm, conn_hbm, halo_hbm, grad_hbm, volume_hbm, moduli_hbm, owner_hbm) = refs[:8]
    (state_hbm, props_hbm, green_hbm, plane_hbm) = refs[8:12]
    residual_out, got, order_out = refs[12:15]
    (st, trade_send, trade_recv, trade_new, raw_send, raw_recv, raw_new) = refs[15:22]
    (mix_trade, mix_send, mix_recv, mix_new, props, green, plane) = refs[22:29]
    buffers = refs[29:34]
    (note_send, note_recv, mean_src, mean_raw, mean_mix, mean_far, stage, mean_all) = refs[34:42]
    (halo_send, halo_recv, force_send, force_recv, mixed, strain_ref, onehot, forces, rows_i) = refs[42:51]
    (disp, load, conn, halo, grad, volume, moduli, owner) = refs[51:59]
    (source_vec, source_ref, order_vec, residual, laws, load_sem, recv, sent) = refs[59:]
    ranks, rows = trade_recv.shape[:2]
    groups, half = ranks * rows, rows // 2
    own_nodes, elements, halos = disp.shape[1], conn.shape[1], halo.shape[1]
    me, mine = lax.axis_index("macro"), lax.axis_index("vox")
    my_row, my_side = me // ranks, me % ranks
    raw_side = (mine + ranks * groups - me) % ranks
    my_odd, my_pair = my_row % 2, my_row // 2
    R_PROPS, R_NOTE, R_HALO, R_FORCE, R_TRADE, R_MEAN, R_RAW, R_MRAW, R_MIXT, R_MIX, R_MMIX, R_MFAR, R_GOT = range(13)
    f32 = jnp.float32

    def push(src, dst, kind, group, rank):
        pltpu.make_async_remote_copy(
            src_ref=src,
            dst_ref=dst,
            send_sem=sent.at[kind],
            recv_sem=recv.at[kind],
            device_id={"macro": group, "vox": rank},
            device_id_type=pl.DeviceIdType.MESH,
        ).start()

    def deliver(src, dst, kind, group, rank):
        here = (group == me) & (rank == mine)

        @pl.when(here)
        def _():
            pltpu.make_async_copy(src, dst, recv.at[kind]).start()

        @pl.when(jnp.logical_not(here))
        def _():
            push(src, dst, kind, group, rank)

    def settle(ref, kind, fewer):
        count = ref.shape[0]

        @pl.when(fewer)
        def _():
            drain(ref.at[pl.ds(0, count - 1)], sent.at[kind])

        @pl.when(jnp.logical_not(fewer))
        def _():
            drain(ref, sent.at[kind])

    def turn(step, count, block, spot):
        planes = count // block
        line, lane = spot // block, spot % block
        ring = step // block
        line = jnp.where(2 * line < planes, planes - 1 - ring, ring)
        return line * block + (lane + step) % block

    fetches = {}
    for n, (src, dst) in enumerate(
        (
            (owner_hbm, owner),
            (halo_hbm, halo),
            (disp_hbm, disp),
            (state_hbm, st),
            (conn_hbm, conn),
            (grad_hbm, grad),
            (props_hbm, props.at[mine]),
            (green_hbm, green),
            (plane_hbm, plane),
            (volume_hbm, volume),
            (moduli_hbm, moduli),
            (load_hbm, load),
        )
    ):
        fetches[n] = pltpu.make_async_copy(src, dst, load_sem.at[n])
        fetches[n].start()

    barrier = pltpu.get_barrier_semaphore()
    total = groups * ranks
    flat = me * ranks + mine

    def greet(k, carry):
        other = (flat + k) % total
        pl.semaphore_signal(
            barrier,
            inc=1,
            device_id={"macro": other // ranks, "vox": other % ranks},
            device_id_type=pl.DeviceIdType.MESH,
        )
        return carry

    lax.fori_loop(1, total, greet, 0)

    rows_i[...] = jnp.full(rows_i.shape, -1, jnp.int32)
    fetches[0].wait()
    rows_i[0:1, 0:elements] = owner[...]
    owner_row = rows_i[0:1, :].astype(f32)
    square = (LANES, LANES)
    owner_col = to_column(owner_row, LANES)
    before = count_up(square, 0) < count_up(square, 1)
    same = (owner_col == owner_row) & before
    rank_row = jnp.sum(jnp.where(same, 1.0, 0.0), axis=0, keepdims=True)
    slot_row = jnp.where(owner_row >= 0.0, rank_row * groups + owner_row, -1.0)
    slot_col = to_column(slot_row, LANES)
    hit = slot_col == count_up(square, 1).astype(f32)
    spots = jnp.where(hit, count_up(square, 0).astype(f32), 0.0)
    source_vec[...] = jnp.sum(spots, axis=0, keepdims=True).astype(jnp.int32)
    to_scalars = pltpu.make_async_copy(source_vec, source_ref, load_sem.at[12])
    to_scalars.start()

    fetches[1].wait()
    fetches[2].wait()
    rows_i[1:2, own_nodes : own_nodes + halos] = halo[...]
    halo_match = (count_up(square, 0) == rows_i[1:2, :]).astype(jnp.bfloat16)
    halo_send[...] = jnp.zeros(halo_send.shape, f32)
    halo_send[0:3, 0:own_nodes] = disp[...]
    own_disp = halo_send[...]
    halo_send[...] = select_dot(own_disp, halo_match, False)

    to_scalars.wait()
    fetches[3].wait()

    def slab_of(slot):
        return st[:, jnp.clip(source_ref[0, slot], 0, elements - 1)]

    def expect(count, sem):
        drain(got.at[pl.ds(0, count)], sem)

    def gather_trade(low, stride, start, here, away, turns):
        for o in turns:

            def gather(i, carry, o=o):
                slab = slab_of(low + ranks * (stride * i + start) + (mine + o) % ranks)
                if o == 0:
                    here[mine, i] = slab
                else:
                    away[o - 1, i] = slab
                return carry

            lax.fori_loop(0, away.shape[1], gather, 0)

    gather_trade(0, 1, 0, trade_recv, trade_send, range(1, ranks))
    if levels > 1:

        def gather_raw(d, carry):
            raw_send[d] = slab_of(groups + d)
            return carry

        lax.fori_loop(0, groups, gather_raw, 0)
    pl.semaphore_wait(barrier, total - 1)

    row_block = math.gcd(rows, 2)

    def side_of(o):
        side = (mine + o) % ranks
        return side, (side + ranks * groups - me) % ranks

    def send_raw(o):
        side, spot = side_of(o)

        def step(t, carry):
            d = ranks * turn(t, rows, row_block, my_row) + spot
            deliver(raw_send.at[d], raw_recv.at[mine, my_row], R_RAW, d, side)
            return carry

        lax.fori_loop(0, rows, step, 0)

    def send_mix(o):
        side, spot = side_of(o)

        def step(t, carry):
            u = turn(t, half, 1, my_pair)
            d = ranks * (2 * u + my_odd) + spot
            deliver(mix_send.at[u * ranks + spot], mix_recv.at[mine, half + my_pair], R_MIX, d, side)
            return carry

        lax.fori_loop(0, half, step, 0)

    push(halo_send, halo_recv, R_HALO, (me + 1) % groups, mine)
    for o in range(1, ranks):
        push(props_hbm, props.at[mine], R_PROPS, me, (mine + o) % ranks)
    for o in range(1, ranks):
        push(trade_send.at[o - 1], trade_recv.at[mine], R_TRADE, me, (mine + o) % ranks)
    if levels > 1:
        send_raw(0)
    gather_trade(0, 1, 0, trade_recv, trade_send, range(1))
    if levels > 2:
        gather_trade(2 * groups, 2, 1 - my_odd, mix_recv, mix_trade, range(ranks))

        def gather_mix(v, carry):
            mix_send[v] = slab_of(2 * groups + ranks * (2 * (v // ranks) + my_odd) + v % ranks)
            return carry

        lax.fori_loop(0, groups // 2, gather_mix, 0)

    fetches[4].wait()
    fetches[5].wait()
    tall = (LANES, elements)
    for a in range(conn.shape[0]):
        onehot[a] = (count_up(tall, 0) == conn[a : a + 1, :]).astype(jnp.bfloat16)
    drain(halo_recv, recv.at[R_HALO])
    lane8 = count_up((8, LANES), 1)
    near = jnp.where(lane8 < own_nodes, own_disp, halo_recv[...])
    products = [jnp.zeros((8, elements), f32) for _ in range(3)]
    for a in range(conn.shape[0]):
        moved = select_dot(near, onehot[a], False)
        for j in range(3):
            products[j] = products[j] + moved * grad[j, a : a + 1, :]
    strain_ref[...] = jnp.zeros(strain_ref.shape, f32)
    strain_rows = [
        products[0][0:1],
        products[1][1:2],
        products[2][2:3],
        0.5 * (products[2][1:2] + products[1][2:3]),
        0.5 * (products[2][0:1] + products[0][2:3]),
        0.5 * (products[1][0:1] + products[0][1:2]),
    ]
    for c in range(6):
        strain_ref[c : c + 1, 0:elements] = strain_rows[c]
    all_strain = strain_ref[...]

    def matched(ids):
        return ids.astype(f32) == slot_row

    wide = (groups, LANES)
    note = jnp.zeros(wide, f32)
    strain_pieces = pieces_of(all_strain)

    def strain_of(ids):
        match = jnp.where(matched(ids), 1.0, 0.0).astype(jnp.bfloat16)
        parts = [
            lax.dot_general(match, piece, (((1,), (1,)), ((), ())), preferred_element_type=f32)
            for piece in strain_pieces
        ]
        return parts[0] + (parts[1] + parts[2])

    for lv in range(1, levels):
        held = strain_of(count_up(wide, 0) + lv * groups)
        note = note + pltpu.roll(held, 16 * lv, 1)
    for lv in range(levels):
        held = jnp.where(matched(count_up(wide, 0) + lv * groups), 1.0, 0.0)
        note = jnp.where(count_up(wide, 1) == 8 + lv, jnp.sum(held, axis=1, keepdims=True), note)
    for d in range(groups):
        note_send[d] = note[d : d + 1, :]

    def send_note(t, carry):
        d = turn(t, groups, math.gcd(groups, 4), me)
        deliver(note_send.at[d], note_recv.at[my_side * rows + my_row], R_NOTE, d, mine)
        return carry

    lax.fori_loop(0, groups, send_note, 0)
    fetches[6].wait()
    fetches[7].wait()
    fetches[8].wait()
    if ranks > 1:
        drain(props.at[pl.ds(0, ranks - 1)], recv.at[R_PROPS])
    prepare_law(props, laws)

    def send_row(t, turns):
        i = turn(t, rows, row_block, my_row)
        for o in turns:
            h = (mine + o) % ranks
            deliver(trade_new.at[h, i], got.at[me], R_GOT, ranks * i + mine, h)

    def send_new(low, high, turns):
        def step(t, carry):
            send_row(t, turns)
            return carry

        lax.fori_loop(low, high, step, 0)

    def send_mixed(turns):
        def step(t, carry):
            u = turn(t, half, 1, my_pair)
            for o in turns:
                h = (mine + o) % ranks
                spot = ranks * (2 * u + 1 - my_odd) + mine
                push(mix_new.at[h, u], got.at[2 * groups + me], R_GOT + 2, spot, h)
            return carry

        lax.fori_loop(0, half, step, 0)

    def give_back(new, first, count, low, kind, stride, start):
        def step(i, carry):
            for o in range(ranks):
                h = (mine + o) % ranks
                giver = ranks * (stride * i + start) + raw_side
                deliver(new.at[h, first + i], got.at[low + giver], kind, me, h)
            return carry

        lax.fori_loop(0, count, step, 0)

    def send_means(means, first, count, dst, kind, stride, start):
        for i in range(count):
            stage[first + i if count < rows else rows + i] = means[first + i : first + i + 1, :]

        def step(t, carry):
            i = turn(t, count, math.gcd(count, 2), my_row * count // rows)
            for h in range(ranks):
                src = stage.at[first + i if count < rows else rows + i]
                deliver(src, dst, kind, ranks * (stride * i + start) + raw_side, h)
            return carry

        lax.fori_loop(0, count, step, 0)

    near, far = range(1), range(1, ranks)

    def trade_mix():
        for o in far:
            push(mix_trade.at[o - 1], mix_recv.at[mine, pl.ds(0, half)], R_MIXT, me, (mine + o) % ranks)

    def first_hook(step):
        if levels > 2:
            pl.when(step == SWEEPS - 2)(lambda: send_mix(0))
            pl.when(step == SWEEPS - 1)(trade_mix)

    def second_hook(step):
        if levels > 2:

            @pl.when(step >= SWEEPS - 2)
            def _():
                low = 2 * (step - (SWEEPS - 2))
                send_row(low, far)
                send_row(low + 1, far)

    def third_hook(step):
        @pl.when(step < SWEEPS // 2)
        def _():
            send_new(half * step, half * step + half, near)

    strain = strain_of(ranks * count_up((rows, LANES), 0) + mine)
    if ranks > 1:
        expect((ranks - 1) * rows, recv.at[R_TRADE])
    if levels > 1:
        for o in far:
            send_raw(o)
    means = solve_rows(trade_recv, strain, 0, trade_new, laws, green, plane, buffers, first_hook)
    mean_src[mine] = means
    for o in far:
        push(mean_src.at[mine], mean_src.at[mine], R_MEAN, me, (mine + o) % ranks)
    if levels == 1:
        send_new(0, rows, range(ranks))

    drain(note_recv, recv.at[R_NOTE])
    flags = note_recv[:, 0, :]
    spot = count_up(wide, 0)
    giver = (ranks * (spot % rows) + spot // rows).astype(f32)
    lane = count_up(wide, 1)
    counts = jnp.sum(jnp.where((lane >= 8) & (lane < 8 + levels), flags, 0.0), axis=1, keepdims=True)
    tall_count = jnp.sum(
        jnp.where(
            (count_up(wide, 0) == lane) & (lane < groups), jnp.broadcast_to(counts, wide), 0.0
        ),
        axis=0,
        keepdims=True,
    )
    lane_giver = (ranks * (lane % rows) + lane // rows).astype(f32)
    earlier = (lane_giver < giver) & (lane < groups)
    place = jnp.sum(jnp.where(earlier, tall_count, 0.0), axis=1, keepdims=True)
    picks = jnp.zeros((1, LANES), f32)
    for lv in range(levels):
        held = jnp.sum(jnp.where(lane == 8 + lv, flags, 0.0), axis=1, keepdims=True)
        chosen = (place == lane.astype(f32)) & (held > 0.5)
        picks = picks + jnp.sum(jnp.where(chosen, lv * groups + giver, 0.0), axis=0, keepdims=True)
        place = place + held
    order_vec[...] = picks.astype(jnp.int32)
    give_order = pltpu.make_async_copy(order_vec, order_out, load_sem.at[12])
    give_order.start()

    if levels > 1:
        expect(groups, recv.at[R_RAW])
        if levels > 2:
            for o in far:
                send_mix(o)
        strain = note_recv[pl.ds(raw_side * rows, rows), 0, :]
        means = solve_rows(raw_recv, strain, 16, raw_new, laws, green, plane, buffers, second_hook)
        send_means(means, 0, rows, mean_raw.at[me], R_MRAW, 1, 0)
        give_back(raw_new, 0, rows, groups, R_GOT + 1, 1, 0)
        if levels > 2:
            send_new(half, rows, far)
        else:
            send_new(0, rows, range(ranks))
    if levels > 2:
        mixed[...] = strain_of(2 * groups + ranks * (2 * count_up((8, LANES), 0) + 1 - my_odd) + mine)
        mixed[...] = pltpu.roll(mixed[...], 32, 1)
        for u in range(half):
            mixed[half + u : half + u + 1, :] = note_recv[raw_side * rows + 2 * u + my_odd][0:1, :]
        if ranks > 1:
            expect((ranks - 1) * half, recv.at[R_MIXT])
        expect(ranks * half, recv.at[R_MIX])
        means = solve_rows(mix_recv, mixed[0:rows, :], 32, mix_new, laws, green, plane, buffers, third_hook)
        mean_mix[mine] = means
        for o in far:
            push(mean_mix.at[mine], mean_mix.at[mine], R_MMIX, me, (mine + o) % ranks)
        send_means(means, half, half, mean_far.at[my_pair * ranks + my_side], R_MFAR, 2, my_odd)
        send_mixed(far)
        give_back(mix_new, half, half, 2 * groups, R_GOT + 2, 2, my_odd)
        send_mixed(near)
    fetches[9].wait()
    fetches[10].wait()
    fetches[11].wait()
    deep = (levels * groups, LANES)
    k = count_up(deep, 0)
    inside = k % groups
    known = ranks * (inside % rows) + inside // rows
    if ranks > 1:
        drain(mean_src.at[pl.ds(0, ranks - 1)], recv.at[R_MEAN])
    for y in range(ranks):
        mean_all[y * rows : (y + 1) * rows, :] = mean_src[y]
    if levels > 1:
        drain(mean_raw, recv.at[R_MRAW])
        mean_all[groups : 2 * groups, :] = mean_raw[:, 0, :]
        known = jnp.where(k < groups, known, k)
    if levels > 2:
        if ranks > 1:
            drain(mean_mix.at[pl.ds(0, ranks - 1)], recv.at[R_MMIX])
        drain(mean_far, recv.at[R_MFAR])
        middle = 2 * groups + groups // 2
        for y in range(ranks):
            low = 2 * groups + y * half
            mean_all[low : low + half, :] = mean_mix[y, 0:half, :]
        mean_all[middle:, :] = mean_far[:, 0, :]
        from_src = 2 * groups + ranks * (2 * (inside % half) + 1 - my_odd) + inside // half
        v = inside - groups // 2
        from_raw = 2 * groups + ranks * (2 * (v // ranks) + my_odd) + v % ranks
        known = jnp.where(k < 2 * groups, known, jnp.where(k < middle, from_src, from_raw))
    match = jnp.where(matched(known), 1.0, 0.0).astype(jnp.bfloat16)
    mean_t = jnp.transpose(mean_all[...])[0:8, :]
    averaged = select_dot(mean_t, match, False)[:, 0:elements]
    strain = all_strain[0:8, 0:elements]
    lame, shear = moduli[0:1, :], moduli[1:2, :]
    lateral = lame * (strain[0:1] + strain[1:2] + strain[2:3])
    plastic = owner[...] >= 0
    stress = []
    for c in range(6):
        plain = 2.0 * shear * strain[c : c + 1]
        plain = lateral + plain if c < 3 else plain
        stress.append(jnp.where(plastic, averaged[c : c + 1], plain))
    tensor = [[stress[0], stress[5], stress[4]], [stress[5], stress[1], stress[3]], [stress[4], stress[3], stress[2]]]
    forces[...] = jnp.zeros(forces.shape, f32)
    for i in range(3):
        force = volume[...] * (
            tensor[i][0] * grad[0] + tensor[i][1] * grad[1] + tensor[i][2] * grad[2]
        )
        for a in range(conn.shape[0]):
            forces[a, i : i + 1, :] = force[a : a + 1, :]
    assembled = jnp.zeros((8, LANES), f32)
    for a in range(conn.shape[0]):
        assembled = assembled + select_dot(forces[a], onehot[a], True)
    force_send[...] = assembled
    push(force_send, force_recv, R_FORCE, (me + groups - 1) % groups, mine)
    drain(force_recv, recv.at[R_FORCE])
    lane8 = count_up((8, LANES), 1)
    beyond = (lane8 >= own_nodes) & (lane8 < own_nodes + halos)
    back = jnp.where(beyond, force_recv[...], 0.0)
    total_force = assembled + select_dot(back, halo_match, True)
    residual[...] = total_force[0:3, 0:own_nodes] - load[...]
    give_residual = pltpu.make_async_copy(residual, residual_out, load_sem.at[13])
    give_residual.start()

    for lv in range(levels):
        drain(got.at[pl.ds(lv * groups, groups)], recv.at[R_GOT + lv])
    give_order.wait()
    give_residual.wait()
    drain(note_send.at[pl.ds(0, groups - 1)], sent.at[R_NOTE])
    drain(halo_send, sent.at[R_HALO])
    drain(force_send, sent.at[R_FORCE])
    if ranks > 1:
        drain(props.at[pl.ds(0, ranks - 1)], sent.at[R_PROPS])
    if ranks > 1:
        drain(trade_send, sent.at[R_TRADE])
        drain(mean_src.at[pl.ds(0, ranks - 1)], sent.at[R_MEAN])
    settle(got.at[pl.ds(0, groups)], R_GOT, my_side == mine)
    own = (2 * me) % ranks == mine
    if levels > 1:
        settle(raw_send, R_RAW, own)
        settle(mean_raw, R_MRAW, own)
        if ranks > 1:
            expect((ranks - 1) * rows, sent.at[R_GOT + 1])
    if levels > 2:
        settle(mix_send, R_MIX, own)
        settle(mean_far, R_MFAR, own)
        if ranks > 1:
            drain(mix_trade, sent.at[R_MIXT])
            drain(mean_mix.at[pl.ds(0, ranks - 1)], sent.at[R_MMIX])
        expect(ranks * half + (ranks - 1) * half, sent.at[R_GOT + 2])


def exchange(smalls, state, moduli, tables, levels):
    groups, ranks = lax.axis_size("macro"), lax.axis_size("vox")
    rows = groups // ranks
    thickness = state.shape[2]
    half, extra, mix = rows // 2, min(levels - 1, 1), 1 if levels > 2 else 0
    nodes, corners, elements = smalls[0].shape[1], smalls[2].shape[0], smalls[2].shape[1]
    slab = (7, thickness, VOX_PLANE)
    hbm = pl.BlockSpec(memory_space=pltpu.HBM)
    f32 = jnp.float32
    kinds = 13 + levels
    cells = levels * VOX_SIDE * rows * VOX_PLANE
    tile = pltpu.VMEM((8, LANES), f32)
    return pl.pallas_call(
        functools.partial(exchange_kernel, levels),
        out_shape=[
            jax.ShapeDtypeStruct((3, nodes), f32),
            jax.ShapeDtypeStruct((levels * groups,) + slab, f32),
            jax.ShapeDtypeStruct((1, LANES), jnp.int32),
        ],
        in_specs=[hbm] * (len(smalls) + 2 + len(tables)),
        out_specs=[hbm] * 3,
        scratch_shapes=[
            pltpu.VMEM(state.shape, f32),
            pltpu.VMEM((max(ranks - 1, 1), rows) + slab, f32),
            pltpu.VMEM((ranks, rows) + slab, f32),
            pltpu.VMEM((ranks, rows) + slab, f32),
            pltpu.VMEM((groups if extra else 1,) + slab, f32),
            pltpu.VMEM((ranks, rows if extra else 1) + slab, f32),
            pltpu.VMEM((ranks, rows if extra else 1) + slab, f32),
            pltpu.VMEM((max(ranks - 1, 1), half if mix else 1) + slab, f32),
            pltpu.VMEM((groups // 2 if mix else 1,) + slab, f32),
            pltpu.VMEM((ranks, rows if mix else 1) + slab, f32),
            pltpu.VMEM((ranks, rows if mix else 1) + slab, f32),
            pltpu.VMEM((ranks,) + moduli.shape, f32),
            pltpu.VMEM(tables[0].shape, f32),
            pltpu.VMEM(tables[1].shape, tables[1].dtype),
            pltpu.VMEM((7, VOX_SIDE, rows, VOX_PLANE), f32),
            pltpu.VMEM((6, VOX_SIDE, rows, VOX_PLANE), f32),
            pltpu.VMEM((6, VOX_SIDE, rows, VOX_PLANE), f32),
            pltpu.VMEM((6, HALF + 1, rows, VOX_PLANE), f32),
            pltpu.VMEM((6, HALF - 1, rows, VOX_PLANE), f32),
            pltpu.VMEM((groups, 1, LANES), f32),
            pltpu.VMEM((groups, 1, LANES), f32),
            pltpu.VMEM((ranks, rows, LANES), f32),
            pltpu.VMEM((groups, 1, LANES), f32),
            pltpu.VMEM((ranks, rows, LANES), f32),
            pltpu.VMEM((groups // 2, 1, LANES), f32),
            pltpu.VMEM((2 * rows, 1, LANES), f32),
            pltpu.VMEM((levels * groups, LANES), f32),
            tile,
            tile,
            tile,
            tile,
            tile,
            pltpu.VMEM((LANES, LANES), f32),
            pltpu.VMEM((corners, LANES, elements), jnp.bfloat16),
            pltpu.VMEM((corners, 8, elements), f32),
            pltpu.VMEM((8, LANES), jnp.int32),
        ]
        + [pltpu.VMEM(small.shape, small.dtype) for small in smalls]
        + [
            pltpu.VMEM((1, LANES), jnp.int32),
            pltpu.SMEM((1, LANES), jnp.int32),
            pltpu.VMEM((1, LANES), jnp.int32),
            pltpu.VMEM((3, nodes), f32),
            pltpu.VMEM((ranks, 6) + moduli.shape[1:], f32),
            pltpu.SemaphoreType.DMA((14,)),
            pltpu.SemaphoreType.DMA((kinds,)),
            pltpu.SemaphoreType.DMA((kinds,)),
        ],
        compiler_params=pltpu.CompilerParams(
            collective_id=0, has_side_effects=True, vmem_limit_bytes=63 * 2**20
        ),
        cost_estimate=pl.CostEstimate(
            flops=SWEEPS * 2 * 3 * 2 * 6 * cells * VOX_PLANE,
            bytes_accessed=4 * 7 * cells * 4,
            transcendentals=SWEEPS * cells,
        ),
    )(*smalls, state, moduli, *tables)


def pick_kernel(order_hbm, got, residual, residual_out, moved, order_ref, held, load_sem, slot_sem, out_sem):
    count, slots = held.shape[0], got.shape[0]
    fetch = pltpu.make_async_copy(order_hbm, order_ref, load_sem.at[0])
    fetch.start()
    keep = pltpu.make_async_copy(residual, residual_out, load_sem.at[1])
    keep.start()
    fetch.wait()

    def take(j):
        slot = jnp.clip(order_ref[0, j], 0, slots - 1)
        return pltpu.make_async_copy(got.at[slot], held.at[j], slot_sem.at[j])

    for j in range(count):
        take(j).start()
    for j in range(count):
        drain(held.at[j], slot_sem.at[j])
        pltpu.make_async_copy(held.at[j], moved.at[:, j], out_sem).start()
    keep.wait()
    drain(held, out_sem)


def pick_rows(order, got, residual):
    slab = got.shape[1:]
    hbm = pl.BlockSpec(memory_space=pltpu.HBM)
    return pl.pallas_call(
        pick_kernel,
        out_shape=[
            jax.ShapeDtypeStruct(residual.shape, jnp.float32),
            jax.ShapeDtypeStruct(slab[:1] + (RECV_AGG,) + slab[1:], jnp.float32),
        ],
        in_specs=[hbm] * 3,
        out_specs=[hbm] * 2,
        scratch_shapes=[
            pltpu.SMEM(order.shape, jnp.int32),
            pltpu.VMEM((RECV_AGG,) + slab, jnp.float32),
            pltpu.SemaphoreType.DMA((2,)),
            pltpu.SemaphoreType.DMA((RECV_AGG,)),
            pltpu.SemaphoreType.DMA,
        ],
        compiler_params=pltpu.CompilerParams(vmem_limit_bytes=63 * 2**20),
    )(order, got, residual)


def local(
    displacement,
    load,
    conn,
    halo_list,
    grad_ops,
    volume,
    elastic_moduli,
    plastic_mask,
    new_owner,
    state,
    micro_moduli,
):
    groups = lax.axis_size("macro")
    tables = (jnp.asarray(green_tables()), plane_tables())
    levels = (PLASTIC_MAX + groups - 1) // groups
    assert levels <= 3 and groups // lax.axis_size("vox") == 2 * SWEEPS
    smalls = (
        displacement,
        load,
        conn,
        halo_list[None, :],
        grad_ops,
        volume[None, :],
        elastic_moduli,
        new_owner[None, :],
    )
    residual, got, order = exchange(smalls, state, micro_moduli, tables, levels)
    return tuple(pick_rows(order, got, residual))


def solution(mesh):
    return jax.shard_map(
        local,
        mesh=mesh,
        in_specs=(
            P(None, "macro"),
            P(None, "macro"),
            P(None, "macro"),
            P("macro"),
            P(None, None, "macro"),
            P("macro"),
            P(None, "macro"),
            P("macro"),
            P("macro"),
            P(None, "macro", "vox", None),
            P(None, "vox", None),
        ),
        out_specs=(P(None, "macro"), P(None, "macro", "vox", None)),
        check_vma=False,
    )
```

```python
import functools
import math

import jax
import jax.numpy as jnp
import numpy as np
from jax import lax
from jax.experimental import pallas as pl
from jax.experimental.pallas import tpu as pltpu
from jax.sharding import PartitionSpec as P

RECV_AGG = 24
PLASTIC_MAX = 48
VOX_SIDE = 16
VOX_PLANE = 256
SWEEPS = 4
HALF = VOX_SIDE // 2
LANES = 128

LAM_REF = 3.0
MU_REF = 3.0

ROOT = math.sqrt(0.5)
COS1 = math.cos(math.pi / 8)
COS3 = math.cos(3 * math.pi / 8)
PAIRS = [(i, j) for i in range(6) for j in range(i, 6)]


def green_tables():
    line = np.arange(VOX_SIDE)
    signed = np.where(line < HALF, line, line - VOX_SIDE).astype(np.float64)
    freq = np.stack(np.meshgrid(signed, signed, signed, indexing="ij"))
    norm = np.sum(freq * freq, axis=0)
    inverse = np.where(norm > 0, 1.0 / np.maximum(norm, 1.0), 0.0)
    coupling = (LAM_REF + MU_REF) / (LAM_REF + 2.0 * MU_REF)
    spots = [(0, 0), (1, 1), (2, 2), (1, 2), (0, 2), (0, 1)]
    table = np.zeros((6, 6) + norm.shape)
    for j, (a, b) in enumerate(spots):
        tau = np.zeros((3, 3))
        tau[a, b] = tau[b, a] = 1.0
        trac = np.einsum("ij,jxyz->ixyz", tau, freq)
        along = np.sum(freq * trac, axis=0) * inverse
        wave = (trac - coupling * along * freq) * inverse / MU_REF
        for i, (c, d) in enumerate(spots):
            table[i, j] = 0.5 * (freq[c] * wave[d] + freq[d] * wave[c])
    back = -line % VOX_SIDE
    flipped = table[:, :, back][:, :, :, back][:, :, :, :, back]
    even = 0.5 * (table + flipped) / VOX_SIDE**3
    even[:, 3:] *= 0.5
    stacked = np.stack([even[i, j] for i, j in PAIRS])
    return stacked.reshape(len(PAIRS), VOX_SIDE, VOX_PLANE).astype(np.float32)


def plane_tables():
    plane = np.arange(VOX_PLANE)
    rows, cols = plane // VOX_SIDE, plane % VOX_SIDE
    phase = (rows[:, None] * rows[None, :] + cols[:, None] * cols[None, :]) % VOX_SIDE
    angle = phase * (2.0 * math.pi / VOX_SIDE)
    plus = jnp.asarray((np.cos(angle) + np.sin(angle)).astype(np.float32))
    minus = jnp.asarray((np.cos(angle) - np.sin(angle)).astype(np.float32))
    out = []
    for table in (plus, minus):
        high = table.astype(jnp.bfloat16)
        out += [high, (table - high.astype(jnp.float32)).astype(jnp.bfloat16)]
    return jnp.stack(out)


def cosine_line(a):
    sums = [None] + [a[x] + a[8 - x] for x in (1, 2, 3)]
    diffs = [None] + [a[x] - a[8 - x] for x in (1, 2, 3)]
    even0, odd0 = a[0] + a[8], a[0] - a[8]
    outer, inner = even0 + a[4], even0 - a[4]
    spread = sums[1] + sums[3]
    slant = ROOT * (sums[1] - sums[3])
    mid = ROOT * diffs[2]
    first = COS1 * diffs[1] + COS3 * diffs[3]
    second = COS3 * diffs[1] - COS1 * diffs[3]
    top, low = odd0 + mid, odd0 - mid
    core = outer + sums[2]
    return [
        core + spread,
        top + first,
        inner + slant,
        low + second,
        outer - sums[2],
        low - second,
        inner - slant,
        top - first,
        core - spread,
    ]


def sine_line(b):
    sums = [None] + [b[x] + b[8 - x] for x in (1, 2, 3)]
    diffs = [None] + [b[x] - b[8 - x] for x in (1, 2, 3)]
    slant = ROOT * (diffs[1] + diffs[3])
    mid = ROOT * sums[2]
    first = COS3 * sums[1] + COS1 * sums[3]
    second = COS1 * sums[1] - COS3 * sums[3]
    return [
        None,
        (first + mid) + b[4],
        slant + diffs[2],
        (second + mid) - b[4],
        diffs[1] - diffs[3],
        (second - mid) + b[4],
        slant - diffs[2],
        (first - mid) - b[4],
    ]


def split_dot(block, table_ref, first):
    high = block.astype(jnp.bfloat16)
    low = (block - high.astype(jnp.float32)).astype(jnp.bfloat16)
    dot = functools.partial(jnp.dot, preferred_element_type=jnp.float32)
    return dot(high, table_ref[first]) + (dot(high, table_ref[first + 1]) + dot(low, table_ref[first]))


def prepare_law(props, laws):
    for h in range(props.shape[0]):
        lam, mu, yield_base, harden = [props[h, n] for n in range(4)]
        stiff_inv = 1.0 / (3.0 * mu + harden)
        laws[h, 0] = 2.0 * mu
        laws[h, 1] = lam + 2.0 * mu * (1.0 / 3.0)
        laws[h, 2] = yield_base * (0.5 / mu)
        laws[h, 3] = harden * (0.5 / mu)
        laws[h, 4] = stiff_inv
        laws[h, 5] = 3.0 * mu * stiff_inv


def voxel_law(strain, state, laws, row):
    two_mu, bulk, yield_base, harden, stiff_inv, soften = [laws[n, row, :] for n in range(6)]
    elastic = [strain[c] - state[c] for c in range(6)]
    trace = elastic[0] + elastic[1] + elastic[2]
    third = trace * (1.0 / 3.0)
    shape = [elastic[c] - third for c in range(3)] + elastic[3:]
    normal = shape[0] * shape[0] + shape[1] * shape[1] + shape[2] * shape[2]
    shear = shape[3] * shape[3] + shape[4] * shape[4] + shape[5] * shape[5]
    squared = jnp.maximum(1.5 * normal + 3.0 * shear, 1e-30)
    inverse = lax.rsqrt(squared)
    strength = yield_base + harden * state[6]
    share = jnp.maximum(1.0 - strength * inverse, 0.0)
    keep = two_mu * (1.0 - soften * share)
    pressure = bulk * trace
    stress = [pressure + keep * shape[c] for c in range(3)] + [keep * shape[c] for c in range(3, 6)]
    return stress, shape, (two_mu * stiff_inv) * share, squared * inverse


def solve_rows(pieces, strain, base, out, laws, green, plane, buffers, hook):
    stx, eps, work, cos_ref, sin_ref = buffers
    ranks, rows, _, thickness, _ = pieces.shape
    batch = math.gcd(thickness, 4)

    def bring(c, carry):
        for h in range(ranks):
            stx[c, h * thickness : (h + 1) * thickness] = jnp.swapaxes(pieces[h, :, c], 0, 1)
        return carry

    lax.fori_loop(0, 7, bring, 0)
    for c in range(6):
        eps[c] = jnp.broadcast_to(strain[:, base + c : base + c + 1][None], (VOX_SIDE, rows, VOX_PLANE))

    def sweep(step, carry):
        hook(step)
        for h in range(ranks):

            def law(step, inner, h=h):
                for part in range(batch):
                    place = step * batch + part
                    x = h * thickness + place
                    strain = [eps[c, x] for c in range(6)]
                    state = [stx[c, x] for c in range(7)]
                    stress = voxel_law(strain, state, laws.at[h], pl.ds(place, 1))[0]
                    for c in range(6):
                        work[c, x] = stress[c]
                return inner

            lax.fori_loop(0, thickness // batch, law, 0)

        def forward(c, inner):
            field = [work[c, x] for x in range(VOX_SIDE)]
            sums = [field[0]] + [field[x] + field[VOX_SIDE - x] for x in range(1, HALF)] + [field[HALF]]
            diffs = [None] + [field[x] - field[VOX_SIDE - x] for x in range(1, HALF)]
            for k, value in enumerate(cosine_line(sums)):
                cos_ref[c, k] = value
            for k, value in enumerate(sine_line(diffs)):
                if k > 0:
                    sin_ref[c, k - 1] = value
            return inner

        lax.fori_loop(0, 6, forward, 0)

        def transform():
            for ref, first in ((cos_ref, 0), (sin_ref, 2)):
                flat = ref[...].reshape(6 * ref.shape[1] * rows, VOX_PLANE)
                ref[...] = split_dot(flat, plane, first).reshape(ref.shape)

        def apply(field, k):
            row = pl.ds(k, 1)
            field = field[:3] + [2.0 * field[c] for c in range(3, 6)]
            total = [None] * 6
            for n, (i, j) in enumerate(PAIRS):
                entry = green[n, row, :]
                for a, b in [(i, j), (j, i)][: 1 + (i != j)]:
                    term = entry * field[b]
                    total[a] = term if total[a] is None else total[a] + term
            return total

        transform()
        for k in (0, HALF):
            result = apply([cos_ref[c, k] for c in range(6)], k)
            for c in range(6):
                cos_ref[c, k] = result[c]

        def mix(k, inner):
            even = [cos_ref[c, k] for c in range(6)]
            odd = [sin_ref[c, k - 1] for c in range(6)]
            ahead = apply([even[c] + odd[c] for c in range(6)], k)
            behind = apply([even[c] - odd[c] for c in range(6)], VOX_SIDE - k)
            for c in range(6):
                cos_ref[c, k] = ahead[c] + behind[c]
                sin_ref[c, k - 1] = ahead[c] - behind[c]
            return inner

        lax.fori_loop(1, HALF, mix, 0)
        transform()

        def backward(c, inner):
            even = cosine_line([cos_ref[c, k] for k in range(HALF + 1)])
            odd = sine_line([None] + [sin_ref[c, k - 1] for k in range(1, HALF)])
            eps[c, 0] = eps[c, 0] - even[0]
            eps[c, HALF] = eps[c, HALF] - even[HALF]
            for x in range(1, HALF):
                eps[c, x] = eps[c, x] - (even[x] + odd[x])
                eps[c, VOX_SIDE - x] = eps[c, VOX_SIDE - x] - (even[x] - odd[x])
            return inner

        lax.fori_loop(0, 6, backward, 0)
        return carry

    lax.fori_loop(0, SWEEPS, sweep, 0)
    totals = (jnp.zeros((rows, VOX_PLANE), jnp.float32),) * 6
    for h in range(ranks):

        def finish(place, totals, h=h):
            x = h * thickness + place
            strain = [eps[c, x] for c in range(6)]
            state = [stx[c, x] for c in range(7)]
            stress, shape, gain, size = voxel_law(strain, state, laws.at[h], pl.ds(place, 1))
            for c in range(6):
                stx[c, x] = state[c] + (1.5 * gain) * shape[c]
            stx[6, x] = state[6] + gain * size
            return tuple(totals[c] + stress[c] for c in range(6))

        totals = lax.fori_loop(0, thickness, finish, totals)

    def give(c, carry):
        for h in range(ranks):
            out[h, :, c] = jnp.swapaxes(stx[c, h * thickness : (h + 1) * thickness], 0, 1)
        return carry

    lax.fori_loop(0, 7, give, 0)
    lane = lax.broadcasted_iota(jnp.int32, (rows, LANES), 1)
    means = jnp.zeros((rows, LANES), jnp.float32)
    for c in range(6):
        total = jnp.sum(totals[c], axis=1, keepdims=True) / VOX_SIDE**3
        means = jnp.where(lane == c, total, means)
    return means


def drain(ref, sem):
    pltpu.make_async_copy(ref, ref, sem).wait()


def pieces_of(value):
    high = value.astype(jnp.bfloat16)
    rest = value - high.astype(jnp.float32)
    middle = rest.astype(jnp.bfloat16)
    low = (rest - middle.astype(jnp.float32)).astype(jnp.bfloat16)
    return high, middle, low


def select_dot(value, match, lanes):
    contract = (((1,), (1 if lanes else 0,)), ((), ()))
    parts = [
        lax.dot_general(piece, match, contract, preferred_element_type=jnp.float32)
        for piece in pieces_of(value)
    ]
    return parts[0] + (parts[1] + parts[2])


def count_up(shape, axis):
    return lax.broadcasted_iota(jnp.int32, shape, axis)


def to_column(row, size):
    spot = count_up((size, LANES), 0) == count_up((size, LANES), 1)
    return jnp.sum(jnp.where(spot, row, 0.0), axis=1, keepdims=True)


def exchange_kernel(levels, *refs):
    (disp_hbm, load_hbm, conn_hbm, halo_hbm, grad_hbm, volume_hbm, moduli_hbm, owner_hbm) = refs[:8]
    (state_hbm, props_hbm, green_hbm, plane_hbm) = refs[8:12]
    residual_out, got, order_out = refs[12:15]
    (st, trade_send, trade_recv, trade_new, raw_send, raw_recv, raw_new) = refs[15:22]
    (mix_trade, mix_send, mix_recv, mix_new, props, green, plane) = refs[22:29]
    buffers = refs[29:34]
    (note_send, note_recv, mean_src, mean_raw, mean_mix, mean_far, stage, mean_all) = refs[34:42]
    (halo_send, halo_recv, force_send, force_recv, mixed, strain_ref, onehot, forces, rows_i) = refs[42:51]
    (disp, load, conn, halo, grad, volume, moduli, owner) = refs[51:59]
    (source_vec, source_ref, order_vec, residual, laws, load_sem, recv, sent) = refs[59:]
    ranks, rows = trade_recv.shape[:2]
    groups, half = ranks * rows, rows // 2
    own_nodes, elements, halos = disp.shape[1], conn.shape[1], halo.shape[1]
    me, mine = lax.axis_index("macro"), lax.axis_index("vox")
    my_row, my_side = me // ranks, me % ranks
    raw_side = (mine + ranks * groups - me) % ranks
    my_odd, my_pair = my_row % 2, my_row // 2
    R_PROPS, R_NOTE, R_HALO, R_FORCE, R_TRADE, R_MEAN, R_RAW, R_MRAW, R_MIXT, R_MIX, R_MMIX, R_MFAR, R_GOT = range(13)
    f32 = jnp.float32

    def push(src, dst, kind, group, rank):
        pltpu.make_async_remote_copy(
            src_ref=src,
            dst_ref=dst,
            send_sem=sent.at[kind],
            recv_sem=recv.at[kind],
            device_id={"macro": group, "vox": rank},
            device_id_type=pl.DeviceIdType.MESH,
        ).start()

    def deliver(src, dst, kind, group, rank):
        here = (group == me) & (rank == mine)

        @pl.when(here)
        def _():
            pltpu.make_async_copy(src, dst, recv.at[kind]).start()

        @pl.when(jnp.logical_not(here))
        def _():
            push(src, dst, kind, group, rank)

    def settle(ref, kind, fewer):
        count = ref.shape[0]

        @pl.when(fewer)
        def _():
            drain(ref.at[pl.ds(0, count - 1)], sent.at[kind])

        @pl.when(jnp.logical_not(fewer))
        def _():
            drain(ref, sent.at[kind])

    def turn(step, count, block, spot):
        planes = count // block
        line, lane = spot // block, spot % block
        ring = step // block
        line = jnp.where(2 * line < planes, planes - 1 - ring, ring)
        return line * block + (lane + step) % block

    pltpu.make_async_copy(state_hbm, st, load_sem.at[3]).start()
    barrier = pltpu.get_barrier_semaphore()
    total = groups * ranks
    flat = me * ranks + mine

    def greet(k, carry):
        other = (flat + 1 + (k + total // 2) % (total - 1)) % total
        pl.semaphore_signal(
            barrier,
            inc=1,
            device_id={"macro": other // ranks, "vox": other % ranks},
            device_id_type=pl.DeviceIdType.MESH,
        )
        return carry

    lax.fori_loop(0, total - 1, greet, 0)

    fetches = {}
    for n, (src, dst) in enumerate(
        (
            (owner_hbm, owner),
            (halo_hbm, halo),
            (disp_hbm, disp),
            (state_hbm, st),
            (conn_hbm, conn),
            (grad_hbm, grad),
            (props_hbm, props.at[mine]),
            (green_hbm, green),
            (plane_hbm, plane),
            (volume_hbm, volume),
            (moduli_hbm, moduli),
            (load_hbm, load),
        )
    ):
        fetches[n] = pltpu.make_async_copy(src, dst, load_sem.at[n])
        if n != 3:
            fetches[n].start()


    rows_i[...] = jnp.full(rows_i.shape, -1, jnp.int32)
    fetches[0].wait()
    rows_i[0:1, 0:elements] = owner[...]
    owner_row = rows_i[0:1, :].astype(f32)
    square = (LANES, LANES)
    owner_col = to_column(owner_row, LANES)
    before = count_up(square, 0) < count_up(square, 1)
    same = (owner_col == owner_row) & before
    rank_row = jnp.sum(jnp.where(same, 1.0, 0.0), axis=0, keepdims=True)
    slot_row = jnp.where(owner_row >= 0.0, rank_row * groups + owner_row, -1.0)
    slot_col = to_column(slot_row, LANES)
    hit = slot_col == count_up(square, 1).astype(f32)
    spots = jnp.where(hit, count_up(square, 0).astype(f32), 0.0)
    source_vec[...] = jnp.sum(spots, axis=0, keepdims=True).astype(jnp.int32)
    to_scalars = pltpu.make_async_copy(source_vec, source_ref, load_sem.at[12])
    to_scalars.start()

    fetches[1].wait()
    fetches[2].wait()
    rows_i[1:2, own_nodes : own_nodes + halos] = halo[...]
    halo_match = (count_up(square, 0) == rows_i[1:2, :]).astype(jnp.bfloat16)
    halo_send[...] = jnp.zeros(halo_send.shape, f32)
    halo_send[0:3, 0:own_nodes] = disp[...]
    own_disp = halo_send[...]
    halo_send[...] = select_dot(own_disp, halo_match, False)

    to_scalars.wait()
    fetches[3].wait()

    def slab_of(slot):
        return st[:, jnp.clip(source_ref[0, slot], 0, elements - 1)]

    def expect(count, sem):
        drain(got.at[pl.ds(0, count)], sem)

    def gather_trade(low, stride, start, here, away, turns):
        for o in turns:

            def gather(i, carry, o=o):
                slab = slab_of(low + ranks * (stride * i + start) + (mine + o) % ranks)
                if o == 0:
                    here[mine, i] = slab
                else:
                    away[o - 1, i] = slab
                return carry

            lax.fori_loop(0, away.shape[1], gather, 0)

    gather_trade(0, 1, 0, trade_recv, trade_send, range(1, ranks))
    if levels > 1:

        def gather_raw(d, carry):
            raw_send[d] = slab_of(groups + d)
            return carry

        lax.fori_loop(0, groups, gather_raw, 0)
    pl.semaphore_wait(barrier, total - 1)

    row_block = math.gcd(rows, 2)

    def side_of(o):
        side = (mine + o) % ranks
        return side, (side + ranks * groups - me) % ranks

    def send_raw(o):
        side, spot = side_of(o)

        def step(t, carry):
            d = ranks * turn(t, rows, row_block, my_row) + spot
            deliver(raw_send.at[d], raw_recv.at[mine, my_row], R_RAW, d, side)
            return carry

        lax.fori_loop(0, rows, step, 0)

    def send_mix(o):
        side, spot = side_of(o)

        def step(t, carry):
            u = turn(t, half, 1, my_pair)
            d = ranks * (2 * u + my_odd) + spot
            deliver(mix_send.at[u * ranks + spot], mix_recv.at[mine, half + my_pair], R_MIX, d, side)
            return carry

        lax.fori_loop(0, half, step, 0)

    push(halo_send, halo_recv, R_HALO, (me + 1) % groups, mine)
    for o in range(1, ranks):
        push(props_hbm, props.at[mine], R_PROPS, me, (mine + o) % ranks)
    for o in range(1, ranks):
        push(trade_send.at[o - 1], trade_recv.at[mine], R_TRADE, me, (mine + o) % ranks)
    if levels > 1:
        send_raw(0)
    gather_trade(0, 1, 0, trade_recv, trade_send, range(1))
    if levels > 2:
        gather_trade(2 * groups, 2, 1 - my_odd, mix_recv, mix_trade, range(ranks))

        def gather_mix(v, carry):
            mix_send[v] = slab_of(2 * groups + ranks * (2 * (v // ranks) + my_odd) + v % ranks)
            return carry

        lax.fori_loop(0, groups // 2, gather_mix, 0)

    fetches[4].wait()
    fetches[5].wait()
    tall = (LANES, elements)
    for a in range(conn.shape[0]):
        onehot[a] = (count_up(tall, 0) == conn[a : a + 1, :]).astype(jnp.bfloat16)
    drain(halo_recv, recv.at[R_HALO])
    lane8 = count_up((8, LANES), 1)
    near = jnp.where(lane8 < own_nodes, own_disp, halo_recv[...])
    products = [jnp.zeros((8, elements), f32) for _ in range(3)]
    for a in range(conn.shape[0]):
        moved = select_dot(near, onehot[a], False)
        for j in range(3):
            products[j] = products[j] + moved * grad[j, a : a + 1, :]
    strain_ref[...] = jnp.zeros(strain_ref.shape, f32)
    strain_rows = [
        products[0][0:1],
        products[1][1:2],
        products[2][2:3],
        0.5 * (products[2][1:2] + products[1][2:3]),
        0.5 * (products[2][0:1] + products[0][2:3]),
        0.5 * (products[1][0:1] + products[0][1:2]),
    ]
    for c in range(6):
        strain_ref[c : c + 1, 0:elements] = strain_rows[c]
    all_strain = strain_ref[...]

    def matched(ids):
        return ids.astype(f32) == slot_row

    wide = (groups, LANES)
    note = jnp.zeros(wide, f32)
    strain_pieces = pieces_of(all_strain)

    def strain_of(ids):
        match = jnp.where(matched(ids), 1.0, 0.0).astype(jnp.bfloat16)
        parts = [
            lax.dot_general(match, piece, (((1,), (1,)), ((), ())), preferred_element_type=f32)
            for piece in strain_pieces
        ]
        return parts[0] + (parts[1] + parts[2])

    for lv in range(1, levels):
        held = strain_of(count_up(wide, 0) + lv * groups)
        note = note + pltpu.roll(held, 16 * lv, 1)
    for lv in range(levels):
        held = jnp.where(matched(count_up(wide, 0) + lv * groups), 1.0, 0.0)
        note = jnp.where(count_up(wide, 1) == 8 + lv, jnp.sum(held, axis=1, keepdims=True), note)
    for d in range(groups):
        note_send[d] = note[d : d + 1, :]

    def send_note(t, carry):
        d = turn(t, groups, math.gcd(groups, 4), me)
        deliver(note_send.at[d], note_recv.at[my_side * rows + my_row], R_NOTE, d, mine)
        return carry

    lax.fori_loop(0, groups, send_note, 0)
    fetches[6].wait()
    fetches[7].wait()
    fetches[8].wait()
    if ranks > 1:
        drain(props.at[pl.ds(0, ranks - 1)], recv.at[R_PROPS])
    prepare_law(props, laws)

    def send_row(t, turns):
        i = turn(t, rows, row_block, my_row)
        for o in turns:
            h = (mine + o) % ranks
            deliver(trade_new.at[h, i], got.at[me], R_GOT, ranks * i + mine, h)

    def send_new(low, high, turns):
        def step(t, carry):
            send_row(t, turns)
            return carry

        lax.fori_loop(low, high, step, 0)

    def send_mixed(turns):
        def step(t, carry):
            u = turn(t, half, 1, my_pair)
            for o in turns:
                h = (mine + o) % ranks
                spot = ranks * (2 * u + 1 - my_odd) + mine
                push(mix_new.at[h, u], got.at[2 * groups + me], R_GOT + 2, spot, h)
            return carry

        lax.fori_loop(0, half, step, 0)

    def give_back(new, first, count, low, kind, stride, start):
        def step(i, carry):
            for o in range(ranks):
                h = (mine + o) % ranks
                giver = ranks * (stride * i + start) + raw_side
                deliver(new.at[h, first + i], got.at[low + giver], kind, me, h)
            return carry

        lax.fori_loop(0, count, step, 0)

    def send_means(means, first, count, dst, kind, stride, start):
        for i in range(count):
            stage[first + i if count < rows else rows + i] = means[first + i : first + i + 1, :]

        def step(t, carry):
            i = turn(t, count, math.gcd(count, 2), my_row * count // rows)
            for h in range(ranks):
                src = stage.at[first + i if count < rows else rows + i]
                deliver(src, dst, kind, ranks * (stride * i + start) + raw_side, h)
            return carry

        lax.fori_loop(0, count, step, 0)

    near, far = range(1), range(1, ranks)

    def trade_mix():
        for o in far:
            push(mix_trade.at[o - 1], mix_recv.at[mine, pl.ds(0, half)], R_MIXT, me, (mine + o) % ranks)

    def first_hook(step):
        if levels > 2:
            pl.when(step == SWEEPS - 2)(lambda: send_mix(0))
            pl.when(step == SWEEPS - 1)(trade_mix)

    def second_hook(step):
        if levels > 2:

            @pl.when(step >= SWEEPS - 2)
            def _():
                low = 2 * (step - (SWEEPS - 2))
                send_row(low, far)
                send_row(low + 1, far)

    def third_hook(step):
        pl.when(step < SWEEPS - 1)(lambda: send_new(2 * step + 2, 2 * step + 4, near))

    strain = strain_of(ranks * count_up((rows, LANES), 0) + mine)
    if ranks > 1:
        expect((ranks - 1) * rows, recv.at[R_TRADE])
    if levels > 1:
        for o in far:
            send_raw(o)
    means = solve_rows(trade_recv, strain, 0, trade_new, laws, green, plane, buffers, first_hook)
    mean_src[mine] = means
    for o in far:
        push(mean_src.at[mine], mean_src.at[mine], R_MEAN, me, (mine + o) % ranks)
    if levels == 1:
        send_new(0, rows, range(ranks))

    drain(note_recv, recv.at[R_NOTE])
    flags = note_recv[:, 0, :]
    spot = count_up(wide, 0)
    giver = (ranks * (spot % rows) + spot // rows).astype(f32)
    lane = count_up(wide, 1)
    counts = jnp.sum(jnp.where((lane >= 8) & (lane < 8 + levels), flags, 0.0), axis=1, keepdims=True)
    tall_count = jnp.sum(
        jnp.where(
            (count_up(wide, 0) == lane) & (lane < groups), jnp.broadcast_to(counts, wide), 0.0
        ),
        axis=0,
        keepdims=True,
    )
    lane_giver = (ranks * (lane % rows) + lane // rows).astype(f32)
    earlier = (lane_giver < giver) & (lane < groups)
    place = jnp.sum(jnp.where(earlier, tall_count, 0.0), axis=1, keepdims=True)
    picks = jnp.zeros((1, LANES), f32)
    for lv in range(levels):
        held = jnp.sum(jnp.where(lane == 8 + lv, flags, 0.0), axis=1, keepdims=True)
        chosen = (place == lane.astype(f32)) & (held > 0.5)
        picks = picks + jnp.sum(jnp.where(chosen, lv * groups + giver, 0.0), axis=0, keepdims=True)
        place = place + held
    order_vec[...] = picks.astype(jnp.int32)
    give_order = pltpu.make_async_copy(order_vec, order_out, load_sem.at[12])
    give_order.start()

    if levels > 1:
        expect(groups, recv.at[R_RAW])
        if levels > 2:
            for o in far:
                send_mix(o)
        strain = note_recv[pl.ds(raw_side * rows, rows), 0, :]
        means = solve_rows(raw_recv, strain, 16, raw_new, laws, green, plane, buffers, second_hook)
        send_means(means, 0, rows, mean_raw.at[me], R_MRAW, 1, 0)
        give_back(raw_new, 0, rows, groups, R_GOT + 1, 1, 0)
        if levels > 2:
            send_new(half, rows, far)
            send_new(0, 2, near)
        else:
            send_new(0, rows, range(ranks))
    if levels > 2:
        mixed[...] = strain_of(2 * groups + ranks * (2 * count_up((8, LANES), 0) + 1 - my_odd) + mine)
        mixed[...] = pltpu.roll(mixed[...], 32, 1)
        for u in range(half):
            mixed[half + u : half + u + 1, :] = note_recv[raw_side * rows + 2 * u + my_odd][0:1, :]
        if ranks > 1:
            expect((ranks - 1) * half, recv.at[R_MIXT])
        expect(ranks * half, recv.at[R_MIX])
        means = solve_rows(mix_recv, mixed[0:rows, :], 32, mix_new, laws, green, plane, buffers, third_hook)
        mean_mix[mine] = means
        for o in far:
            push(mean_mix.at[mine], mean_mix.at[mine], R_MMIX, me, (mine + o) % ranks)
        send_means(means, half, half, mean_far.at[my_pair * ranks + my_side], R_MFAR, 2, my_odd)
        send_mixed(far)
        give_back(mix_new, half, half, 2 * groups, R_GOT + 2, 2, my_odd)
        send_mixed(near)
    fetches[9].wait()
    fetches[10].wait()
    fetches[11].wait()
    deep = (levels * groups, LANES)
    k = count_up(deep, 0)
    inside = k % groups
    known = ranks * (inside % rows) + inside // rows
    if ranks > 1:
        drain(mean_src.at[pl.ds(0, ranks - 1)], recv.at[R_MEAN])
    for y in range(ranks):
        mean_all[y * rows : (y + 1) * rows, :] = mean_src[y]
    if levels > 1:
        drain(mean_raw, recv.at[R_MRAW])
        mean_all[groups : 2 * groups, :] = mean_raw[:, 0, :]
        known = jnp.where(k < groups, known, k)
    if levels > 2:
        if ranks > 1:
            drain(mean_mix.at[pl.ds(0, ranks - 1)], recv.at[R_MMIX])
        drain(mean_far, recv.at[R_MFAR])
        middle = 2 * groups + groups // 2
        for y in range(ranks):
            low = 2 * groups + y * half
            mean_all[low : low + half, :] = mean_mix[y, 0:half, :]
        mean_all[middle:, :] = mean_far[:, 0, :]
        from_src = 2 * groups + ranks * (2 * (inside % half) + 1 - my_odd) + inside // half
        v = inside - groups // 2
        from_raw = 2 * groups + ranks * (2 * (v // ranks) + my_odd) + v % ranks
        known = jnp.where(k < 2 * groups, known, jnp.where(k < middle, from_src, from_raw))
    match = jnp.where(matched(known), 1.0, 0.0).astype(jnp.bfloat16)
    mean_t = jnp.transpose(mean_all[...])[0:8, :]
    averaged = select_dot(mean_t, match, False)[:, 0:elements]
    strain = all_strain[0:8, 0:elements]
    lame, shear = moduli[0:1, :], moduli[1:2, :]
    lateral = lame * (strain[0:1] + strain[1:2] + strain[2:3])
    plastic = owner[...] >= 0
    stress = []
    for c in range(6):
        plain = 2.0 * shear * strain[c : c + 1]
        plain = lateral + plain if c < 3 else plain
        stress.append(jnp.where(plastic, averaged[c : c + 1], plain))
    tensor = [[stress[0], stress[5], stress[4]], [stress[5], stress[1], stress[3]], [stress[4], stress[3], stress[2]]]
    forces[...] = jnp.zeros(forces.shape, f32)
    for i in range(3):
        force = volume[...] * (
            tensor[i][0] * grad[0] + tensor[i][1] * grad[1] + tensor[i][2] * grad[2]
        )
        for a in range(conn.shape[0]):
            forces[a, i : i + 1, :] = force[a : a + 1, :]
    assembled = jnp.zeros((8, LANES), f32)
    for a in range(conn.shape[0]):
        assembled = assembled + select_dot(forces[a], onehot[a], True)
    force_send[...] = assembled
    push(force_send, force_recv, R_FORCE, (me + groups - 1) % groups, mine)
    drain(force_recv, recv.at[R_FORCE])
    lane8 = count_up((8, LANES), 1)
    beyond = (lane8 >= own_nodes) & (lane8 < own_nodes + halos)
    back = jnp.where(beyond, force_recv[...], 0.0)
    total_force = assembled + select_dot(back, halo_match, True)
    residual[...] = total_force[0:3, 0:own_nodes] - load[...]
    give_residual = pltpu.make_async_copy(residual, residual_out, load_sem.at[13])
    give_residual.start()

    for lv in range(levels):
        drain(got.at[pl.ds(lv * groups, groups)], recv.at[R_GOT + lv])
    give_order.wait()
    give_residual.wait()
    drain(note_send.at[pl.ds(0, groups - 1)], sent.at[R_NOTE])
    drain(halo_send, sent.at[R_HALO])
    drain(force_send, sent.at[R_FORCE])
    if ranks > 1:
        drain(props.at[pl.ds(0, ranks - 1)], sent.at[R_PROPS])
    if ranks > 1:
        drain(trade_send, sent.at[R_TRADE])
        drain(mean_src.at[pl.ds(0, ranks - 1)], sent.at[R_MEAN])
    settle(got.at[pl.ds(0, groups)], R_GOT, my_side == mine)
    own = (2 * me) % ranks == mine
    if levels > 1:
        settle(raw_send, R_RAW, own)
        settle(mean_raw, R_MRAW, own)
        if ranks > 1:
            expect((ranks - 1) * rows, sent.at[R_GOT + 1])
    if levels > 2:
        settle(mix_send, R_MIX, own)
        settle(mean_far, R_MFAR, own)
        if ranks > 1:
            drain(mix_trade, sent.at[R_MIXT])
            drain(mean_mix.at[pl.ds(0, ranks - 1)], sent.at[R_MMIX])
        expect(ranks * half + (ranks - 1) * half, sent.at[R_GOT + 2])


def exchange(smalls, state, moduli, tables, levels):
    groups, ranks = lax.axis_size("macro"), lax.axis_size("vox")
    rows = groups // ranks
    thickness = state.shape[2]
    half, extra, mix = rows // 2, min(levels - 1, 1), 1 if levels > 2 else 0
    nodes, corners, elements = smalls[0].shape[1], smalls[2].shape[0], smalls[2].shape[1]
    slab = (7, thickness, VOX_PLANE)
    hbm = pl.BlockSpec(memory_space=pltpu.HBM)
    f32 = jnp.float32
    kinds = 13 + levels
    cells = levels * VOX_SIDE * rows * VOX_PLANE
    tile = pltpu.VMEM((8, LANES), f32)
    return pl.pallas_call(
        functools.partial(exchange_kernel, levels),
        out_shape=[
            jax.ShapeDtypeStruct((3, nodes), f32),
            jax.ShapeDtypeStruct((levels * groups,) + slab, f32),
            jax.ShapeDtypeStruct((1, LANES), jnp.int32),
        ],
        in_specs=[hbm] * (len(smalls) + 2 + len(tables)),
        out_specs=[hbm] * 3,
        scratch_shapes=[
            pltpu.VMEM(state.shape, f32),
            pltpu.VMEM((max(ranks - 1, 1), rows) + slab, f32),
            pltpu.VMEM((ranks, rows) + slab, f32),
            pltpu.VMEM((ranks, rows) + slab, f32),
            pltpu.VMEM((groups if extra else 1,) + slab, f32),
            pltpu.VMEM((ranks, rows if extra else 1) + slab, f32),
            pltpu.VMEM((ranks, rows if extra else 1) + slab, f32),
            pltpu.VMEM((max(ranks - 1, 1), half if mix else 1) + slab, f32),
            pltpu.VMEM((groups // 2 if mix else 1,) + slab, f32),
            pltpu.VMEM((ranks, rows if mix else 1) + slab, f32),
            pltpu.VMEM((ranks, rows if mix else 1) + slab, f32),
            pltpu.VMEM((ranks,) + moduli.shape, f32),
            pltpu.VMEM(tables[0].shape, f32),
            pltpu.VMEM(tables[1].shape, tables[1].dtype),
            pltpu.VMEM((7, VOX_SIDE, rows, VOX_PLANE), f32),
            pltpu.VMEM((6, VOX_SIDE, rows, VOX_PLANE), f32),
            pltpu.VMEM((6, VOX_SIDE, rows, VOX_PLANE), f32),
            pltpu.VMEM((6, HALF + 1, rows, VOX_PLANE), f32),
            pltpu.VMEM((6, HALF - 1, rows, VOX_PLANE), f32),
            pltpu.VMEM((groups, 1, LANES), f32),
            pltpu.VMEM((groups, 1, LANES), f32),
            pltpu.VMEM((ranks, rows, LANES), f32),
            pltpu.VMEM((groups, 1, LANES), f32),
            pltpu.VMEM((ranks, rows, LANES), f32),
            pltpu.VMEM((groups // 2, 1, LANES), f32),
            pltpu.VMEM((2 * rows, 1, LANES), f32),
            pltpu.VMEM((levels * groups, LANES), f32),
            tile,
            tile,
            tile,
            tile,
            tile,
            pltpu.VMEM((LANES, LANES), f32),
            pltpu.VMEM((corners, LANES, elements), jnp.bfloat16),
            pltpu.VMEM((corners, 8, elements), f32),
            pltpu.VMEM((8, LANES), jnp.int32),
        ]
        + [pltpu.VMEM(small.shape, small.dtype) for small in smalls]
        + [
            pltpu.VMEM((1, LANES), jnp.int32),
            pltpu.SMEM((1, LANES), jnp.int32),
            pltpu.VMEM((1, LANES), jnp.int32),
            pltpu.VMEM((3, nodes), f32),
            pltpu.VMEM((ranks, 6) + moduli.shape[1:], f32),
            pltpu.SemaphoreType.DMA((14,)),
            pltpu.SemaphoreType.DMA((kinds,)),
            pltpu.SemaphoreType.DMA((kinds,)),
        ],
        compiler_params=pltpu.CompilerParams(
            collective_id=0, has_side_effects=True, vmem_limit_bytes=63 * 2**20
        ),
        cost_estimate=pl.CostEstimate(
            flops=SWEEPS * 2 * 3 * 2 * 6 * cells * VOX_PLANE,
            bytes_accessed=4 * 7 * cells * 4,
            transcendentals=SWEEPS * cells,
        ),
    )(*smalls, state, moduli, *tables)


def pick_kernel(order_hbm, got, residual, residual_out, moved, order_ref, held, load_sem, slot_sem, out_sem):
    count, slots = held.shape[0], got.shape[0]
    fetch = pltpu.make_async_copy(order_hbm, order_ref, load_sem.at[0])
    fetch.start()
    keep = pltpu.make_async_copy(residual, residual_out, load_sem.at[1])
    keep.start()
    fetch.wait()

    def take(j):
        slot = jnp.clip(order_ref[0, j], 0, slots - 1)
        return pltpu.make_async_copy(got.at[slot], held.at[j], slot_sem.at[j])

    for j in range(count):
        take(j).start()
    for j in range(count):
        drain(held.at[j], slot_sem.at[j])
        pltpu.make_async_copy(held.at[j], moved.at[:, j], out_sem).start()
    keep.wait()
    drain(held, out_sem)


def pick_rows(order, got, residual):
    slab = got.shape[1:]
    hbm = pl.BlockSpec(memory_space=pltpu.HBM)
    return pl.pallas_call(
        pick_kernel,
        out_shape=[
            jax.ShapeDtypeStruct(residual.shape, jnp.float32),
            jax.ShapeDtypeStruct(slab[:1] + (RECV_AGG,) + slab[1:], jnp.float32),
        ],
        in_specs=[hbm] * 3,
        out_specs=[hbm] * 2,
        scratch_shapes=[
            pltpu.SMEM(order.shape, jnp.int32),
            pltpu.VMEM((RECV_AGG,) + slab, jnp.float32),
            pltpu.SemaphoreType.DMA((2,)),
            pltpu.SemaphoreType.DMA((RECV_AGG,)),
            pltpu.SemaphoreType.DMA,
        ],
        compiler_params=pltpu.CompilerParams(vmem_limit_bytes=63 * 2**20),
    )(order, got, residual)


def local(
    displacement,
    load,
    conn,
    halo_list,
    grad_ops,
    volume,
    elastic_moduli,
    plastic_mask,
    new_owner,
    state,
    micro_moduli,
):
    groups = lax.axis_size("macro")
    tables = (jnp.asarray(green_tables()), plane_tables())
    levels = (PLASTIC_MAX + groups - 1) // groups
    assert levels <= 3 and groups // lax.axis_size("vox") == 2 * SWEEPS
    smalls = (
        displacement,
        load,
        conn,
        halo_list[None, :],
        grad_ops,
        volume[None, :],
        elastic_moduli,
        new_owner[None, :],
    )
    residual, got, order = exchange(smalls, state, micro_moduli, tables, levels)
    return tuple(pick_rows(order, got, residual))


def solution(mesh):
    return jax.shard_map(
        local,
        mesh=mesh,
        in_specs=(
            P(None, "macro"),
            P(None, "macro"),
            P(None, "macro"),
            P("macro"),
            P(None, None, "macro"),
            P("macro"),
            P(None, "macro"),
            P("macro"),
            P("macro"),
            P(None, "macro", "vox", None),
            P(None, "vox", None),
        ),
        out_specs=(P(None, "macro"), P(None, "macro", "vox", None)),
        check_vma=False,
    )
```
